128 devices in a mesh: view: 8 (over x_lo, y), point: 16 (over x_hi, z, core).
Axes of the slice: x: 4 (x_hi: 2, x_lo: 2; x = x_hi * 2 + x_lo), y: 4, z: 4, core: 2. Of those that a mesh axis runs over, the one named last changes fastest.
Arguments:
- features: bfloat16 [512, 32, 128, 256], P(('view', 'point')), may hold values from -6 to 6
- tiles: int32 [512, 2], P(('view', 'point')), may hold values from 0 to 7, as said below
- masks: int32 [512, 32, 128], P(('view', 'point')), may hold values from 0 to 1
- w_self: bfloat16 [3, 256, 256], replicated, may hold values from -0.375 to 0.375
- w_col: bfloat16 [3, 256, 256], replicated, may hold values from -0.09375 to 0.09375
- w_row: bfloat16 [3, 256, 256], replicated, may hold values from -0.03125 to 0.03125
- bias: float32 [3, 256], replicated, may hold values from -3 to 3
Outputs:
- result: bfloat16 [512, 32, 128, 256], P(('view', 'point'))
The draws below stay inside these ranges and needn't reach their ends.
Inputs may be any that keep to these rules, and one draw needn't show every extreme that they name: `tiles`: column 0 is a view tile of the slot's own view block, below 4. Column 1 below 4 is a point tile of the device's own point block; otherwise, minus 4, a point tile of the block of the next device along point, the last device's next being the first. No two slots name the same tile.
All inputs are finite; a program needn't handle non-finite values.
Results may differ from the reference program's by a relative error of at most 0.0051.
Values sent between devices are 32-bit elements; how exact they have to be, the bound alone decides.
No kernel may reach another device: no remote copies, remote signals or barrier semaphores. Data moves between devices by JAX's collectives and lax.ppermute only.
A program may use at most 128 MiB of HBM per device.

```python
import jax
import jax.numpy as jnp
from jax import lax

D = 256
TV = 32
TP = 128
VT_DEV = 4
PT_DEV = 4
SLOTS = 4
LAYERS = 3
ALL_SLOTS = 512
N_VIEW = 8
N_POINT = 16


def tile_layout(key):
    base_key = jax.random.fold_in(key, 7)
    help_key, order_key = jax.random.split(base_key)
    cell_total = VT_DEV * PT_DEV
    helped = jax.random.randint(help_key, (N_VIEW, N_POINT), 0, SLOTS + 1).astype(jnp.int32)
    order_keys = jax.random.split(order_key, N_VIEW * N_POINT)
    cell_order = jax.vmap(lambda subkey: jax.random.permutation(subkey, cell_total))(order_keys)
    cell_order = cell_order.reshape(N_VIEW, N_POINT, cell_total).astype(jnp.int32)
    helped_after = jnp.roll(helped, -1, axis=1)
    owned = SLOTS - helped_after
    slot_index = jnp.arange(SLOTS, dtype=jnp.int32)[None, None, :]
    is_owned = slot_index < owned[..., None]
    own_pick = jnp.minimum(helped[..., None] + slot_index, cell_total - 1)
    after_pick = jnp.maximum(slot_index - owned[..., None], 0)
    order_after = jnp.roll(cell_order, -1, axis=1)
    own_cell = jnp.take_along_axis(cell_order, own_pick, axis=2)
    after_cell = jnp.take_along_axis(order_after, after_pick, axis=2)
    chosen = jnp.where(is_owned, own_cell, after_cell)
    offset = jnp.where(is_owned, 0, PT_DEV)
    view_column = chosen // PT_DEV
    point_column = chosen % PT_DEV + offset
    stacked = jnp.stack([view_column, point_column], axis=-1)
    return stacked.reshape(N_VIEW * N_POINT * SLOTS, 2).astype(jnp.int32)


def draw_tiles(key, part):
    return tile_layout(key)


def draw_masks(key, part):
    slot_ids = jnp.arange(ALL_SLOTS, dtype=jnp.int32)
    device_index = slot_ids // SLOTS
    view_pos = device_index // N_POINT
    point_pos = device_index % N_POINT
    threshold = 150 + 350 * point_pos // max(N_POINT - 1, 1) + 350 * view_pos // max(N_VIEW - 1, 1)
    drawn = jax.random.randint(jax.random.fold_in(key, 3), (ALL_SLOTS, TV, TP), 0, 1000)
    return (drawn < threshold[:, None, None]).astype(jnp.int32)


def block_scale(stream_key, shape, cuts, least, top_value):
    def one(axis_at, shards_of):
        steps = jax.random.uniform(jax.random.fold_in(jax.random.fold_in(stream_key, 6), axis_at), (shards_of,), jnp.float32, least / len(cuts), top_value / len(cuts))
        return jnp.repeat(jnp.exp(steps), shape[axis_at] // shards_of).reshape((-1,) + (1,) * (len(shape) - axis_at - 1))

    loudness = one(*cuts[0])
    for cut in cuts[1:]:
        loudness = loudness * one(*cut)
    return loudness


def scatter_about(stream_key, shape, width, reach, pieces=(), held_as=jnp.bfloat16):
    entries = jax.random.normal(stream_key, shape, jnp.float32) * width
    if len(pieces) > 0:
        entries = block_scale(stream_key, shape, pieces, -0.22, 0.18) * entries
    return jnp.clip(entries, min=-reach, max=reach).astype(held_as)


def setup_inputs(seed: int = 0) -> dict:
    seeds = jax.random.split(jax.random.key(seed), 8)
    return {
        "features": scatter_about(seeds[0], (ALL_SLOTS, TV, TP, D), 1.0, 6.0, ((0, 128),)),
        "tiles": draw_tiles(jax.random.fold_in(seeds[7], 71), 0),
        "masks": draw_masks(jax.random.fold_in(seeds[7], 71), 0),
        "w_self": scatter_about(seeds[3], (LAYERS, D, D), D ** -0.5, 0.375),
        "w_col": scatter_about(seeds[4], (LAYERS, D, D), (D * 16) ** -0.5, 0.09375),
        "w_row": scatter_about(seeds[5], (LAYERS, D, D), (D * 128) ** -0.5, 0.03125),
        "bias": scatter_about(seeds[6], (LAYERS, D), 0.5, 3.0, (), jnp.float32),
    }


def reference(features, tiles, masks, w_self, w_col, w_row, bias):
    device_index = jnp.arange(ALL_SLOTS, dtype=jnp.int32) // SLOTS
    view_pos = device_index // N_POINT
    point_pos = device_index % N_POINT
    view_tile = (view_pos * VT_DEV + tiles[:, 0]).astype(jnp.int32)
    point_tile = ((point_pos + tiles[:, 1] // PT_DEV) % N_POINT * PT_DEV + tiles[:, 1] % PT_DEV).astype(jnp.int32)
    view_tiles_all = VT_DEV * N_VIEW
    point_tiles_all = PT_DEV * N_POINT
    mask_f = masks.astype(jnp.float32)
    row_count = jax.ops.segment_sum(lax.optimization_barrier(jnp.sum(mask_f, axis=2)), view_tile, view_tiles_all)
    col_count = jax.ops.segment_sum(lax.optimization_barrier(jnp.sum(mask_f, axis=1)), point_tile, point_tiles_all)
    row_scale = 1.0 / jnp.sqrt(jnp.maximum(row_count, 1.0))
    col_scale = 1.0 / jnp.sqrt(jnp.maximum(col_count, 1.0))
    devices_all = ALL_SLOTS // SLOTS
    mask_blocks = masks.reshape(devices_all, SLOTS, TV, TP)
    view_blocks = view_tile.reshape(devices_all, SLOTS)
    point_blocks = point_tile.reshape(devices_all, SLOTS)
    current = features
    for layer_step in range(LAYERS):
        feat_blocks = current.reshape(devices_all, SLOTS, TV, TP, D)

        def slot_sums(block_args):
            block_feat, block_mask = block_args
            feat32 = block_feat.astype(jnp.float32)
            mask32 = block_mask.astype(jnp.float32)
            row_part = jnp.einsum('src,srcd->srd', mask32, feat32)
            col_part = jnp.einsum('src,srcd->scd', mask32, feat32)
            return (row_part, col_part)
        row_part, col_part = lax.map(slot_sums, (feat_blocks, mask_blocks))
        row_sum = jax.ops.segment_sum(row_part.reshape(ALL_SLOTS, TV, D), view_tile, view_tiles_all)
        col_sum = jax.ops.segment_sum(col_part.reshape(ALL_SLOTS, TP, D), point_tile, point_tiles_all)
        row_term = (row_sum * row_scale[..., None]).astype(jnp.bfloat16)
        col_term = (col_sum * col_scale[..., None]).astype(jnp.bfloat16)
        row_proj = jnp.dot(row_term.reshape(-1, D), w_row[layer_step], preferred_element_type=jnp.float32).reshape(view_tiles_all, TV, D)
        col_proj = jnp.dot(col_term.reshape(-1, D), w_col[layer_step], preferred_element_type=jnp.float32).reshape(point_tiles_all, TP, D)
        weight_self = w_self[layer_step]
        bias_row = bias[layer_step]

        def layer_block(block_args):
            block_feat, block_mask, block_view, block_point = block_args
            self_proj = jnp.dot(block_feat.reshape(-1, D), weight_self, preferred_element_type=jnp.float32).reshape(SLOTS, TV, TP, D)
            mixed_sum = self_proj + col_proj[block_point][:, None, :, :] + row_proj[block_view][:, :, None, :] + bias_row
            return (jnp.maximum(mixed_sum, 0.0) * block_mask.astype(jnp.float32)[..., None]).astype(jnp.bfloat16)
        current = lax.map(layer_block, (feat_blocks, mask_blocks, view_blocks, point_blocks)).reshape(ALL_SLOTS, TV, TP, D)
    return current
```

```python
import functools

import jax
import jax.numpy as jnp
from jax import lax
from jax.experimental import pallas as pl
from jax.experimental.pallas import tpu as pltpu
from jax.sharding import PartitionSpec as P

VT_DEV = 4
PT_DEV = 4
LAYERS = 3
SLOTS = 4
TV = 32
TP = 128
D = 256
N_VIEW = 8
PER = TP // N_VIEW
DATA = SLOTS * PER
EXTRA = 8
CC = 64
RC = 8
F32 = jnp.float32
BF16 = jnp.bfloat16
VMEM = pltpu.VMEM


def first_sums(tiles_ref, x_ref, m_ref, col_ref, row_ref, mt_ref, part_ref):
    slot = pl.program_id(0)

    @pl.when(slot == 0)
    def _():
        row_ref[...] = jnp.zeros_like(row_ref)
        for s in range(SLOTS):
            mask = m_ref[s].astype(F32)
            mask_t = mask.T
            mt_ref[s] = mask_t
            col_count = jnp.sum(mask, axis=0, keepdims=True)
            point_id = jnp.full((1, D), tiles_ref[s, 1], jnp.int32).astype(F32)
            padded = jnp.concatenate([col_count, jnp.zeros((1, D - TP), F32)], axis=1)
            for peer in range(N_VIEW):
                col_ref[peer, DATA + s : DATA + s + 1, :] = point_id
                col_ref[peer, DATA + SLOTS + s : DATA + SLOTS + s + 1, :] = padded
            row_count = jnp.sum(mask_t, axis=0, keepdims=True)
            padded_row = jnp.concatenate([row_count, jnp.zeros((1, D - TV), F32)], axis=1)
            for v in range(VT_DEV):
                hit = jnp.where(tiles_ref[s, 0] == v, 1.0, 0.0).astype(F32)
                at = VT_DEV * TV + v
                row_ref[at : at + 1, :] += padded_row * hit

    mask_t = mt_ref[slot]
    for c0 in range(0, TP, CC):
        acc = jnp.zeros((CC, D), F32)
        for r in range(TV):
            val = x_ref[0, r, c0 : c0 + CC, :].astype(F32) * mask_t[c0 : c0 + CC, r : r + 1]
            acc = acc + val
            total = jnp.sum(val, axis=0, keepdims=True)
            if c0 == 0:
                part_ref[r : r + 1, :] = total
            else:
                part_ref[r : r + 1, :] += total
        for k in range(CC // PER):
            col_ref[c0 // PER + k, pl.ds(pl.multiple_of(slot * PER, PER), PER), :] = acc[
                k * PER : (k + 1) * PER
            ]
    view_at = pl.multiple_of(tiles_ref[slot, 0] * TV, TV)
    row_ref[pl.ds(view_at, TV), :] += part_ref[...]


def layer_body(
    last, tiles_ref, x_ref, mt_ref, ret_ref, row_ref, scale_ref, w_ref, wr_ref, *rest
):
    if last:
        out_ref, proj_ref = rest
    else:
        out_ref, col_ref, nrow_ref, proj_ref, part_ref = rest
    slot = pl.program_id(0)

    @pl.when(slot == 0)
    def _():
        if not last:
            nrow_ref[...] = jnp.zeros_like(nrow_ref)
        scale = scale_ref[...]
        lane = lax.broadcasted_iota(jnp.int32, (TV, TP), 1)
        line = lax.broadcasted_iota(jnp.int32, (TV, TP), 0)
        for v in range(VT_DEV):
            count = jnp.broadcast_to(scale[v : v + 1, :TP], (TV, TP))
            count = jnp.sum(jnp.where(lane == line, count, 0.0), axis=1, keepdims=True)
            factor = 1.0 / jnp.sqrt(jnp.maximum(count, 1.0))
            term = (row_ref[v * TV : (v + 1) * TV, :] * factor).astype(BF16)
            proj_ref[v * TV : (v + 1) * TV, :] = jnp.dot(
                term, wr_ref[...], preferred_element_type=F32
            )

    view_at = pl.multiple_of(tiles_ref[slot, 0] * TV, TV)
    row_proj = proj_ref[pl.ds(view_at, TV), :]
    weight = w_ref[...]
    mask_t = mt_ref[slot]
    col_proj = ret_ref[:, pl.ds(pl.multiple_of(slot * PER, PER), PER), :].reshape(TP, D)
    for c0 in range(0, TP, CC):
        acc = jnp.zeros((CC, D), F32)
        col_here = col_proj[c0 : c0 + CC]
        for r0 in range(0, TV, RC):
            block = x_ref[0, r0 : r0 + RC, c0 : c0 + CC, :].reshape(RC * CC, D)
            prod = jnp.dot(block, weight, preferred_element_type=F32)
            for k in range(RC):
                r = r0 + k
                val = prod[k * CC : (k + 1) * CC] + col_here + row_proj[r : r + 1, :]
                val = jnp.maximum(val, 0.0) * mask_t[c0 : c0 + CC, r : r + 1]
                out_ref[0, r, c0 : c0 + CC, :] = val.astype(BF16)
                if not last:
                    acc = acc + val
                    total = jnp.sum(val, axis=0, keepdims=True)
                    if c0 == 0:
                        part_ref[r : r + 1, :] = total
                    else:
                        part_ref[r : r + 1, :] += total
        if not last:
            for k in range(CC // PER):
                col_ref[c0 // PER + k, pl.ds(pl.multiple_of(slot * PER, PER), PER), :] = acc[
                    k * PER : (k + 1) * PER
                ]
    if not last:
        nrow_ref[pl.ds(view_at, TV), :] += part_ref[...]


def owner_sums(first, place_ref, got_ref, ids_ref, a_ref, b_ref):
    for ref, which in ((a_ref, 0), (b_ref, 1)):
        base = place_ref[which]
        for j in range(PT_DEV):
            q = (jnp.full((1, D), base, jnp.int32) + j).astype(F32)
            acc = jnp.zeros((PER, D), F32)
            cnt = jnp.zeros((1, D), F32)
            for d in range(N_VIEW):
                for s in range(SLOTS):
                    hit = ids_ref[d, s : s + 1, :] == q
                    acc = acc + jnp.where(hit, got_ref[d, s * PER : (s + 1) * PER, :], 0.0)
                    if first:
                        cnt = cnt + jnp.where(hit, ids_ref[d, SLOTS + s : SLOTS + s + 1, :], 0.0)
            ref[j * PER : (j + 1) * PER, :] = acc
            if first:
                ref[DATA + j : DATA + j + 1, :] = cnt
        if first:
            ref[DATA + PT_DEV :, :] = jnp.zeros((EXTRA - PT_DEV, D), F32)


def owner_project(
    first, place_ref, a_ref, b_ref, ra_ref, rb_ref, ids_ref, cnt_ref, w_ref, bias_ref, *rest
):
    if first:
        ret_ref, ncnt_ref = rest
    else:
        (ret_ref,) = rest
    mine = place_ref[2] * PER
    lane = lax.broadcasted_iota(jnp.int32, (PER, TP), 1)
    line = lax.broadcasted_iota(jnp.int32, (PER, TP), 0) + mine
    projs = []
    for which, (ref, rref) in enumerate(((a_ref, ra_ref), (b_ref, rb_ref))):
        terms = []
        for j in range(PT_DEV):
            total = ref[j * PER : (j + 1) * PER, :] + rref[j * PER : (j + 1) * PER, :]
            if first:
                count = ref[DATA + j : DATA + j + 1, :] + rref[DATA + j : DATA + j + 1, :]
                ncnt_ref[which * PT_DEV + j : which * PT_DEV + j + 1, :] = count
            else:
                count = cnt_ref[which * PT_DEV + j : which * PT_DEV + j + 1, :]
            count = jnp.broadcast_to(count[:, :TP], (PER, TP))
            count = jnp.sum(jnp.where(lane == line, count, 0.0), axis=1, keepdims=True)
            factor = 1.0 / jnp.sqrt(jnp.maximum(count, 1.0))
            terms.append((total * factor).astype(BF16))
        term = jnp.concatenate(terms, axis=0)
        projs.append(jnp.dot(term, w_ref[...], preferred_element_type=F32) + bias_ref[...])
    for d in range(N_VIEW):
        for s in range(SLOTS):
            point_id = ids_ref[d, s : s + 1, :]
            out = jnp.zeros((PER, D), F32)
            for which in range(2):
                base = place_ref[which]
                for j in range(PT_DEV):
                    q = (jnp.full((1, D), base, jnp.int32) + j).astype(F32)
                    out = jnp.where(point_id == q, projs[which][j * PER : (j + 1) * PER], out)
            ret_ref[d, s * PER : (s + 1) * PER, :] = out


def full(memory_space=VMEM):
    return pl.BlockSpec(memory_space=memory_space)


def shards(features, tiles, masks, w_self, w_col, w_row, bias):
    params = pltpu.CompilerParams(vmem_limit_bytes=48 * 1024 * 1024)
    tile_block = (1, TV, TP, D)

    def whole(shape):
        return pl.BlockSpec(shape, lambda i, t: (0,) * len(shape))

    slot_spec = pl.BlockSpec(tile_block, lambda i, t: (i, 0, 0, 0))
    me_view = lax.axis_index("view")
    me_point = lax.axis_index("point")
    even = (me_point % 2) == 0
    off_a = jnp.where(even, PT_DEV, 0)
    place = jnp.stack([off_a, PT_DEV - off_a, me_view]).astype(jnp.int32)
    n_point = lax.axis_size("point")
    pair_a = [(i, i ^ 1) for i in range(n_point)]
    pair_b = [(i, (i + 1) % n_point if i % 2 else (i - 1) % n_point) for i in range(n_point)]

    col_pay, row_pay, mask_t = pl.pallas_call(
        first_sums,
        out_shape=(
            jax.ShapeDtypeStruct((N_VIEW, DATA + EXTRA, D), F32),
            jax.ShapeDtypeStruct((VT_DEV * TV + 8, D), F32),
            jax.ShapeDtypeStruct((SLOTS, TP, TV), F32),
        ),
        grid_spec=pltpu.PrefetchScalarGridSpec(
            num_scalar_prefetch=1,
            grid=(SLOTS,),
            in_specs=[slot_spec, whole((SLOTS, TV, TP))],
            out_specs=(
                whole((N_VIEW, DATA + EXTRA, D)),
                whole((VT_DEV * TV + 8, D)),
                whole((SLOTS, TP, TV)),
            ),
            scratch_shapes=[pltpu.VMEM((TV, D), F32)],
        ),
        compiler_params=params,
        name="first_sums",
    )(tiles, features, masks)

    current = features
    ids = None
    counts = None
    row_counts = None
    for layer_step in range(LAYERS):
        first = layer_step == 0
        last = layer_step == LAYERS - 1
        got = lax.all_to_all(col_pay, "view", 0, 0, tiled=True)
        row_sum = row_pay
        for flip in (1, 2, 6, 8):
            row_sum = row_sum + lax.ppermute(
                row_sum, "point", [(i, i ^ flip) for i in range(n_point)]
            )
        if first:
            ids = got[:, DATA:, :]
            row_counts = row_sum[VT_DEV * TV :, :]
        extra = EXTRA if first else 0
        part_a, part_b = pl.pallas_call(
            functools.partial(owner_sums, first),
            out_shape=[jax.ShapeDtypeStruct((DATA + extra, D), F32)] * 2,
            in_specs=[full(pltpu.SMEM), full(), full()],
            out_specs=[full(), full()],
            compiler_params=params,
            name="owner_sums",
        )(place, got, ids)
        from_a = lax.ppermute(part_a, "point", pair_a)
        from_b = lax.ppermute(part_b, "point", pair_b)
        out_shape = [jax.ShapeDtypeStruct((N_VIEW, DATA, D), F32)]
        if first:
            out_shape.append(jax.ShapeDtypeStruct((2 * PT_DEV, D), F32))
        outs = pl.pallas_call(
            functools.partial(owner_project, first),
            out_shape=out_shape,
            in_specs=[full(pltpu.SMEM)] + [full()] * 8,
            out_specs=[full()] * len(out_shape),
            compiler_params=params,
            name="owner_project",
        )(
            place,
            part_a,
            part_b,
            from_a,
            from_b,
            ids,
            ids[0] if first else counts,
            w_col[layer_step],
            bias[layer_step][None, :],
        )
        if first:
            counts = outs[1]
        back = lax.all_to_all(outs[0], "view", 0, 0, tiled=True)
        out_shape = [jax.ShapeDtypeStruct(features.shape, BF16)]
        out_specs = [slot_spec]
        scratch = [pltpu.VMEM((VT_DEV * TV, D), F32)]
        if not last:
            out_shape += [
                jax.ShapeDtypeStruct((N_VIEW, DATA, D), F32),
                jax.ShapeDtypeStruct((VT_DEV * TV, D), F32),
            ]
            out_specs += [whole((N_VIEW, DATA, D)), whole((VT_DEV * TV, D))]
            scratch.append(pltpu.VMEM((TV, D), F32))
        outs = pl.pallas_call(
            functools.partial(layer_body, last),
            out_shape=out_shape,
            grid_spec=pltpu.PrefetchScalarGridSpec(
                num_scalar_prefetch=1,
                grid=(SLOTS,),
                in_specs=[
                    slot_spec,
                    whole((SLOTS, TP, TV)),
                    whole((N_VIEW, DATA, D)),
                    whole(row_sum.shape),
                    whole((8, D)),
                    whole((D, D)),
                    whole((D, D)),
                ],
                out_specs=out_specs,
                scratch_shapes=scratch,
            ),
            compiler_params=params,
            name="layer_body",
        )(tiles, current, mask_t, back, row_sum, row_counts, w_self[layer_step], w_row[layer_step])
        current = outs[0]
        if not last:
            col_pay, row_pay = outs[1], outs[2]
    return current


def solution(mesh):
    in_specs = (
        P(("view", "point"), None, None, None),
        P(("view", "point"), None),
        P(("view", "point"), None, None),
        P(),
        P(),
        P(),
        P(),
    )
    out_specs = P(("view", "point"), None, None, None)
    return jax.shard_map(shards, mesh=mesh, in_specs=in_specs, out_specs=out_specs, check_vma=False)
```

```python
import functools

import jax
import jax.numpy as jnp
from jax import lax
from jax.experimental import pallas as pl
from jax.experimental.pallas import tpu as pltpu
from jax.sharding import PartitionSpec as P

VT_DEV = 4
PT_DEV = 4
LAYERS = 3
SLOTS = 4
TV = 32
TP = 128
D = 256
N_VIEW = 8
PER = TP // N_VIEW
DATA = SLOTS * PER
EXTRA = 8
CC = 64
RC = 8
F32 = jnp.float32
BF16 = jnp.bfloat16
VMEM = pltpu.VMEM


def first_sums(tiles_ref, x_ref, m_ref, col_ref, row_ref, mt_ref, part_ref):
    slot = pl.program_id(0)

    @pl.when(slot == 0)
    def _():
        row_ref[...] = jnp.zeros_like(row_ref)
        for s in range(SLOTS):
            mask = m_ref[s].astype(F32)
            mask_t = mask.T
            mt_ref[s] = mask_t
            col_count = jnp.sum(mask, axis=0, keepdims=True)
            point_id = jnp.full((1, D), tiles_ref[s, 1], jnp.int32).astype(F32)
            padded = jnp.concatenate([col_count, jnp.zeros((1, D - TP), F32)], axis=1)
            for peer in range(N_VIEW):
                col_ref[peer, DATA + s : DATA + s + 1, :] = point_id
                col_ref[peer, DATA + SLOTS + s : DATA + SLOTS + s + 1, :] = padded
            row_count = jnp.sum(mask_t, axis=0, keepdims=True)
            padded_row = jnp.concatenate([row_count, jnp.zeros((1, D - TV), F32)], axis=1)
            for v in range(VT_DEV):
                hit = jnp.where(tiles_ref[s, 0] == v, 1.0, 0.0).astype(F32)
                at = VT_DEV * TV + v
                row_ref[at : at + 1, :] += padded_row * hit

    mask_t = mt_ref[slot]
    for c0 in range(0, TP, CC):
        acc = jnp.zeros((CC, D), F32)
        for r in range(TV):
            val = x_ref[0, r, c0 : c0 + CC, :].astype(F32) * mask_t[c0 : c0 + CC, r : r + 1]
            acc = acc + val
            total = jnp.sum(val, axis=0, keepdims=True)
            if c0 == 0:
                part_ref[r : r + 1, :] = total
            else:
                part_ref[r : r + 1, :] += total
        for k in range(CC // PER):
            col_ref[c0 // PER + k, pl.ds(pl.multiple_of(slot * PER, PER), PER), :] = acc[
                k * PER : (k + 1) * PER
            ]
    view_at = pl.multiple_of(tiles_ref[slot, 0] * TV, TV)
    row_ref[pl.ds(view_at, TV), :] += part_ref[...]


def layer_body(
    last, tiles_ref, x_ref, mt_ref, ret_ref, row_ref, scale_ref, w_ref, wr_ref, *rest
):
    if last:
        out_ref, proj_ref = rest
    else:
        out_ref, col_ref, nrow_ref, proj_ref, part_ref = rest
    slot = pl.program_id(0)

    @pl.when(slot == 0)
    def _():
        if not last:
            nrow_ref[...] = jnp.zeros_like(nrow_ref)
        scale = scale_ref[...]
        lane = lax.broadcasted_iota(jnp.int32, (TV, TP), 1)
        line = lax.broadcasted_iota(jnp.int32, (TV, TP), 0)
        for v in range(VT_DEV):
            count = jnp.broadcast_to(scale[v : v + 1, :TP], (TV, TP))
            count = jnp.sum(jnp.where(lane == line, count, 0.0), axis=1, keepdims=True)
            factor = 1.0 / jnp.sqrt(jnp.maximum(count, 1.0))
            term = (row_ref[v * TV : (v + 1) * TV, :] * factor).astype(BF16)
            proj_ref[v * TV : (v + 1) * TV, :] = jnp.dot(
                term, wr_ref[...], preferred_element_type=F32
            )

    view_at = pl.multiple_of(tiles_ref[slot, 0] * TV, TV)
    row_proj = proj_ref[pl.ds(view_at, TV), :]
    weight = w_ref[...]
    mask_t = mt_ref[slot]
    col_proj = ret_ref[:, pl.ds(pl.multiple_of(slot * PER, PER), PER), :].reshape(TP, D)
    for c0 in range(0, TP, CC):
        acc = jnp.zeros((CC, D), F32)
        col_here = col_proj[c0 : c0 + CC]
        for r0 in range(0, TV, RC):
            block = x_ref[0, r0 : r0 + RC, c0 : c0 + CC, :].reshape(RC * CC, D)
            prod = jnp.dot(block, weight, preferred_element_type=F32)
            for k in range(RC):
                r = r0 + k
                val = prod[k * CC : (k + 1) * CC] + col_here + row_proj[r : r + 1, :]
                val = jnp.maximum(val, 0.0) * mask_t[c0 : c0 + CC, r : r + 1]
                out_ref[0, r, c0 : c0 + CC, :] = val.astype(BF16)
                if not last:
                    acc = acc + val
                    total = jnp.sum(val, axis=0, keepdims=True)
                    if c0 == 0:
                        part_ref[r : r + 1, :] = total
                    else:
                        part_ref[r : r + 1, :] += total
        if not last:
            for k in range(CC // PER):
                col_ref[c0 // PER + k, pl.ds(pl.multiple_of(slot * PER, PER), PER), :] = acc[
                    k * PER : (k + 1) * PER
                ]
    if not last:
        nrow_ref[pl.ds(view_at, TV), :] += part_ref[...]


def owner_sums(first, place_ref, got_ref, ids_ref, a_ref, b_ref):
    for ref, which in ((a_ref, 0), (b_ref, 1)):
        base = place_ref[which]
        for j in range(PT_DEV):
            q = (jnp.full((1, D), base, jnp.int32) + j).astype(F32)
            acc = jnp.zeros((PER, D), F32)
            cnt = jnp.zeros((1, D), F32)
            for d in range(N_VIEW):
                for s in range(SLOTS):
                    hit = ids_ref[d, s : s + 1, :] == q
                    acc = acc + jnp.where(hit, got_ref[d, s * PER : (s + 1) * PER, :], 0.0)
                    if first:
                        cnt = cnt + jnp.where(hit, ids_ref[d, SLOTS + s : SLOTS + s + 1, :], 0.0)
            ref[j * PER : (j + 1) * PER, :] = acc
            if first:
                ref[DATA + j : DATA + j + 1, :] = cnt
        if first:
            ref[DATA + PT_DEV :, :] = jnp.zeros((EXTRA - PT_DEV, D), F32)


def owner_project(
    first, place_ref, a_ref, b_ref, ra_ref, rb_ref, ids_ref, cnt_ref, w_ref, bias_ref, *rest
):
    if first:
        ret_ref, ncnt_ref = rest
    else:
        (ret_ref,) = rest
    mine = place_ref[2] * PER
    lane = lax.broadcasted_iota(jnp.int32, (PER, TP), 1)
    line = lax.broadcasted_iota(jnp.int32, (PER, TP), 0) + mine
    projs = []
    for which, (ref, rref) in enumerate(((a_ref, ra_ref), (b_ref, rb_ref))):
        terms = []
        for j in range(PT_DEV):
            total = ref[j * PER : (j + 1) * PER, :] + rref[j * PER : (j + 1) * PER, :]
            if first:
                count = ref[DATA + j : DATA + j + 1, :] + rref[DATA + j : DATA + j + 1, :]
                ncnt_ref[which * PT_DEV + j : which * PT_DEV + j + 1, :] = count
            else:
                count = cnt_ref[which * PT_DEV + j : which * PT_DEV + j + 1, :]
            count = jnp.broadcast_to(count[:, :TP], (PER, TP))
            count = jnp.sum(jnp.where(lane == line, count, 0.0), axis=1, keepdims=True)
            factor = 1.0 / jnp.sqrt(jnp.maximum(count, 1.0))
            terms.append((total * factor).astype(BF16))
        term = jnp.concatenate(terms, axis=0)
        projs.append(jnp.dot(term, w_ref[...], preferred_element_type=F32) + bias_ref[...])
    for d in range(N_VIEW):
        for s in range(SLOTS):
            point_id = ids_ref[d, s : s + 1, :]
            out = jnp.zeros((PER, D), F32)
            for which in range(2):
                base = place_ref[which]
                for j in range(PT_DEV):
                    q = (jnp.full((1, D), base, jnp.int32) + j).astype(F32)
                    out = jnp.where(point_id == q, projs[which][j * PER : (j + 1) * PER], out)
            ret_ref[d, s * PER : (s + 1) * PER, :] = out


def doubled(block, flip):
    devices = range(lax.axis_size("point"))
    return block + lax.ppermute(block, "point", [(i, i ^ flip) for i in devices])


def full(memory_space=VMEM):
    return pl.BlockSpec(memory_space=memory_space)


def shards(features, tiles, masks, w_self, w_col, w_row, bias):
    params = pltpu.CompilerParams(vmem_limit_bytes=48 * 1024 * 1024)
    tile_block = (1, TV, TP, D)

    def whole(shape):
        return pl.BlockSpec(shape, lambda i, t: (0,) * len(shape))

    slot_spec = pl.BlockSpec(tile_block, lambda i, t: (i, 0, 0, 0))
    me_view = lax.axis_index("view")
    me_point = lax.axis_index("point")
    even = (me_point % 2) == 0
    off_a = jnp.where(even, PT_DEV, 0)
    place = jnp.stack([off_a, PT_DEV - off_a, me_view]).astype(jnp.int32)
    n_point = lax.axis_size("point")
    pair_a = [(i, i ^ 1) for i in range(n_point)]
    pair_b = [(i, (i + 1) % n_point if i % 2 else (i - 1) % n_point) for i in range(n_point)]

    col_pay, row_pay, mask_t = pl.pallas_call(
        first_sums,
        out_shape=(
            jax.ShapeDtypeStruct((N_VIEW, DATA + EXTRA, D), F32),
            jax.ShapeDtypeStruct((VT_DEV * TV + 8, D), F32),
            jax.ShapeDtypeStruct((SLOTS, TP, TV), F32),
        ),
        grid_spec=pltpu.PrefetchScalarGridSpec(
            num_scalar_prefetch=1,
            grid=(SLOTS,),
            in_specs=[slot_spec, whole((SLOTS, TV, TP))],
            out_specs=(
                whole((N_VIEW, DATA + EXTRA, D)),
                whole((VT_DEV * TV + 8, D)),
                whole((SLOTS, TP, TV)),
            ),
            scratch_shapes=[pltpu.VMEM((TV, D), F32)],
        ),
        compiler_params=params,
        name="first_sums",
    )(tiles, features, masks)

    current = features
    ids = None
    counts = None
    row_counts = None
    for layer_step in range(LAYERS):
        first = layer_step == 0
        last = layer_step == LAYERS - 1
        row_sum = doubled(row_pay, 1)
        col_pay, row_sum = lax.optimization_barrier((col_pay, row_sum))
        got = lax.all_to_all(col_pay, "view", 0, 0, tiled=True)
        row_sum = doubled(row_sum, 2)
        got, row_sum = lax.optimization_barrier((got, row_sum))
        if first:
            ids = got[:, DATA:, :]
        extra = EXTRA if first else 0
        part_a, part_b = pl.pallas_call(
            functools.partial(owner_sums, first),
            out_shape=[jax.ShapeDtypeStruct((DATA + extra, D), F32)] * 2,
            in_specs=[full(pltpu.SMEM), full(), full()],
            out_specs=[full(), full()],
            compiler_params=params,
            name="owner_sums",
        )(place, got, ids)
        from_a = lax.ppermute(part_a, "point", pair_a)
        from_b = lax.ppermute(part_b, "point", pair_b)
        row_sum = doubled(row_sum, 6)
        from_a, from_b, row_sum = lax.optimization_barrier((from_a, from_b, row_sum))
        row_sum = doubled(row_sum, 8)
        if first:
            row_counts = row_sum[VT_DEV * TV :, :]
        out_shape = [jax.ShapeDtypeStruct((N_VIEW, DATA, D), F32)]
        if first:
            out_shape.append(jax.ShapeDtypeStruct((2 * PT_DEV, D), F32))
        outs = pl.pallas_call(
            functools.partial(owner_project, first),
            out_shape=out_shape,
            in_specs=[full(pltpu.SMEM)] + [full()] * 8,
            out_specs=[full()] * len(out_shape),
            compiler_params=params,
            name="owner_project",
        )(
            place,
            part_a,
            part_b,
            from_a,
            from_b,
            ids,
            ids[0] if first else counts,
            w_col[layer_step],
            bias[layer_step][None, :],
        )
        if first:
            counts = outs[1]
        back = lax.all_to_all(outs[0], "view", 0, 0, tiled=True)
        out_shape = [jax.ShapeDtypeStruct(features.shape, BF16)]
        out_specs = [slot_spec]
        scratch = [pltpu.VMEM((VT_DEV * TV, D), F32)]
        if not last:
            out_shape += [
                jax.ShapeDtypeStruct((N_VIEW, DATA, D), F32),
                jax.ShapeDtypeStruct((VT_DEV * TV, D), F32),
            ]
            out_specs += [whole((N_VIEW, DATA, D)), whole((VT_DEV * TV, D))]
            scratch.append(pltpu.VMEM((TV, D), F32))
        outs = pl.pallas_call(
            functools.partial(layer_body, last),
            out_shape=out_shape,
            grid_spec=pltpu.PrefetchScalarGridSpec(
                num_scalar_prefetch=1,
                grid=(SLOTS,),
                in_specs=[
                    slot_spec,
                    whole((SLOTS, TP, TV)),
                    whole((N_VIEW, DATA, D)),
                    whole(row_sum.shape),
                    whole((8, D)),
                    whole((D, D)),
                    whole((D, D)),
                ],
                out_specs=out_specs,
                scratch_shapes=scratch,
            ),
            compiler_params=params,
            name="layer_body",
        )(tiles, current, mask_t, back, row_sum, row_counts, w_self[layer_step], w_row[layer_step])
        current = outs[0]
        if not last:
            col_pay, row_pay = outs[1], outs[2]
    return current


def solution(mesh):
    in_specs = (
        P(("view", "point"), None, None, None),
        P(("view", "point"), None),
        P(("view", "point"), None, None),
        P(),
        P(),
        P(),
        P(),
    )
    out_specs = P(("view", "point"), None, None, None)
    return jax.shard_map(shards, mesh=mesh, in_specs=in_specs, out_specs=out_specs, check_vma=False)
```

```python
import functools

import jax
import jax.numpy as jnp
from jax import lax
from jax.experimental import pallas as pl
from jax.experimental.pallas import tpu as pltpu
from jax.sharding import PartitionSpec as P

VT_DEV = 4
PT_DEV = 4
LAYERS = 3
SLOTS = 4
TV = 32
TP = 128
D = 256
N_VIEW = 8
PER = TP // N_VIEW
DATA = SLOTS * PER
EXTRA = 8
ROWS = VT_DEV * TV
RC = 4
F32 = jnp.float32
BF16 = jnp.bfloat16
SMALL = pltpu.CompilerParams(vmem_limit_bytes=8 * 1024 * 1024)
LARGE = pltpu.CompilerParams(vmem_limit_bytes=48 * 1024 * 1024)


def full(memory_space=pltpu.VMEM):
    return pl.BlockSpec(memory_space=memory_space)


def spread(counts, first_lane, rows):
    lane = lax.broadcasted_iota(jnp.int32, (rows, TP), 1)
    line = lax.broadcasted_iota(jnp.int32, (rows, TP), 0) + first_lane
    picked = jnp.where(lane == line, jnp.broadcast_to(counts, (rows, TP)), 0.0)
    count = jnp.sum(picked, axis=1, keepdims=True)
    return jnp.broadcast_to(1.0 / jnp.sqrt(jnp.maximum(count, 1.0)), (rows, D))


def first_sums(tiles_ref, x_ref, m_ref, col_ref, row_ref):
    slot = pl.program_id(0)
    mask = m_ref[0].astype(F32)
    mask_t = mask.T
    col_count = jnp.sum(mask, axis=0, keepdims=True)
    row_count = jnp.sum(mask_t, axis=0, keepdims=True)
    padded = jnp.concatenate([col_count, jnp.zeros((1, D - TP), F32)], axis=1)
    padded_row = jnp.concatenate([row_count, jnp.zeros((1, D - TV), F32)], axis=1)
    point_id = jnp.full((1, D), tiles_ref[1, slot], jnp.int32).astype(F32)

    @pl.when(slot == 0)
    def _():
        row_ref[...] = jnp.zeros_like(row_ref)

    for s in range(SLOTS):

        @pl.when(slot == s)
        def _():
            for peer in range(N_VIEW):
                col_ref[peer, DATA + s : DATA + s + 1, :] = point_id
                col_ref[peer, DATA + SLOTS + s : DATA + SLOTS + s + 1, :] = padded

    for v in range(VT_DEV):
        hit = jnp.where(tiles_ref[0, slot] == v, 1.0, 0.0).astype(F32)
        row_ref[ROWS + v : ROWS + v + 1, :] += padded_row * hit
    acc = None
    totals = []
    for r in range(TV):
        val = x_ref[0, r].astype(F32) * mask_t[:, r : r + 1]
        acc = val if acc is None else acc + val
        totals.append(jnp.sum(val, axis=0, keepdims=True))
    store_sums(slot, tiles_ref, acc, totals, col_ref, row_ref)


def store_sums(slot, tiles_ref, acc, totals, col_ref, row_ref):
    here = pl.ds(pl.multiple_of(slot * PER, PER), PER)
    for peer in range(N_VIEW):
        col_ref[peer, here, :] = acc[peer * PER : (peer + 1) * PER]
    view_at = pl.multiple_of(tiles_ref[0, slot] * TV, TV)
    row_ref[pl.ds(view_at, TV), :] += jnp.concatenate(totals, axis=0)


def layer_body(layer, last, tiles_ref, x_ref, m_ref, ret_ref, rowp_ref, w_ref, out_ref, *sums):
    slot = pl.program_id(0)
    if not last:
        col_ref, row_ref = sums

        @pl.when(slot == 0)
        def _():
            row_ref[...] = jnp.zeros_like(row_ref)

    view_at = pl.multiple_of(tiles_ref[0, slot] * TV, TV)
    row_proj = rowp_ref[pl.ds(view_at, TV), :]
    weight = w_ref[layer]
    mask_t = m_ref[0].astype(F32).T
    here = pl.ds(pl.multiple_of(slot * PER, PER), PER)
    col_proj = ret_ref[:, here, :].reshape(TP, D)
    acc = None
    totals = []
    for r0 in range(0, TV, RC):
        block = x_ref[0, r0 : r0 + RC].reshape(RC * TP, D)
        prod = jnp.dot(block, weight, preferred_element_type=F32)
        for k in range(RC):
            r = r0 + k
            val = prod[k * TP : (k + 1) * TP] + col_proj + row_proj[r : r + 1, :]
            val = jnp.maximum(val, 0.0) * mask_t[:, r : r + 1]
            out_ref[0, r] = val.astype(BF16)
            if not last:
                acc = val if acc is None else acc + val
                totals.append(jnp.sum(val, axis=0, keepdims=True))
    if not last:
        store_sums(slot, tiles_ref, acc, totals, col_ref, row_ref)


def owner_sums(first, at_ref, got_ref, a_ref, b_ref, *sums):
    for ref in sums:
        ref[...] = jnp.zeros_like(ref)
    for d in range(N_VIEW):
        for s in range(SLOTS):
            place = at_ref[d, s]
            rows = pl.ds(pl.multiple_of(place * PER, PER), PER)
            sums[s][rows, :] += got_ref[d, s * PER : (s + 1) * PER, :]
            if first:
                line = pl.ds(2 * DATA + place, 1)
                sums[s][line, :] += got_ref[d, DATA + SLOTS + s : DATA + SLOTS + s + 1, :]
    for n, ref in enumerate((a_ref, b_ref)):
        spots = [(0, slice(n * DATA, (n + 1) * DATA), DATA)]
        if first:
            start = 2 * DATA + n * PT_DEV
            spots.append((DATA, slice(start, start + PT_DEV), PT_DEV))
            ref[DATA + PT_DEV :, :] = jnp.zeros((EXTRA - PT_DEV, D), F32)
        for to, rows, size in spots:
            ref[to : to + size, :] = (sums[0][rows, :] + sums[1][rows, :]) + (
                sums[2][rows, :] + sums[3][rows, :]
            )


def owner_project(first, layer, at_ref, me_ref, a_ref, b_ref, ra_ref, rb_ref, w_ref, bias_ref, *rest):
    if first:
        ret_ref, scale_ref, proj_ref = rest
    else:
        scale_ref, ret_ref, proj_ref = rest
    for n, (ref, rref) in enumerate(((a_ref, ra_ref), (b_ref, rb_ref))):
        if first:
            for j in range(PT_DEV):
                line = slice(DATA + j, DATA + j + 1)
                count = ref[line, :TP] + rref[line, :TP]
                at = n * DATA + j * PER
                scale_ref[at : at + PER, :] = spread(count, me_ref[0] * PER, PER)
        half = slice(n * DATA, (n + 1) * DATA)
        term = ((ref[:DATA, :] + rref[:DATA, :]) * scale_ref[half, :]).astype(BF16)
        proj = jnp.dot(term, w_ref[layer], preferred_element_type=F32)
        proj_ref[half, :] = proj + bias_ref[layer : layer + 1, :]
    for d in range(N_VIEW):
        for s in range(SLOTS):
            rows = pl.ds(pl.multiple_of(at_ref[d, s] * PER, PER), PER)
            ret_ref[d, s * PER : (s + 1) * PER, :] = proj_ref[rows, :]


def view_project(first, layer, row_ref, *rest):
    if first:
        w_ref, out_ref, scale_ref = rest
        for v in range(VT_DEV):
            count = row_ref[ROWS + v : ROWS + v + 1, :TP]
            scale_ref[v * TV : (v + 1) * TV, :] = spread(count, 0, TV)
    else:
        scale_ref, w_ref, out_ref = rest
    term = (row_ref[:ROWS, :] * scale_ref[...]).astype(BF16)
    out_ref[...] = jnp.dot(term, w_ref[layer], preferred_element_type=F32)


def array(*shape, dtype=F32):
    return jax.ShapeDtypeStruct(shape, dtype)


def call(kernel, name, out_shape, in_specs, scratch=()):
    return pl.pallas_call(
        kernel,
        out_shape=out_shape,
        in_specs=in_specs,
        out_specs=[full()] * len(out_shape),
        scratch_shapes=list(scratch),
        compiler_params=SMALL,
        name=name,
    )


def doubled(block, partner):
    route = [(i, partner(i)) for i in range(lax.axis_size("point"))]
    return block + lax.ppermute(block, "point", route)


def shards(features, tiles, masks, w_self, w_col, w_row, bias):
    barrier = lax.optimization_barrier
    smem = full(pltpu.SMEM)
    me_view = lax.axis_index("view").astype(jnp.int32)
    even = (lax.axis_index("point") % 2) == 0
    n_point = lax.axis_size("point")
    pair_a = [(i, i ^ 1) for i in range(n_point)]
    pair_b = [(i, (i + 1) % n_point if i % 2 else (i - 1) % n_point) for i in range(n_point)]
    tiles_t = pltpu.with_memory_space_constraint(tiles.T, pltpu.HBM)
    slot_shape = (SLOTS, TV, TP, D)
    ret_shape = array(N_VIEW, DATA, D)

    def whole(*shape):
        return pl.BlockSpec(shape, lambda i, t: (0,) * len(shape))

    slot_spec = pl.BlockSpec((1, TV, TP, D), lambda i, t: (i, 0, 0, 0))
    mask_spec = pl.BlockSpec((1, TV, TP), lambda i, t: (i, 0, 0))

    def by_slot(kernel, name, out_shape, in_specs, out_specs):
        return pl.pallas_call(
            kernel,
            out_shape=out_shape,
            grid_spec=pltpu.PrefetchScalarGridSpec(
                num_scalar_prefetch=1, grid=(SLOTS,), in_specs=in_specs, out_specs=out_specs
            ),
            compiler_params=LARGE,
            name=name,
        )

    masks = pltpu.with_memory_space_constraint(masks, pltpu.HBM)
    features = pltpu.with_memory_space_constraint(features, pltpu.HBM)
    col_pay, row_sum = by_slot(
        first_sums,
        "first_sums",
        [array(N_VIEW, DATA + EXTRA, D), array(ROWS + 8, D)],
        [slot_spec, mask_spec],
        [whole(N_VIEW, DATA + EXTRA, D), whole(ROWS + 8, D)],
    )(tiles_t, features, masks)

    state = features
    place = col_scale = row_scale = None
    for layer in range(LAYERS):
        first = layer == 0
        last = layer == LAYERS - 1
        got = lax.all_to_all(col_pay, "view", 0, 0, tiled=True)
        row_sum = doubled(row_sum, lambda i: i ^ 8)
        got, row_sum = barrier((got, row_sum))
        row_sum = doubled(row_sum, lambda i: i ^ 2)
        if first:
            point_id = got[:, DATA : DATA + SLOTS, 0].astype(jnp.int32)
            place = jnp.where(even, point_id ^ PT_DEV, point_id)
        extra = EXTRA if first else 0
        part_a, part_b = call(
            functools.partial(owner_sums, first),
            "owner_sums",
            [array(DATA + extra, D)] * 2,
            [smem, full()],
            [pltpu.VMEM((2 * DATA + extra, D), F32)] * SLOTS,
        )(place, got)
        from_a = lax.ppermute(part_a, "point", pair_a)
        from_b = lax.ppermute(part_b, "point", pair_b)
        row_sum = doubled(row_sum, lambda i: i ^ 1)
        from_a, from_b, row_sum = barrier((from_a, from_b, row_sum))
        row_sum = doubled(row_sum, lambda i: i ^ 6)
        outs = call(
            functools.partial(owner_project, first, layer),
            "owner_project",
            [ret_shape] + ([array(2 * DATA, D)] if first else []),
            [smem, smem] + [full()] * (6 if first else 7),
            [pltpu.VMEM((2 * DATA, D), F32)],
        )(
            place,
            me_view[None],
            part_a,
            part_b,
            from_a,
            from_b,
            w_col,
            bias,
            *(() if first else (col_scale,)),
        )
        if first:
            col_scale = outs[1]
        back = lax.all_to_all(outs[0], "view", 0, 0, tiled=True)
        outs = call(
            functools.partial(view_project, first, layer),
            "view_project",
            [array(ROWS, D)] * (2 if first else 1),
            [full()] * (2 if first else 3),
        )(row_sum, *(() if first else (row_scale,)), w_row)
        row_proj = outs[0]
        if first:
            row_scale = outs[1]
        outs = by_slot(
            functools.partial(layer_body, layer, last),
            "layer_body",
            [array(*slot_shape, dtype=BF16)] + ([] if last else [ret_shape, array(ROWS, D)]),
            [
                slot_spec,
                mask_spec,
                whole(N_VIEW, DATA, D),
                whole(ROWS, D),
                whole(LAYERS, D, D),
            ],
            [slot_spec] + ([] if last else [whole(N_VIEW, DATA, D), whole(ROWS, D)]),
        )(tiles_t, state, masks, back, row_proj, w_self)
        if last:
            return outs[0]
        state, col_pay, row_sum = outs


def solution(mesh):
    in_specs = (
        P(("view", "point"), None, None, None),
        P(("view", "point"), None),
        P(("view", "point"), None, None),
        P(),
        P(),
        P(),
        P(),
    )
    out_specs = P(("view", "point"), None, None, None)
    return jax.shard_map(shards, mesh=mesh, in_specs=in_specs, out_specs=out_specs, check_vma=False)
```

```python
import functools

import jax
import jax.numpy as jnp
from jax import lax
from jax.experimental import pallas as pl
from jax.experimental.pallas import tpu as pltpu
from jax.sharding import PartitionSpec as P

VT_DEV = 4
PT_DEV = 4
LAYERS = 3
SLOTS = 4
TV = 32
TP = 128
D = 256
N_VIEW = 8
PER = TP // N_VIEW
DATA = SLOTS * PER
EXTRA = 8
ROWS = VT_DEV * TV
RC = 4
F32 = jnp.float32
BF16 = jnp.bfloat16
SMALL = pltpu.CompilerParams(vmem_limit_bytes=8 * 1024 * 1024)
LARGE = pltpu.CompilerParams(vmem_limit_bytes=48 * 1024 * 1024)


def full(memory_space=pltpu.VMEM):
    return pl.BlockSpec(memory_space=memory_space)


def spread(counts, first_lane, rows):
    lane = lax.broadcasted_iota(jnp.int32, (rows, TP), 1)
    line = lax.broadcasted_iota(jnp.int32, (rows, TP), 0) + first_lane
    picked = jnp.where(lane == line, jnp.broadcast_to(counts, (rows, TP)), 0.0)
    count = jnp.sum(picked, axis=1, keepdims=True)
    return jnp.broadcast_to(1.0 / jnp.sqrt(jnp.maximum(count, 1.0)), (rows, D))


def first_sums(tiles_ref, x_ref, m_ref, col_ref, row_ref):
    slot = pl.program_id(0)
    mask = m_ref[0].astype(F32)
    mask_t = mask.T
    col_count = jnp.sum(mask, axis=0, keepdims=True)
    row_count = jnp.sum(mask_t, axis=0, keepdims=True)
    padded = jnp.concatenate([col_count, jnp.zeros((1, D - TP), F32)], axis=1)
    padded_row = jnp.concatenate([row_count, jnp.zeros((1, D - TV), F32)], axis=1)
    point_id = jnp.full((1, D), tiles_ref[1, slot], jnp.int32).astype(F32)

    @pl.when(slot == 0)
    def _():
        row_ref[...] = jnp.zeros_like(row_ref)

    for s in range(SLOTS):

        @pl.when(slot == s)
        def _():
            for peer in range(N_VIEW):
                col_ref[peer, DATA + s : DATA + s + 1, :] = point_id
                col_ref[peer, DATA + SLOTS + s : DATA + SLOTS + s + 1, :] = padded

    for v in range(VT_DEV):
        hit = jnp.where(tiles_ref[0, slot] == v, 1.0, 0.0).astype(F32)
        row_ref[ROWS + v : ROWS + v + 1, :] += padded_row * hit
    acc = None
    totals = []
    for r in range(TV):
        val = x_ref[0, r].astype(F32) * mask_t[:, r : r + 1]
        acc = val if acc is None else acc + val
        totals.append(jnp.sum(val, axis=0, keepdims=True))
    store_sums(slot, tiles_ref, acc, totals, col_ref, row_ref)


def store_sums(slot, tiles_ref, acc, totals, col_ref, row_ref):
    here = pl.ds(pl.multiple_of(slot * PER, PER), PER)
    for peer in range(N_VIEW):
        col_ref[peer, here, :] = acc[peer * PER : (peer + 1) * PER]
    view_at = pl.multiple_of(tiles_ref[0, slot] * TV, TV)
    row_ref[pl.ds(view_at, TV), :] += jnp.concatenate(totals, axis=0)


def layer_body(layer, last, tiles_ref, x_ref, m_ref, ret_ref, rowp_ref, w_ref, out_ref, *sums):
    slot = pl.program_id(0)
    if not last:
        col_ref, row_ref = sums

        @pl.when(slot == 0)
        def _():
            row_ref[...] = jnp.zeros_like(row_ref)

    view_at = pl.multiple_of(tiles_ref[0, slot] * TV, TV)
    row_proj = rowp_ref[pl.ds(view_at, TV), :]
    weight = w_ref[layer]
    mask_t = m_ref[0].astype(F32).T
    here = pl.ds(pl.multiple_of(slot * PER, PER), PER)
    col_proj = ret_ref[:, here, :].reshape(TP, D)
    acc = None
    totals = []
    for r0 in range(0, TV, RC):
        block = x_ref[0, r0 : r0 + RC].reshape(RC * TP, D)
        prod = jnp.dot(block, weight, preferred_element_type=F32)
        for k in range(RC):
            r = r0 + k
            val = prod[k * TP : (k + 1) * TP] + col_proj + row_proj[r : r + 1, :]
            val = jnp.maximum(val, 0.0) * mask_t[:, r : r + 1]
            out_ref[0, r] = val.astype(BF16)
            if not last:
                acc = val if acc is None else acc + val
                totals.append(jnp.sum(val, axis=0, keepdims=True))
    if not last:
        store_sums(slot, tiles_ref, acc, totals, col_ref, row_ref)


def owner_sums(first, at_ref, got_ref, a_ref, b_ref, *sums):
    for ref in sums:
        ref[...] = jnp.zeros_like(ref)
    for d in range(N_VIEW):
        for s in range(SLOTS):
            place = at_ref[d, s]
            rows = pl.ds(pl.multiple_of(place * PER, PER), PER)
            sums[s][rows, :] += got_ref[d, s * PER : (s + 1) * PER, :]
            if first:
                line = pl.ds(2 * DATA + place, 1)
                sums[s][line, :] += got_ref[d, DATA + SLOTS + s : DATA + SLOTS + s + 1, :]
    for n, ref in enumerate((a_ref, b_ref)):
        spots = [(0, slice(n * DATA, (n + 1) * DATA), DATA)]
        if first:
            start = 2 * DATA + n * PT_DEV
            spots.append((DATA, slice(start, start + PT_DEV), PT_DEV))
            ref[DATA + PT_DEV :, :] = jnp.zeros((EXTRA - PT_DEV, D), F32)
        for to, rows, size in spots:
            ref[to : to + size, :] = (sums[0][rows, :] + sums[1][rows, :]) + (
                sums[2][rows, :] + sums[3][rows, :]
            )


def owner_project(first, layer, at_ref, me_ref, a_ref, b_ref, ra_ref, rb_ref, w_ref, bias_ref, *rest):
    if first:
        ret_ref, scale_ref, proj_ref = rest
    else:
        scale_ref, ret_ref, proj_ref = rest
    for n, (ref, rref) in enumerate(((a_ref, ra_ref), (b_ref, rb_ref))):
        if first:
            for j in range(PT_DEV):
                line = slice(DATA + j, DATA + j + 1)
                count = ref[line, :TP] + rref[line, :TP]
                at = n * DATA + j * PER
                scale_ref[at : at + PER, :] = spread(count, me_ref[0] * PER, PER)
        half = slice(n * DATA, (n + 1) * DATA)
        term = ((ref[:DATA, :] + rref[:DATA, :]) * scale_ref[half, :]).astype(BF16)
        proj = jnp.dot(term, w_ref[layer], preferred_element_type=F32)
        proj_ref[half, :] = proj + bias_ref[layer : layer + 1, :]
    for d in range(N_VIEW):
        for s in range(SLOTS):
            rows = pl.ds(pl.multiple_of(at_ref[d, s] * PER, PER), PER)
            ret_ref[d, s * PER : (s + 1) * PER, :] = proj_ref[rows, :]


def view_project(first, layer, row_ref, *rest):
    if first:
        w_ref, out_ref, scale_ref = rest
        for v in range(VT_DEV):
            count = row_ref[ROWS + v : ROWS + v + 1, :TP]
            scale_ref[v * TV : (v + 1) * TV, :] = spread(count, 0, TV)
    else:
        scale_ref, w_ref, out_ref = rest
    term = (row_ref[:ROWS, :] * scale_ref[...]).astype(BF16)
    out_ref[...] = jnp.dot(term, w_ref[layer], preferred_element_type=F32)


def array(*shape, dtype=F32):
    return jax.ShapeDtypeStruct(shape, dtype)


def call(kernel, name, out_shape, in_specs, scratch=()):
    return pl.pallas_call(
        kernel,
        out_shape=out_shape,
        in_specs=in_specs,
        out_specs=[full()] * len(out_shape),
        scratch_shapes=list(scratch),
        compiler_params=SMALL,
        name=name,
    )


def doubled(block, partner):
    route = [(i, partner(i)) for i in range(lax.axis_size("point"))]
    return block + lax.ppermute(block, "point", route)


def shards(features, tiles, masks, w_self, w_col, w_row, bias):
    barrier = lax.optimization_barrier
    smem = full(pltpu.SMEM)
    me_view = lax.axis_index("view").astype(jnp.int32)
    even = (lax.axis_index("point") % 2) == 0
    n_point = lax.axis_size("point")
    pair_a = [(i, i ^ 1) for i in range(n_point)]
    pair_b = [(i, (i + 1) % n_point if i % 2 else (i - 1) % n_point) for i in range(n_point)]
    tiles_t = pltpu.with_memory_space_constraint(tiles.T, pltpu.HBM)
    slot_shape = (SLOTS, TV, TP, D)
    ret_shape = array(N_VIEW, DATA, D)

    def whole(*shape):
        return pl.BlockSpec(shape, lambda i, t: (0,) * len(shape))

    slot_spec = pl.BlockSpec((1, TV, TP, D), lambda i, t: (i, 0, 0, 0))
    mask_spec = pl.BlockSpec((1, TV, TP), lambda i, t: (i, 0, 0))

    def by_slot(kernel, name, out_shape, in_specs, out_specs):
        return pl.pallas_call(
            kernel,
            out_shape=out_shape,
            grid_spec=pltpu.PrefetchScalarGridSpec(
                num_scalar_prefetch=1, grid=(SLOTS,), in_specs=in_specs, out_specs=out_specs
            ),
            compiler_params=LARGE,
            name=name,
        )

    masks = pltpu.with_memory_space_constraint(masks, pltpu.HBM)
    features = pltpu.with_memory_space_constraint(features, pltpu.HBM)
    col_pay, row_sum = by_slot(
        first_sums,
        "first_sums",
        [array(N_VIEW, DATA + EXTRA, D), array(ROWS + 8, D)],
        [slot_spec, mask_spec],
        [whole(N_VIEW, DATA + EXTRA, D), whole(ROWS + 8, D)],
    )(tiles_t, features, masks)

    state = features
    place = col_scale = row_scale = None
    for layer in range(LAYERS):
        first = layer == 0
        last = layer == LAYERS - 1
        got = lax.all_to_all(col_pay, "view", 0, 0, tiled=True)
        row_sum = doubled(row_sum, lambda i: i ^ 2)
        row_sum = doubled(row_sum, lambda i: i ^ 1)
        got, row_sum = barrier((got, row_sum))
        if first:
            point_id = got[:, DATA : DATA + SLOTS, 0].astype(jnp.int32)
            place = jnp.where(even, point_id ^ PT_DEV, point_id)
        extra = EXTRA if first else 0
        part_a, part_b = call(
            functools.partial(owner_sums, first),
            "owner_sums",
            [array(DATA + extra, D)] * 2,
            [smem, full()],
            [pltpu.VMEM((2 * DATA + extra, D), F32)] * SLOTS,
        )(place, got)
        part_a, part_b, row_sum = barrier((part_a, part_b, row_sum))
        from_b = lax.ppermute(part_b, "point", pair_b)
        from_a = lax.ppermute(part_a, "point", pair_a)
        row_sum = doubled(row_sum, lambda i: i ^ 6)
        from_a, from_b, row_sum = barrier((from_a, from_b, row_sum))
        row_sum = doubled(row_sum, lambda i: i ^ 8)
        outs = call(
            functools.partial(owner_project, first, layer),
            "owner_project",
            [ret_shape] + ([array(2 * DATA, D)] if first else []),
            [smem, smem] + [full()] * (6 if first else 7),
            [pltpu.VMEM((2 * DATA, D), F32)],
        )(
            place,
            me_view[None],
            part_a,
            part_b,
            from_a,
            from_b,
            w_col,
            bias,
            *(() if first else (col_scale,)),
        )
        if first:
            col_scale = outs[1]
        back = lax.all_to_all(outs[0], "view", 0, 0, tiled=True)
        outs = call(
            functools.partial(view_project, first, layer),
            "view_project",
            [array(ROWS, D)] * (2 if first else 1),
            [full()] * (2 if first else 3),
        )(row_sum, *(() if first else (row_scale,)), w_row)
        row_proj = outs[0]
        if first:
            row_scale = outs[1]
        outs = by_slot(
            functools.partial(layer_body, layer, last),
            "layer_body",
            [array(*slot_shape, dtype=BF16)] + ([] if last else [ret_shape, array(ROWS, D)]),
            [
                slot_spec,
                mask_spec,
                whole(N_VIEW, DATA, D),
                whole(ROWS, D),
                whole(LAYERS, D, D),
            ],
            [slot_spec] + ([] if last else [whole(N_VIEW, DATA, D), whole(ROWS, D)]),
        )(tiles_t, state, masks, back, row_proj, w_self)
        if last:
            return outs[0]
        state, col_pay, row_sum = outs


def solution(mesh):
    in_specs = (
        P(("view", "point"), None, None, None),
        P(("view", "point"), None),
        P(("view", "point"), None, None),
        P(),
        P(),
        P(),
        P(),
    )
    out_specs = P(("view", "point"), None, None, None)
    return jax.shard_map(shards, mesh=mesh, in_specs=in_specs, out_specs=out_specs, check_vma=False)
```

```python
import functools

import jax
import jax.numpy as jnp
from jax import lax
from jax.experimental import pallas as pl
from jax.experimental.pallas import tpu as pltpu
from jax.sharding import PartitionSpec as P

VT_DEV = 4
PT_DEV = 4
LAYERS = 3
SLOTS = 4
TV = 32
TP = 128
D = 256
N_VIEW = 8
PER = TP // N_VIEW
DATA = SLOTS * PER
EXTRA = 8
ROWS = VT_DEV * TV
RC = 4
EARLY = pl.CostEstimate(flops=40_000_000_000, transcendentals=0, bytes_accessed=100_000_000)
F32 = jnp.float32
BF16 = jnp.bfloat16
SMALL = pltpu.CompilerParams(vmem_limit_bytes=8 * 1024 * 1024)
LARGE = pltpu.CompilerParams(vmem_limit_bytes=48 * 1024 * 1024)


def full(memory_space=pltpu.VMEM):
    return pl.BlockSpec(memory_space=memory_space)


def spread(counts, first_lane, rows):
    lane = lax.broadcasted_iota(jnp.int32, (rows, TP), 1)
    line = lax.broadcasted_iota(jnp.int32, (rows, TP), 0) + first_lane
    picked = jnp.where(lane == line, jnp.broadcast_to(counts, (rows, TP)), 0.0)
    count = jnp.sum(picked, axis=1, keepdims=True)
    return jnp.broadcast_to(1.0 / jnp.sqrt(jnp.maximum(count, 1.0)), (rows, D))


def first_sums(tiles_ref, x_ref, m_ref, col_ref, row_ref):
    slot = pl.program_id(0)
    mask = m_ref[0].astype(F32)
    mask_t = mask.T
    col_count = jnp.sum(mask, axis=0, keepdims=True)
    row_count = jnp.sum(mask_t, axis=0, keepdims=True)
    padded = jnp.concatenate([col_count, jnp.zeros((1, D - TP), F32)], axis=1)
    padded_row = jnp.concatenate([row_count, jnp.zeros((1, D - TV), F32)], axis=1)
    point_id = jnp.full((1, D), tiles_ref[1, slot], jnp.int32).astype(F32)

    @pl.when(slot == 0)
    def _():
        row_ref[...] = jnp.zeros_like(row_ref)

    for s in range(SLOTS):

        @pl.when(slot == s)
        def _():
            for peer in range(N_VIEW):
                col_ref[peer, DATA + s : DATA + s + 1, :] = point_id
                col_ref[peer, DATA + SLOTS + s : DATA + SLOTS + s + 1, :] = padded

    for v in range(VT_DEV):
        hit = jnp.where(tiles_ref[0, slot] == v, 1.0, 0.0).astype(F32)
        row_ref[ROWS + v : ROWS + v + 1, :] += padded_row * hit
    acc = None
    totals = []
    for r in range(TV):
        val = x_ref[0, r].astype(F32) * mask_t[:, r : r + 1]
        acc = val if acc is None else acc + val
        totals.append(jnp.sum(val, axis=0, keepdims=True))
    store_sums(slot, tiles_ref, acc, totals, col_ref, row_ref)


def store_sums(slot, tiles_ref, acc, totals, col_ref, row_ref):
    here = pl.ds(pl.multiple_of(slot * PER, PER), PER)
    for peer in range(N_VIEW):
        col_ref[peer, here, :] = acc[peer * PER : (peer + 1) * PER]
    view_at = pl.multiple_of(tiles_ref[0, slot] * TV, TV)
    row_ref[pl.ds(view_at, TV), :] += jnp.concatenate(totals, axis=0)


def layer_body(layer, last, tiles_ref, x_ref, m_ref, ret_ref, rowp_ref, w_ref, out_ref, *sums):
    slot = pl.program_id(0)
    if not last:
        col_ref, row_ref = sums

        @pl.when(slot == 0)
        def _():
            row_ref[...] = jnp.zeros_like(row_ref)

    view_at = pl.multiple_of(tiles_ref[0, slot] * TV, TV)
    row_proj = rowp_ref[pl.ds(view_at, TV), :]
    weight = w_ref[layer]
    mask_t = m_ref[0].astype(F32).T
    here = pl.ds(pl.multiple_of(slot * PER, PER), PER)
    col_proj = ret_ref[:, here, :].reshape(TP, D)
    acc = None
    totals = []
    for r0 in range(0, TV, RC):
        block = x_ref[0, r0 : r0 + RC].reshape(RC * TP, D)
        prod = jnp.dot(block, weight, preferred_element_type=F32)
        for k in range(RC):
            r = r0 + k
            val = prod[k * TP : (k + 1) * TP] + col_proj + row_proj[r : r + 1, :]
            val = jnp.maximum(val, 0.0) * mask_t[:, r : r + 1]
            out_ref[0, r] = val.astype(BF16)
            if not last:
                acc = val if acc is None else acc + val
                totals.append(jnp.sum(val, axis=0, keepdims=True))
    if not last:
        store_sums(slot, tiles_ref, acc, totals, col_ref, row_ref)


def owner_sums(first, at_ref, got_ref, a_ref, b_ref, *sums):
    for ref in sums:
        ref[...] = jnp.zeros_like(ref)
    for d in range(N_VIEW):
        for s in range(SLOTS):
            place = at_ref[d, s]
            rows = pl.ds(pl.multiple_of(place * PER, PER), PER)
            sums[s][rows, :] += got_ref[d, s * PER : (s + 1) * PER, :]
            if first:
                line = pl.ds(2 * DATA + place, 1)
                sums[s][line, :] += got_ref[d, DATA + SLOTS + s : DATA + SLOTS + s + 1, :]
    for n, ref in enumerate((a_ref, b_ref)):
        spots = [(0, slice(n * DATA, (n + 1) * DATA), DATA)]
        if first:
            start = 2 * DATA + n * PT_DEV
            spots.append((DATA, slice(start, start + PT_DEV), PT_DEV))
            ref[DATA + PT_DEV :, :] = jnp.zeros((EXTRA - PT_DEV, D), F32)
        for to, rows, size in spots:
            ref[to : to + size, :] = (sums[0][rows, :] + sums[1][rows, :]) + (
                sums[2][rows, :] + sums[3][rows, :]
            )


def owner_project(first, layer, at_ref, me_ref, a_ref, b_ref, ra_ref, rb_ref, w_ref, bias_ref, *rest):
    if first:
        ret_ref, scale_ref, proj_ref = rest
    else:
        scale_ref, ret_ref, proj_ref = rest
    for n, (ref, rref) in enumerate(((a_ref, ra_ref), (b_ref, rb_ref))):
        if first:
            for j in range(PT_DEV):
                line = slice(DATA + j, DATA + j + 1)
                count = ref[line, :TP] + rref[line, :TP]
                at = n * DATA + j * PER
                scale_ref[at : at + PER, :] = spread(count, me_ref[0] * PER, PER)
        half = slice(n * DATA, (n + 1) * DATA)
        term = ((ref[:DATA, :] + rref[:DATA, :]) * scale_ref[half, :]).astype(BF16)
        proj = jnp.dot(term, w_ref[layer], preferred_element_type=F32)
        proj_ref[half, :] = proj + bias_ref[layer : layer + 1, :]
    for d in range(N_VIEW):
        for s in range(SLOTS):
            rows = pl.ds(pl.multiple_of(at_ref[d, s] * PER, PER), PER)
            ret_ref[d, s * PER : (s + 1) * PER, :] = proj_ref[rows, :]


def add_rows(mine_ref, other_ref, out_ref):
    out_ref[...] = mine_ref[...] + other_ref[...]


def view_project(first, layer, row_ref, other_ref, *rest):
    if first:
        w_ref, out_ref, scale_ref = rest
        for v in range(VT_DEV):
            line = slice(ROWS + v, ROWS + v + 1)
            count = row_ref[line, :TP] + other_ref[line, :TP]
            scale_ref[v * TV : (v + 1) * TV, :] = spread(count, 0, TV)
    else:
        scale_ref, w_ref, out_ref = rest
    total = row_ref[:ROWS, :] + other_ref[:ROWS, :]
    term = (total * scale_ref[...]).astype(BF16)
    out_ref[...] = jnp.dot(term, w_ref[layer], preferred_element_type=F32)


def array(*shape, dtype=F32):
    return jax.ShapeDtypeStruct(shape, dtype)


def call(kernel, name, out_shape, in_specs, scratch=(), cost=None):
    return pl.pallas_call(
        kernel,
        out_shape=out_shape,
        in_specs=in_specs,
        out_specs=[full()] * len(out_shape),
        scratch_shapes=list(scratch),
        compiler_params=SMALL,
        cost_estimate=cost,
        name=name,
    )


def from_partner(block, flip):
    route = [(i, i ^ flip) for i in range(lax.axis_size("point"))]
    return lax.ppermute(block, "point", route)


def doubled(block, flip):
    return block + from_partner(block, flip)


def shards(features, tiles, masks, w_self, w_col, w_row, bias):
    barrier = lax.optimization_barrier
    smem = full(pltpu.SMEM)
    me_view = lax.axis_index("view").astype(jnp.int32)
    even = (lax.axis_index("point") % 2) == 0
    n_point = lax.axis_size("point")
    pair_a = [(i, i ^ 1) for i in range(n_point)]
    pair_b = [(i, (i + 1) % n_point if i % 2 else (i - 1) % n_point) for i in range(n_point)]
    tiles_t = pltpu.with_memory_space_constraint(tiles.T, pltpu.HBM)
    slot_shape = (SLOTS, TV, TP, D)
    ret_shape = array(N_VIEW, DATA, D)

    def whole(*shape):
        return pl.BlockSpec(shape, lambda i, t: (0,) * len(shape))

    slot_spec = pl.BlockSpec((1, TV, TP, D), lambda i, t: (i, 0, 0, 0))
    mask_spec = pl.BlockSpec((1, TV, TP), lambda i, t: (i, 0, 0))

    def by_slot(kernel, name, out_shape, in_specs, out_specs):
        return pl.pallas_call(
            kernel,
            out_shape=out_shape,
            grid_spec=pltpu.PrefetchScalarGridSpec(
                num_scalar_prefetch=1, grid=(SLOTS,), in_specs=in_specs, out_specs=out_specs
            ),
            compiler_params=LARGE,
            name=name,
        )

    masks = pltpu.with_memory_space_constraint(masks, pltpu.HBM)
    features = pltpu.with_memory_space_constraint(features, pltpu.HBM)
    col_pay, row_sum = by_slot(
        first_sums,
        "first_sums",
        [array(N_VIEW, DATA + EXTRA, D), array(ROWS + 8, D)],
        [slot_spec, mask_spec],
        [whole(N_VIEW, DATA + EXTRA, D), whole(ROWS + 8, D)],
    )(tiles_t, features, masks)

    state = features
    place = col_scale = row_scale = None
    for layer in range(LAYERS):
        first = layer == 0
        last = layer == LAYERS - 1
        got = lax.all_to_all(col_pay, "view", 0, 0, tiled=True)
        (row_sum,) = call(
            add_rows, "add_rows", [array(*row_sum.shape)], [full()] * 2, cost=EARLY
        )(row_sum, from_partner(row_sum, 2))
        row_sum = doubled(row_sum, 1)
        got, row_sum = barrier((got, row_sum))
        if first:
            point_id = got[:, DATA : DATA + SLOTS, 0].astype(jnp.int32)
            place = jnp.where(even, point_id ^ PT_DEV, point_id)
        extra = EXTRA if first else 0
        part_a, part_b = call(
            functools.partial(owner_sums, first),
            "owner_sums",
            [array(DATA + extra, D)] * 2,
            [smem, full()],
            [pltpu.VMEM((2 * DATA + extra, D), F32)] * SLOTS,
        )(place, got)
        part_a, part_b, row_sum = barrier((part_a, part_b, row_sum))
        from_b = lax.ppermute(part_b, "point", pair_b)
        from_a = lax.ppermute(part_a, "point", pair_a)
        row_sum = doubled(row_sum, 6)
        from_a, from_b, row_sum = barrier((from_a, from_b, row_sum))
        row_other = from_partner(row_sum, 8)
        outs = call(
            functools.partial(owner_project, first, layer),
            "owner_project",
            [ret_shape] + ([array(2 * DATA, D)] if first else []),
            [smem, smem] + [full()] * (6 if first else 7),
            [pltpu.VMEM((2 * DATA, D), F32)],
        )(
            place,
            me_view[None],
            part_a,
            part_b,
            from_a,
            from_b,
            w_col,
            bias,
            *(() if first else (col_scale,)),
        )
        if first:
            col_scale = outs[1]
        back = lax.all_to_all(outs[0], "view", 0, 0, tiled=True)
        outs = call(
            functools.partial(view_project, first, layer),
            "view_project",
            [array(ROWS, D)] * (2 if first else 1),
            [full()] * (3 if first else 4),
            cost=EARLY,
        )(row_sum, row_other, *(() if first else (row_scale,)), w_row)
        row_proj = outs[0]
        if first:
            row_scale = outs[1]
        outs = by_slot(
            functools.partial(layer_body, layer, last),
            "layer_body",
            [array(*slot_shape, dtype=BF16)] + ([] if last else [ret_shape, array(ROWS, D)]),
            [
                slot_spec,
                mask_spec,
                whole(N_VIEW, DATA, D),
                whole(ROWS, D),
                whole(LAYERS, D, D),
            ],
            [slot_spec] + ([] if last else [whole(N_VIEW, DATA, D), whole(ROWS, D)]),
        )(tiles_t, state, masks, back, row_proj, w_self)
        if last:
            return outs[0]
        state, col_pay, row_sum = outs


def solution(mesh):
    in_specs = (
        P(("view", "point"), None, None, None),
        P(("view", "point"), None),
        P(("view", "point"), None, None),
        P(),
        P(),
        P(),
        P(),
    )
    out_specs = P(("view", "point"), None, None, None)
    return jax.shard_map(shards, mesh=mesh, in_specs=in_specs, out_specs=out_specs, check_vma=False)
```

```python
import functools

import jax
import jax.numpy as jnp
from jax import lax
from jax.experimental import pallas as pl
from jax.experimental.pallas import tpu as pltpu
from jax.sharding import PartitionSpec as P

VT_DEV = 4
PT_DEV = 4
LAYERS = 3
SLOTS = 4
TV = 32
TP = 128
D = 256
N_VIEW = 8
PER = TP // N_VIEW
DATA = SLOTS * PER
EXTRA = 8
ROWS = VT_DEV * TV
RC = 4
EARLY = pl.CostEstimate(flops=40_000_000_000, transcendentals=0, bytes_accessed=100_000_000)
F32 = jnp.float32
BF16 = jnp.bfloat16
SMALL = pltpu.CompilerParams(vmem_limit_bytes=8 * 1024 * 1024)
LARGE = pltpu.CompilerParams(vmem_limit_bytes=48 * 1024 * 1024)


def full(memory_space=pltpu.VMEM):
    return pl.BlockSpec(memory_space=memory_space)


def spread(counts, first_lane, rows):
    lane = lax.broadcasted_iota(jnp.int32, (rows, TP), 1)
    line = lax.broadcasted_iota(jnp.int32, (rows, TP), 0) + first_lane
    picked = jnp.where(lane == line, jnp.broadcast_to(counts, (rows, TP)), 0.0)
    count = jnp.sum(picked, axis=1, keepdims=True)
    return jnp.broadcast_to(1.0 / jnp.sqrt(jnp.maximum(count, 1.0)), (rows, D))


def first_sums(tiles_ref, x_ref, m_ref, col_ref, row_ref):
    slot = pl.program_id(0)
    mask = m_ref[0].astype(F32)
    mask_t = mask.T
    col_count = jnp.sum(mask, axis=0, keepdims=True)
    row_count = jnp.sum(mask_t, axis=0, keepdims=True)
    padded = jnp.concatenate([col_count, jnp.zeros((1, D - TP), F32)], axis=1)
    padded_row = jnp.concatenate([row_count, jnp.zeros((1, D - TV), F32)], axis=1)
    point_id = jnp.full((1, D), tiles_ref[1, slot], jnp.int32).astype(F32)

    @pl.when(slot == 0)
    def _():
        row_ref[...] = jnp.zeros_like(row_ref)

    for s in range(SLOTS):

        @pl.when(slot == s)
        def _():
            for peer in range(N_VIEW):
                col_ref[peer, DATA + s : DATA + s + 1, :] = point_id
                col_ref[peer, DATA + SLOTS + s : DATA + SLOTS + s + 1, :] = padded

    for v in range(VT_DEV):
        hit = jnp.where(tiles_ref[0, slot] == v, 1.0, 0.0).astype(F32)
        row_ref[ROWS + v : ROWS + v + 1, :] += padded_row * hit
    acc = None
    totals = []
    for r in range(TV):
        val = x_ref[0, r].astype(F32) * mask_t[:, r : r + 1]
        acc = val if acc is None else acc + val
        totals.append(jnp.sum(val, axis=0, keepdims=True))
    store_sums(slot, tiles_ref, acc, totals, col_ref, row_ref)


def store_sums(slot, tiles_ref, acc, totals, col_ref, row_ref):
    here = pl.ds(pl.multiple_of(slot * PER, PER), PER)
    for peer in range(N_VIEW):
        col_ref[peer, here, :] = acc[peer * PER : (peer + 1) * PER]
    view_at = pl.multiple_of(tiles_ref[0, slot] * TV, TV)
    row_ref[pl.ds(view_at, TV), :] += jnp.concatenate(totals, axis=0)


def layer_body(layer, last, tiles_ref, x_ref, m_ref, ret_ref, rowp_ref, w_ref, out_ref, *sums):
    slot = pl.program_id(0)
    if not last:
        col_ref, row_ref = sums

        @pl.when(slot == 0)
        def _():
            row_ref[...] = jnp.zeros_like(row_ref)

    view_at = pl.multiple_of(tiles_ref[0, slot] * TV, TV)
    row_proj = rowp_ref[pl.ds(view_at, TV), :]
    weight = w_ref[layer]
    mask_t = m_ref[0].astype(F32).T
    here = pl.ds(pl.multiple_of(slot * PER, PER), PER)
    col_proj = ret_ref[:, here, :].reshape(TP, D)
    acc = None
    totals = []
    for r0 in range(0, TV, RC):
        block = x_ref[0, r0 : r0 + RC].reshape(RC * TP, D)
        prod = jnp.dot(block, weight, preferred_element_type=F32)
        for k in range(RC):
            r = r0 + k
            val = prod[k * TP : (k + 1) * TP] + col_proj + row_proj[r : r + 1, :]
            val = jnp.maximum(val, 0.0) * mask_t[:, r : r + 1]
            out_ref[0, r] = val.astype(BF16)
            if not last:
                acc = val if acc is None else acc + val
                totals.append(jnp.sum(val, axis=0, keepdims=True))
    if not last:
        store_sums(slot, tiles_ref, acc, totals, col_ref, row_ref)


def owner_sums(first, at_ref, got_ref, row_ref, a_ref, b_ref, *sums):
    b_ref[a_ref.shape[0] :, :] = row_ref[...]
    for ref in sums:
        ref[...] = jnp.zeros_like(ref)
    for d in range(N_VIEW):
        for s in range(SLOTS):
            place = at_ref[d, s]
            rows = pl.ds(pl.multiple_of(place * PER, PER), PER)
            sums[s][rows, :] += got_ref[d, s * PER : (s + 1) * PER, :]
            if first:
                line = pl.ds(2 * DATA + place, 1)
                sums[s][line, :] += got_ref[d, DATA + SLOTS + s : DATA + SLOTS + s + 1, :]
    for n, ref in enumerate((a_ref, b_ref)):
        spots = [(0, slice(n * DATA, (n + 1) * DATA), DATA)]
        if first:
            start = 2 * DATA + n * PT_DEV
            spots.append((DATA, slice(start, start + PT_DEV), PT_DEV))
            ref[DATA + PT_DEV : DATA + EXTRA, :] = jnp.zeros((EXTRA - PT_DEV, D), F32)
        for to, rows, size in spots:
            ref[to : to + size, :] = (sums[0][rows, :] + sums[1][rows, :]) + (
                sums[2][rows, :] + sums[3][rows, :]
            )


def owner_project(first, layer, at_ref, me_ref, a_ref, b_ref, ra_ref, rb_ref, w_ref, bias_ref, *rest):
    if first:
        ret_ref, row_ref, scale_ref, proj_ref = rest
    else:
        scale_ref, ret_ref, row_ref, proj_ref = rest
    row_ref[...] = b_ref[a_ref.shape[0] :, :] + rb_ref[a_ref.shape[0] :, :]
    for n, (ref, rref) in enumerate(((a_ref, ra_ref), (b_ref, rb_ref))):
        if first:
            for j in range(PT_DEV):
                line = slice(DATA + j, DATA + j + 1)
                count = ref[line, :TP] + rref[line, :TP]
                at = n * DATA + j * PER
                scale_ref[at : at + PER, :] = spread(count, me_ref[0] * PER, PER)
        half = slice(n * DATA, (n + 1) * DATA)
        term = ((ref[:DATA, :] + rref[:DATA, :]) * scale_ref[half, :]).astype(BF16)
        proj = jnp.dot(term, w_ref[layer], preferred_element_type=F32)
        proj_ref[half, :] = proj + bias_ref[layer : layer + 1, :]
    for d in range(N_VIEW):
        for s in range(SLOTS):
            rows = pl.ds(pl.multiple_of(at_ref[d, s] * PER, PER), PER)
            ret_ref[d, s * PER : (s + 1) * PER, :] = proj_ref[rows, :]


def add_rows(mine_ref, other_ref, out_ref):
    out_ref[...] = mine_ref[...] + other_ref[...]


def view_project(first, layer, row_ref, other_ref, *rest):
    if first:
        w_ref, out_ref, scale_ref = rest
        for v in range(VT_DEV):
            line = slice(ROWS + v, ROWS + v + 1)
            count = row_ref[line, :TP] + other_ref[line, :TP]
            scale_ref[v * TV : (v + 1) * TV, :] = spread(count, 0, TV)
    else:
        scale_ref, w_ref, out_ref = rest
    total = row_ref[:ROWS, :] + other_ref[:ROWS, :]
    term = (total * scale_ref[...]).astype(BF16)
    out_ref[...] = jnp.dot(term, w_ref[layer], preferred_element_type=F32)


def array(*shape, dtype=F32):
    return jax.ShapeDtypeStruct(shape, dtype)


def call(kernel, name, out_shape, in_specs, scratch=(), cost=None):
    return pl.pallas_call(
        kernel,
        out_shape=out_shape,
        in_specs=in_specs,
        out_specs=[full()] * len(out_shape),
        scratch_shapes=list(scratch),
        compiler_params=SMALL,
        cost_estimate=cost,
        name=name,
    )


def from_partner(block, flip):
    route = [(i, i ^ flip) for i in range(lax.axis_size("point"))]
    return lax.ppermute(block, "point", route)


def doubled(block, flip):
    return block + from_partner(block, flip)


def shards(features, tiles, masks, w_self, w_col, w_row, bias):
    barrier = lax.optimization_barrier
    smem = full(pltpu.SMEM)
    me_view = lax.axis_index("view").astype(jnp.int32)
    even = (lax.axis_index("point") % 2) == 0
    n_point = lax.axis_size("point")
    pair_a = [(i, i ^ 1) for i in range(n_point)]
    pair_b = [(i, (i + 1) % n_point if i % 2 else (i - 1) % n_point) for i in range(n_point)]
    tiles_t = pltpu.with_memory_space_constraint(tiles.T, pltpu.HBM)
    slot_shape = (SLOTS, TV, TP, D)
    ret_shape = array(N_VIEW, DATA, D)

    def whole(*shape):
        return pl.BlockSpec(shape, lambda i, t: (0,) * len(shape))

    slot_spec = pl.BlockSpec((1, TV, TP, D), lambda i, t: (i, 0, 0, 0))
    mask_spec = pl.BlockSpec((1, TV, TP), lambda i, t: (i, 0, 0))

    def by_slot(kernel, name, out_shape, in_specs, out_specs):
        return pl.pallas_call(
            kernel,
            out_shape=out_shape,
            grid_spec=pltpu.PrefetchScalarGridSpec(
                num_scalar_prefetch=1, grid=(SLOTS,), in_specs=in_specs, out_specs=out_specs
            ),
            compiler_params=LARGE,
            name=name,
        )

    masks = pltpu.with_memory_space_constraint(masks, pltpu.HBM)
    features = pltpu.with_memory_space_constraint(features, pltpu.HBM)
    col_pay, row_sum = by_slot(
        first_sums,
        "first_sums",
        [array(N_VIEW, DATA + EXTRA, D), array(ROWS + 8, D)],
        [slot_spec, mask_spec],
        [whole(N_VIEW, DATA + EXTRA, D), whole(ROWS + 8, D)],
    )(tiles_t, features, masks)

    state = features
    place = col_scale = row_scale = None
    for layer in range(LAYERS):
        first = layer == 0
        last = layer == LAYERS - 1
        got = lax.all_to_all(col_pay, "view", 0, 0, tiled=True)
        (row_sum,) = call(
            add_rows, "add_rows", [array(*row_sum.shape)], [full()] * 2, cost=EARLY
        )(row_sum, from_partner(row_sum, 4))
        row_sum = doubled(row_sum, 1)
        got, row_sum = barrier((got, row_sum))
        if first:
            point_id = got[:, DATA : DATA + SLOTS, 0].astype(jnp.int32)
            place = jnp.where(even, point_id ^ PT_DEV, point_id)
        extra = EXTRA if first else 0
        part_a, part_b = call(
            functools.partial(owner_sums, first),
            "owner_sums",
            [array(DATA + extra, D), array(DATA + ROWS + 2 * extra, D)],
            [smem, full(), full()],
            [pltpu.VMEM((2 * DATA + extra, D), F32)] * SLOTS,
        )(place, got, row_sum)
        from_b = lax.ppermute(part_b, "point", pair_b)
        from_a = lax.ppermute(part_a, "point", pair_a)
        outs = call(
            functools.partial(owner_project, first, layer),
            "owner_project",
            [ret_shape, array(ROWS + extra, D)] + ([array(2 * DATA, D)] if first else []),
            [smem, smem] + [full()] * (6 if first else 7),
            [pltpu.VMEM((2 * DATA, D), F32)],
        )(
            place,
            me_view[None],
            part_a,
            part_b,
            from_a,
            from_b,
            w_col,
            bias,
            *(() if first else (col_scale,)),
        )
        row_sum = outs[1]
        row_other = from_partner(row_sum, 8)
        if first:
            col_scale = outs[2]
        back = lax.all_to_all(outs[0], "view", 0, 0, tiled=True)
        outs = call(
            functools.partial(view_project, first, layer),
            "view_project",
            [array(ROWS, D)] * (2 if first else 1),
            [full()] * (3 if first else 4),
            cost=EARLY,
        )(row_sum, row_other, *(() if first else (row_scale,)), w_row)
        row_proj = outs[0]
        if first:
            row_scale = outs[1]
        outs = by_slot(
            functools.partial(layer_body, layer, last),
            "layer_body",
            [array(*slot_shape, dtype=BF16)] + ([] if last else [ret_shape, array(ROWS, D)]),
            [
                slot_spec,
                mask_spec,
                whole(N_VIEW, DATA, D),
                whole(ROWS, D),
                whole(LAYERS, D, D),
            ],
            [slot_spec] + ([] if last else [whole(N_VIEW, DATA, D), whole(ROWS, D)]),
        )(tiles_t, state, masks, back, row_proj, w_self)
        if last:
            return outs[0]
        state, col_pay, row_sum = outs


def solution(mesh):
    in_specs = (
        P(("view", "point"), None, None, None),
        P(("view", "point"), None),
        P(("view", "point"), None, None),
        P(),
        P(),
        P(),
        P(),
    )
    out_specs = P(("view", "point"), None, None, None)
    return jax.shard_map(shards, mesh=mesh, in_specs=in_specs, out_specs=out_specs, check_vma=False)
```

```python
import functools

import jax
import jax.numpy as jnp
from jax import lax
from jax.experimental import pallas as pl
from jax.experimental.pallas import tpu as pltpu
from jax.sharding import PartitionSpec as P

VT_DEV = 4
PT_DEV = 4
LAYERS = 3
SLOTS = 4
TV = 32
TP = 128
D = 256
N_VIEW = 8
PER = TP // N_VIEW
DATA = SLOTS * PER
EXTRA = 8
ROWS = VT_DEV * TV
RC = 4
HALF = SLOTS // 2
EARLY = pl.CostEstimate(flops=40_000_000_000, transcendentals=0, bytes_accessed=100_000_000)
STATE = pl.CostEstimate(flops=1_100_000_000, transcendentals=0, bytes_accessed=12_000_000)
F32 = jnp.float32
BF16 = jnp.bfloat16
SMALL = pltpu.CompilerParams(vmem_limit_bytes=8 * 1024 * 1024)
LARGE = pltpu.CompilerParams(vmem_limit_bytes=48 * 1024 * 1024)


def full(memory_space=pltpu.VMEM):
    return pl.BlockSpec(memory_space=memory_space)


def spread(counts, first_lane, rows):
    lane = lax.broadcasted_iota(jnp.int32, (rows, TP), 1)
    line = lax.broadcasted_iota(jnp.int32, (rows, TP), 0) + first_lane
    picked = jnp.where(lane == line, jnp.broadcast_to(counts, (rows, TP)), 0.0)
    count = jnp.sum(picked, axis=1, keepdims=True)
    return jnp.broadcast_to(1.0 / jnp.sqrt(jnp.maximum(count, 1.0)), (rows, D))


def first_sums(tiles_ref, x_ref, m_ref, col_ref, row_ref):
    slot = pl.program_id(0)
    mask = m_ref[0].astype(F32)
    mask_t = mask.T
    col_count = jnp.sum(mask, axis=0, keepdims=True)
    row_count = jnp.sum(mask_t, axis=0, keepdims=True)
    padded = jnp.concatenate([col_count, jnp.zeros((1, D - TP), F32)], axis=1)
    padded_row = jnp.concatenate([row_count, jnp.zeros((1, D - TV), F32)], axis=1)
    point_id = jnp.full((1, D), tiles_ref[1, slot], jnp.int32).astype(F32)

    @pl.when(slot == 0)
    def _():
        row_ref[...] = jnp.zeros_like(row_ref)

    for s in range(SLOTS):

        @pl.when(slot == s)
        def _():
            for peer in range(N_VIEW):
                col_ref[peer, DATA + s : DATA + s + 1, :] = point_id
                col_ref[peer, DATA + SLOTS + s : DATA + SLOTS + s + 1, :] = padded

    for v in range(VT_DEV):
        hit = jnp.where(tiles_ref[0, slot] == v, 1.0, 0.0).astype(F32)
        row_ref[ROWS + v : ROWS + v + 1, :] += padded_row * hit
    acc = None
    totals = []
    for r in range(TV):
        val = x_ref[0, r].astype(F32) * mask_t[:, r : r + 1]
        acc = val if acc is None else acc + val
        totals.append(jnp.sum(val, axis=0, keepdims=True))
    store_sums(slot, tiles_ref, acc, totals, col_ref, row_ref)


def store_sums(slot, tiles_ref, acc, totals, col_ref, row_ref):
    here = pl.ds(pl.multiple_of(slot * PER, PER), PER)
    for peer in range(N_VIEW):
        col_ref[peer, here, :] = acc[peer * PER : (peer + 1) * PER]
    view_at = pl.multiple_of(tiles_ref[0, slot] * TV, TV)
    row_ref[pl.ds(view_at, TV), :] += jnp.concatenate(totals, axis=0)


def layer_sums(layer, tiles_ref, x_ref, m_ref, ret_ref, rowp_ref, w_ref, *outs):
    layer_body(layer, 0, tiles_ref, x_ref, m_ref, ret_ref, rowp_ref, w_ref, None, *outs)


def layer_state(layer, base, tiles_ref, x_ref, m_ref, ret_ref, rowp_ref, w_ref, *outs):
    layer_body(layer, base, tiles_ref, x_ref, m_ref, ret_ref, rowp_ref, w_ref, outs[-1])


def layer_body(layer, base, tiles_ref, x_ref, m_ref, ret_ref, rowp_ref, w_ref, out_ref, *sums):
    slot = pl.program_id(0) + base
    if sums:
        col_ref, row_ref = sums

        @pl.when(slot == 0)
        def _():
            row_ref[...] = jnp.zeros_like(row_ref)

    view_at = pl.multiple_of(tiles_ref[0, slot] * TV, TV)
    row_proj = rowp_ref[pl.ds(view_at, TV), :]
    weight = w_ref[layer]
    mask_t = m_ref[0].astype(F32).T
    here = pl.ds(pl.multiple_of(slot * PER, PER), PER)
    col_proj = ret_ref[:, here, :].reshape(TP, D)
    acc = None
    totals = []
    for r0 in range(0, TV, RC):
        block = x_ref[0, r0 : r0 + RC].reshape(RC * TP, D)
        prod = jnp.dot(block, weight, preferred_element_type=F32)
        for k in range(RC):
            r = r0 + k
            val = prod[k * TP : (k + 1) * TP] + col_proj + row_proj[r : r + 1, :]
            val = jnp.maximum(val, 0.0) * mask_t[:, r : r + 1]
            if out_ref is not None:
                out_ref[0, r] = val.astype(BF16)
            if sums:
                acc = val if acc is None else acc + val
                totals.append(jnp.sum(val, axis=0, keepdims=True))
    if sums:
        store_sums(slot, tiles_ref, acc, totals, col_ref, row_ref)


def owner_sums(first, at_ref, got_ref, row_ref, a_ref, b_ref, *sums):
    b_ref[a_ref.shape[0] :, :] = row_ref[...]
    for ref in sums:
        ref[...] = jnp.zeros_like(ref)
    for d in range(N_VIEW):
        for s in range(SLOTS):
            place = at_ref[d, s]
            rows = pl.ds(pl.multiple_of(place * PER, PER), PER)
            sums[s][rows, :] += got_ref[d, s * PER : (s + 1) * PER, :]
            if first:
                line = pl.ds(2 * DATA + place, 1)
                sums[s][line, :] += got_ref[d, DATA + SLOTS + s : DATA + SLOTS + s + 1, :]
    for n, ref in enumerate((a_ref, b_ref)):
        spots = [(0, slice(n * DATA, (n + 1) * DATA), DATA)]
        if first:
            start = 2 * DATA + n * PT_DEV
            spots.append((DATA, slice(start, start + PT_DEV), PT_DEV))
            ref[DATA + PT_DEV : DATA + EXTRA, :] = jnp.zeros((EXTRA - PT_DEV, D), F32)
        for to, rows, size in spots:
            ref[to : to + size, :] = (sums[0][rows, :] + sums[1][rows, :]) + (
                sums[2][rows, :] + sums[3][rows, :]
            )


def owner_project(first, layer, at_ref, me_ref, a_ref, b_ref, ra_ref, rb_ref, w_ref, bias_ref, *rest):
    if first:
        ret_ref, row_ref, scale_ref, proj_ref = rest
    else:
        scale_ref, ret_ref, row_ref, proj_ref = rest
    row_ref[...] = b_ref[a_ref.shape[0] :, :] + rb_ref[a_ref.shape[0] :, :]
    for n, (ref, rref) in enumerate(((a_ref, ra_ref), (b_ref, rb_ref))):
        if first:
            for j in range(PT_DEV):
                line = slice(DATA + j, DATA + j + 1)
                count = ref[line, :TP] + rref[line, :TP]
                at = n * DATA + j * PER
                scale_ref[at : at + PER, :] = spread(count, me_ref[0] * PER, PER)
        half = slice(n * DATA, (n + 1) * DATA)
        term = ((ref[:DATA, :] + rref[:DATA, :]) * scale_ref[half, :]).astype(BF16)
        proj = jnp.dot(term, w_ref[layer], preferred_element_type=F32)
        proj_ref[half, :] = proj + bias_ref[layer : layer + 1, :]
    for d in range(N_VIEW):
        for s in range(SLOTS):
            rows = pl.ds(pl.multiple_of(at_ref[d, s] * PER, PER), PER)
            ret_ref[d, s * PER : (s + 1) * PER, :] = proj_ref[rows, :]


def add_rows(mine_ref, other_ref, out_ref):
    out_ref[...] = mine_ref[...] + other_ref[...]


def view_project(first, layer, row_ref, other_ref, *rest):
    if first:
        w_ref, out_ref, scale_ref = rest
        for v in range(VT_DEV):
            line = slice(ROWS + v, ROWS + v + 1)
            count = row_ref[line, :TP] + other_ref[line, :TP]
            scale_ref[v * TV : (v + 1) * TV, :] = spread(count, 0, TV)
    else:
        scale_ref, w_ref, out_ref = rest
    total = row_ref[:ROWS, :] + other_ref[:ROWS, :]
    term = (total * scale_ref[...]).astype(BF16)
    out_ref[...] = jnp.dot(term, w_ref[layer], preferred_element_type=F32)


def array(*shape, dtype=F32):
    return jax.ShapeDtypeStruct(shape, dtype)


def call(kernel, name, out_shape, in_specs, scratch=(), cost=None):
    return pl.pallas_call(
        kernel,
        out_shape=out_shape,
        in_specs=in_specs,
        out_specs=[full()] * len(out_shape),
        scratch_shapes=list(scratch),
        compiler_params=SMALL,
        cost_estimate=cost,
        name=name,
    )


def from_partner(block, flip):
    route = [(i, i ^ flip) for i in range(lax.axis_size("point"))]
    return lax.ppermute(block, "point", route)


def doubled(block, flip):
    return block + from_partner(block, flip)


def shards(features, tiles, masks, w_self, w_col, w_row, bias):
    barrier = lax.optimization_barrier
    smem = full(pltpu.SMEM)
    me_view = lax.axis_index("view").astype(jnp.int32)
    even = (lax.axis_index("point") % 2) == 0
    n_point = lax.axis_size("point")
    pair_a = [(i, i ^ 1) for i in range(n_point)]
    pair_b = [(i, (i + 1) % n_point if i % 2 else (i - 1) % n_point) for i in range(n_point)]
    tiles_t = pltpu.with_memory_space_constraint(tiles.T, pltpu.HBM)
    slot_shape = (SLOTS, TV, TP, D)
    ret_shape = array(N_VIEW, DATA, D)

    def whole(*shape):
        return pl.BlockSpec(shape, lambda i, t: (0,) * len(shape))

    def slot_spec(base=0):
        return pl.BlockSpec((1, TV, TP, D), lambda i, t: (i + base, 0, 0, 0))

    def mask_spec(base=0):
        return pl.BlockSpec((1, TV, TP), lambda i, t: (i + base, 0, 0))

    def by_slot(kernel, name, out_shape, in_specs, out_specs, slots=SLOTS, **kwargs):
        return pl.pallas_call(
            kernel,
            out_shape=out_shape,
            grid_spec=pltpu.PrefetchScalarGridSpec(
                num_scalar_prefetch=1, grid=(slots,), in_specs=in_specs, out_specs=out_specs
            ),
            compiler_params=LARGE,
            name=name,
            **kwargs,
        )

    def layer_specs(base=0):
        return [
            slot_spec(base),
            mask_spec(base),
            whole(N_VIEW, DATA, D),
            whole(ROWS, D),
            whole(LAYERS, D, D),
        ]

    def half_state(which, old, partial):
        base = which * HALF
        tail = [] if partial is None else [partial]
        (out,) = by_slot(
            functools.partial(layer_state, layer - 1, base),
            "layer_state",
            [array(*slot_shape, dtype=BF16)],
            layer_specs(base) + [full(pltpu.HBM)] * len(tail),
            [slot_spec(base)],
            HALF,
            input_output_aliases={6: 0} if tail else {},
            cost_estimate=STATE,
        )(*old, *tail)
        return out

    masks = pltpu.with_memory_space_constraint(masks, pltpu.HBM)
    features = pltpu.with_memory_space_constraint(features, pltpu.HBM)
    col_pay, row_sum = by_slot(
        first_sums,
        "first_sums",
        [array(N_VIEW, DATA + EXTRA, D), array(ROWS + 8, D)],
        [slot_spec(), mask_spec()],
        [whole(N_VIEW, DATA + EXTRA, D), whole(ROWS + 8, D)],
    )(tiles_t, features, masks)

    state = features
    place = col_scale = row_scale = old = None
    for layer in range(LAYERS):
        first = layer == 0
        last = layer == LAYERS - 1
        got = lax.all_to_all(col_pay, "view", 0, 0, tiled=True)
        row_other = from_partner(row_sum, 4)
        if not first:
            row_other, back, row_proj = barrier((row_other, old[3], old[4]))
            old = old[:3] + (back, row_proj, w_self)
            state = half_state(0, old, None)
        (row_sum,) = call(
            add_rows, "add_rows", [array(*row_sum.shape)], [full()] * 2, cost=EARLY
        )(row_sum, row_other)
        row_sum = doubled(row_sum, 1)
        got, row_sum, state = barrier((got, row_sum, state))
        if first:
            point_id = got[:, DATA : DATA + SLOTS, 0].astype(jnp.int32)
            place = jnp.where(even, point_id ^ PT_DEV, point_id)
        extra = EXTRA if first else 0
        part_a, part_b = call(
            functools.partial(owner_sums, first),
            "owner_sums",
            [array(DATA + extra, D), array(DATA + ROWS + 2 * extra, D)],
            [smem, full(), full()],
            [pltpu.VMEM((2 * DATA + extra, D), F32)] * SLOTS,
        )(place, got, row_sum)
        from_b = lax.ppermute(part_b, "point", pair_b)
        from_a = lax.ppermute(part_a, "point", pair_a)
        outs = call(
            functools.partial(owner_project, first, layer),
            "owner_project",
            [ret_shape, array(ROWS + extra, D)] + ([array(2 * DATA, D)] if first else []),
            [smem, smem] + [full()] * (6 if first else 7),
            [pltpu.VMEM((2 * DATA, D), F32)],
        )(
            place,
            me_view[None],
            part_a,
            part_b,
            from_a,
            from_b,
            w_col,
            bias,
            *(() if first else (col_scale,)),
        )
        row_sum = outs[1]
        row_other = from_partner(row_sum, 8)
        if first:
            col_scale = outs[2]
        back = lax.all_to_all(outs[0], "view", 0, 0, tiled=True)
        if not first:
            row_other, state, late, proj = barrier((row_other, state, old[3], old[4]))
            state = half_state(1, old[:3] + (late, proj, w_self), state)
            back, state = barrier((back, state))
        outs = call(
            functools.partial(view_project, first, layer),
            "view_project",
            [array(ROWS, D)] * (2 if first else 1),
            [full()] * (3 if first else 4),
            cost=EARLY,
        )(row_sum, row_other, *(() if first else (row_scale,)), w_row)
        row_proj = outs[0]
        if first:
            row_scale = outs[1]
        old = (tiles_t, state, masks, back, row_proj, w_self)
        if last:
            (out,) = by_slot(
                functools.partial(layer_state, layer, 0),
                "layer_state",
                [array(*slot_shape, dtype=BF16)],
                layer_specs(),
                [slot_spec()],
            )(*old)
            return out
        col_pay, row_sum = by_slot(
            functools.partial(layer_sums, layer),
            "layer_sums",
            [ret_shape, array(ROWS, D)],
            layer_specs(),
            [whole(N_VIEW, DATA, D), whole(ROWS, D)],
        )(*old)


def solution(mesh):
    in_specs = (
        P(("view", "point"), None, None, None),
        P(("view", "point"), None),
        P(("view", "point"), None, None),
        P(),
        P(),
        P(),
        P(),
    )
    out_specs = P(("view", "point"), None, None, None)
    return jax.shard_map(shards, mesh=mesh, in_specs=in_specs, out_specs=out_specs, check_vma=False)
```

```python
import functools

import jax
import jax.numpy as jnp
from jax import lax
from jax.experimental import pallas as pl
from jax.experimental.pallas import tpu as pltpu
from jax.sharding import PartitionSpec as P

VT_DEV = 4
PT_DEV = 4
LAYERS = 3
SLOTS = 4
TV = 32
TP = 128
D = 256
N_VIEW = 8
PER = TP // N_VIEW
DATA = SLOTS * PER
EXTRA = 8
ROWS = VT_DEV * TV
RC = 4
HALF = SLOTS // 2
EARLY = pl.CostEstimate(flops=40_000_000_000, transcendentals=0, bytes_accessed=100_000_000)
STATE = pl.CostEstimate(flops=1_100_000_000, transcendentals=0, bytes_accessed=12_000_000)
F32 = jnp.float32
BF16 = jnp.bfloat16
SMALL = pltpu.CompilerParams(vmem_limit_bytes=8 * 1024 * 1024)
LARGE = pltpu.CompilerParams(vmem_limit_bytes=48 * 1024 * 1024)


def full(memory_space=pltpu.VMEM):
    return pl.BlockSpec(memory_space=memory_space)


def spread(counts, first_lane, rows):
    lane = lax.broadcasted_iota(jnp.int32, (rows, TP), 1)
    line = lax.broadcasted_iota(jnp.int32, (rows, TP), 0) + first_lane
    picked = jnp.where(lane == line, jnp.broadcast_to(counts, (rows, TP)), 0.0)
    count = jnp.sum(picked, axis=1, keepdims=True)
    return jnp.broadcast_to(1.0 / jnp.sqrt(jnp.maximum(count, 1.0)), (rows, D))


def first_sums(tiles_ref, x_ref, m_ref, col_ref, row_ref):
    slot = pl.program_id(0)
    mask = m_ref[0].astype(F32)
    mask_t = mask.T
    col_count = jnp.sum(mask, axis=0, keepdims=True)
    row_count = jnp.sum(mask_t, axis=0, keepdims=True)
    padded = jnp.concatenate([col_count, jnp.zeros((1, D - TP), F32)], axis=1)
    padded_row = jnp.concatenate([row_count, jnp.zeros((1, D - TV), F32)], axis=1)
    point_id = jnp.full((1, D), tiles_ref[1, slot], jnp.int32).astype(F32)

    @pl.when(slot == 0)
    def _():
        row_ref[...] = jnp.zeros_like(row_ref)

    for s in range(SLOTS):

        @pl.when(slot == s)
        def _():
            for peer in range(N_VIEW):
                col_ref[peer, DATA + s : DATA + s + 1, :] = point_id
                col_ref[peer, DATA + SLOTS + s : DATA + SLOTS + s + 1, :] = padded

    for v in range(VT_DEV):
        hit = jnp.where(tiles_ref[0, slot] == v, 1.0, 0.0).astype(F32)
        row_ref[ROWS + v : ROWS + v + 1, :] += padded_row * hit
    acc = None
    totals = []
    for r in range(TV):
        val = x_ref[0, r].astype(F32) * mask_t[:, r : r + 1]
        acc = val if acc is None else acc + val
        totals.append(jnp.sum(val, axis=0, keepdims=True))
    store_sums(slot, tiles_ref, acc, totals, col_ref, row_ref)


def store_sums(slot, tiles_ref, acc, totals, col_ref, row_ref):
    here = pl.ds(pl.multiple_of(slot * PER, PER), PER)
    for peer in range(N_VIEW):
        col_ref[peer, here, :] = acc[peer * PER : (peer + 1) * PER]
    view_at = pl.multiple_of(tiles_ref[0, slot] * TV, TV)
    row_ref[pl.ds(view_at, TV), :] += jnp.concatenate(totals, axis=0)


def layer_sums(layer, tiles_ref, x_ref, m_ref, ret_ref, rowp_ref, w_ref, *outs):
    layer_body(layer, 0, tiles_ref, x_ref, m_ref, ret_ref, rowp_ref, w_ref, None, *outs)


def layer_state(layer, base, tiles_ref, x_ref, m_ref, ret_ref, rowp_ref, w_ref, *outs):
    layer_body(layer, base, tiles_ref, x_ref, m_ref, ret_ref, rowp_ref, w_ref, outs[-1])


def layer_body(layer, base, tiles_ref, x_ref, m_ref, ret_ref, rowp_ref, w_ref, out_ref, *sums):
    slot = pl.program_id(0) + base
    if sums:
        col_ref, row_ref = sums

        @pl.when(slot == 0)
        def _():
            row_ref[...] = jnp.zeros_like(row_ref)

    view_at = pl.multiple_of(tiles_ref[0, slot] * TV, TV)
    row_proj = rowp_ref[pl.ds(view_at, TV), :]
    weight = w_ref[layer]
    mask_t = m_ref[0].astype(F32).T
    here = pl.ds(pl.multiple_of(slot * PER, PER), PER)
    col_proj = ret_ref[:, here, :].reshape(TP, D)
    acc = None
    totals = []
    for r0 in range(0, TV, RC):
        block = x_ref[0, r0 : r0 + RC].reshape(RC * TP, D)
        prod = jnp.dot(block, weight, preferred_element_type=F32)
        for k in range(RC):
            r = r0 + k
            val = prod[k * TP : (k + 1) * TP] + col_proj + row_proj[r : r + 1, :]
            val = jnp.maximum(val, 0.0) * mask_t[:, r : r + 1]
            if out_ref is not None:
                out_ref[0, r] = val.astype(BF16)
            if sums:
                acc = val if acc is None else acc + val
                totals.append(jnp.sum(val, axis=0, keepdims=True))
    if sums:
        store_sums(slot, tiles_ref, acc, totals, col_ref, row_ref)


def owner_sums(first, at_ref, got_ref, row_ref, a_ref, b_ref, *sums):
    b_ref[a_ref.shape[0] :, :] = row_ref[...]
    for ref in sums:
        ref[...] = jnp.zeros_like(ref)
    for d in range(N_VIEW):
        for s in range(SLOTS):
            place = at_ref[d, s]
            rows = pl.ds(pl.multiple_of(place * PER, PER), PER)
            sums[s][rows, :] += got_ref[d, s * PER : (s + 1) * PER, :]
            if first:
                line = pl.ds(2 * DATA + place, 1)
                sums[s][line, :] += got_ref[d, DATA + SLOTS + s : DATA + SLOTS + s + 1, :]
    for n, ref in enumerate((a_ref, b_ref)):
        spots = [(0, slice(n * DATA, (n + 1) * DATA), DATA)]
        if first:
            start = 2 * DATA + n * PT_DEV
            spots.append((DATA, slice(start, start + PT_DEV), PT_DEV))
            ref[DATA + PT_DEV : DATA + EXTRA, :] = jnp.zeros((EXTRA - PT_DEV, D), F32)
        for to, rows, size in spots:
            ref[to : to + size, :] = (sums[0][rows, :] + sums[1][rows, :]) + (
                sums[2][rows, :] + sums[3][rows, :]
            )


def owner_project(first, layer, at_ref, me_ref, a_ref, b_ref, ra_ref, rb_ref, w_ref, bias_ref, *rest):
    if first:
        ret_ref, row_ref, scale_ref, proj_ref = rest
    else:
        scale_ref, ret_ref, row_ref, proj_ref = rest
    row_ref[...] = b_ref[a_ref.shape[0] :, :] + rb_ref[a_ref.shape[0] :, :]
    for n, (ref, rref) in enumerate(((a_ref, ra_ref), (b_ref, rb_ref))):
        if first:
            for j in range(PT_DEV):
                line = slice(DATA + j, DATA + j + 1)
                count = ref[line, :TP] + rref[line, :TP]
                at = n * DATA + j * PER
                scale_ref[at : at + PER, :] = spread(count, me_ref[0] * PER, PER)
        half = slice(n * DATA, (n + 1) * DATA)
        term = ((ref[:DATA, :] + rref[:DATA, :]) * scale_ref[half, :]).astype(BF16)
        proj = jnp.dot(term, w_ref[layer], preferred_element_type=F32)
        proj_ref[half, :] = proj + bias_ref[layer : layer + 1, :]
    for d in range(N_VIEW):
        for s in range(SLOTS):
            rows = pl.ds(pl.multiple_of(at_ref[d, s] * PER, PER), PER)
            ret_ref[d, s * PER : (s + 1) * PER, :] = proj_ref[rows, :]


def add_rows(mine_ref, other_ref, out_ref):
    out_ref[...] = mine_ref[...] + other_ref[...]


def view_project(first, layer, row_ref, other_ref, *rest):
    if first:
        w_ref, out_ref, scale_ref = rest
        for v in range(VT_DEV):
            line = slice(ROWS + v, ROWS + v + 1)
            count = row_ref[line, :TP] + other_ref[line, :TP]
            scale_ref[v * TV : (v + 1) * TV, :] = spread(count, 0, TV)
    else:
        scale_ref, w_ref, out_ref = rest
    total = row_ref[:ROWS, :] + other_ref[:ROWS, :]
    term = (total * scale_ref[...]).astype(BF16)
    out_ref[...] = jnp.dot(term, w_ref[layer], preferred_element_type=F32)


def array(*shape, dtype=F32):
    return jax.ShapeDtypeStruct(shape, dtype)


def call(kernel, name, out_shape, in_specs, scratch=(), cost=None):
    return pl.pallas_call(
        kernel,
        out_shape=out_shape,
        in_specs=in_specs,
        out_specs=[full()] * len(out_shape),
        scratch_shapes=list(scratch),
        compiler_params=SMALL,
        cost_estimate=cost,
        name=name,
    )


def from_partner(block, flip):
    route = [(i, i ^ flip) for i in range(lax.axis_size("point"))]
    return lax.ppermute(block, "point", route)


def doubled(block, flip):
    return block + from_partner(block, flip)


def shards(features, tiles, masks, w_self, w_col, w_row, bias):
    barrier = lax.optimization_barrier
    smem = full(pltpu.SMEM)
    me_view = lax.axis_index("view").astype(jnp.int32)
    even = (lax.axis_index("point") % 2) == 0
    n_point = lax.axis_size("point")
    pair_a = [(i, i ^ 1) for i in range(n_point)]
    pair_b = [(i, (i + 1) % n_point if i % 2 else (i - 1) % n_point) for i in range(n_point)]
    tiles_t = pltpu.with_memory_space_constraint(tiles.T, pltpu.HBM)
    slot_shape = (SLOTS, TV, TP, D)
    ret_shape = array(N_VIEW, DATA, D)

    def whole(*shape):
        return pl.BlockSpec(shape, lambda i, t: (0,) * len(shape))

    def slot_spec(base=0):
        return pl.BlockSpec((1, TV, TP, D), lambda i, t: (i + base, 0, 0, 0))

    def mask_spec(base=0):
        return pl.BlockSpec((1, TV, TP), lambda i, t: (i + base, 0, 0))

    def by_slot(kernel, name, out_shape, in_specs, out_specs, slots=SLOTS, **kwargs):
        return pl.pallas_call(
            kernel,
            out_shape=out_shape,
            grid_spec=pltpu.PrefetchScalarGridSpec(
                num_scalar_prefetch=1, grid=(slots,), in_specs=in_specs, out_specs=out_specs
            ),
            compiler_params=LARGE,
            name=name,
            **kwargs,
        )

    def layer_specs(base=0):
        return [
            slot_spec(base),
            mask_spec(base),
            whole(N_VIEW, DATA, D),
            whole(ROWS, D),
            whole(LAYERS, D, D),
        ]

    def half_state(which, old, partial):
        base = which * HALF
        tail = [] if partial is None else [partial]
        (out,) = by_slot(
            functools.partial(layer_state, layer - 1, base),
            "layer_state",
            [array(*slot_shape, dtype=BF16)],
            layer_specs(base) + [full(pltpu.HBM)] * len(tail),
            [slot_spec(base)],
            HALF,
            input_output_aliases={6: 0} if tail else {},
            cost_estimate=STATE,
        )(*old, *tail)
        return out

    masks = pltpu.with_memory_space_constraint(masks, pltpu.HBM)
    features = pltpu.with_memory_space_constraint(features, pltpu.HBM)
    col_pay, row_sum = by_slot(
        first_sums,
        "first_sums",
        [array(N_VIEW, DATA + EXTRA, D), array(ROWS + 8, D)],
        [slot_spec(), mask_spec()],
        [whole(N_VIEW, DATA + EXTRA, D), whole(ROWS + 8, D)],
    )(tiles_t, features, masks)

    state = features
    place = col_scale = row_scale = old = None
    for layer in range(LAYERS):
        first = layer == 0
        last = layer == LAYERS - 1
        got = lax.all_to_all(col_pay, "view", 0, 0, tiled=True)
        row_other = from_partner(row_sum, 4)
        if not first:
            row_other, back, row_proj = barrier((row_other, old[3], old[4]))
            old = old[:3] + (back, row_proj, w_self)
            state = half_state(0, old, None)
        (row_sum,) = call(
            add_rows, "add_rows", [array(*row_sum.shape)], [full()] * 2, cost=EARLY
        )(row_sum, row_other)
        row_sum, state = barrier((row_sum, state))
        row_sum = doubled(row_sum, 1)
        got, row_sum = barrier((got, row_sum))
        if first:
            point_id = got[:, DATA : DATA + SLOTS, 0].astype(jnp.int32)
            place = jnp.where(even, point_id ^ PT_DEV, point_id)
        extra = EXTRA if first else 0
        part_a, part_b = call(
            functools.partial(owner_sums, first),
            "owner_sums",
            [array(DATA + extra, D), array(DATA + ROWS + 2 * extra, D)],
            [smem, full(), full()],
            [pltpu.VMEM((2 * DATA + extra, D), F32)] * SLOTS,
        )(place, got, row_sum)
        from_b = lax.ppermute(part_b, "point", pair_b)
        from_a = lax.ppermute(part_a, "point", pair_a)
        outs = call(
            functools.partial(owner_project, first, layer),
            "owner_project",
            [ret_shape, array(ROWS + extra, D)] + ([array(2 * DATA, D)] if first else []),
            [smem, smem] + [full()] * (6 if first else 7),
            [pltpu.VMEM((2 * DATA, D), F32)],
        )(
            place,
            me_view[None],
            part_a,
            part_b,
            from_a,
            from_b,
            w_col,
            bias,
            *(() if first else (col_scale,)),
        )
        row_sum = outs[1]
        row_other = from_partner(row_sum, 8)
        if first:
            col_scale = outs[2]
        back = lax.all_to_all(outs[0], "view", 0, 0, tiled=True)
        if not first:
            row_other, state, late, proj = barrier((row_other, state, old[3], old[4]))
            state = half_state(1, old[:3] + (late, proj, w_self), state)
            back, state = barrier((back, state))
        outs = call(
            functools.partial(view_project, first, layer),
            "view_project",
            [array(ROWS, D)] * (2 if first else 1),
            [full()] * (3 if first else 4),
            cost=EARLY,
        )(row_sum, row_other, *(() if first else (row_scale,)), w_row)
        row_proj = outs[0]
        if first:
            row_scale = outs[1]
        old = (tiles_t, state, masks, back, row_proj, w_self)
        if last:
            (out,) = by_slot(
                functools.partial(layer_state, layer, 0),
                "layer_state",
                [array(*slot_shape, dtype=BF16)],
                layer_specs(),
                [slot_spec()],
            )(*old)
            return out
        col_pay, row_sum = by_slot(
            functools.partial(layer_sums, layer),
            "layer_sums",
            [ret_shape, array(ROWS, D)],
            layer_specs(),
            [whole(N_VIEW, DATA, D), whole(ROWS, D)],
        )(*old)


def solution(mesh):
    in_specs = (
        P(("view", "point"), None, None, None),
        P(("view", "point"), None),
        P(("view", "point"), None, None),
        P(),
        P(),
        P(),
        P(),
    )
    out_specs = P(("view", "point"), None, None, None)
    return jax.shard_map(shards, mesh=mesh, in_specs=in_specs, out_specs=out_specs, check_vma=False)
```

```python
import functools

import jax
import jax.numpy as jnp
from jax import lax
from jax.experimental import pallas as pl
from jax.experimental.pallas import tpu as pltpu
from jax.sharding import PartitionSpec as P

VT_DEV = 4
PT_DEV = 4
LAYERS = 3
SLOTS = 4
TV = 32
TP = 128
D = 256
N_VIEW = 8
PER = TP // N_VIEW
DATA = SLOTS * PER
EXTRA = 8
ROWS = VT_DEV * TV
RC = 4
EARLY = pl.CostEstimate(flops=40_000_000_000, transcendentals=0, bytes_accessed=100_000_000)
STATE = pl.CostEstimate(flops=1_100_000_000, transcendentals=0, bytes_accessed=12_000_000)
F32 = jnp.float32
BF16 = jnp.bfloat16
SMALL = pltpu.CompilerParams(vmem_limit_bytes=8 * 1024 * 1024)
LARGE = pltpu.CompilerParams(vmem_limit_bytes=48 * 1024 * 1024)


def full(memory_space=pltpu.VMEM):
    return pl.BlockSpec(memory_space=memory_space)


def spread(counts, first_lane, rows):
    lane = lax.broadcasted_iota(jnp.int32, (rows, TP), 1)
    line = lax.broadcasted_iota(jnp.int32, (rows, TP), 0) + first_lane
    picked = jnp.where(lane == line, jnp.broadcast_to(counts, (rows, TP)), 0.0)
    count = jnp.sum(picked, axis=1, keepdims=True)
    return jnp.broadcast_to(1.0 / jnp.sqrt(jnp.maximum(count, 1.0)), (rows, D))


def first_sums(tiles_ref, x_ref, m_ref, col_ref, row_ref):
    slot = pl.program_id(0)
    mask = m_ref[0].astype(F32)
    mask_t = mask.T
    col_count = jnp.sum(mask, axis=0, keepdims=True)
    row_count = jnp.sum(mask_t, axis=0, keepdims=True)
    padded = jnp.concatenate([col_count, jnp.zeros((1, D - TP), F32)], axis=1)
    padded_row = jnp.concatenate([row_count, jnp.zeros((1, D - TV), F32)], axis=1)
    point_id = jnp.full((1, D), tiles_ref[1, slot], jnp.int32).astype(F32)

    @pl.when(slot == 0)
    def _():
        row_ref[...] = jnp.zeros_like(row_ref)

    for s in range(SLOTS):

        @pl.when(slot == s)
        def _():
            for peer in range(N_VIEW):
                col_ref[peer, DATA + s : DATA + s + 1, :] = point_id
                col_ref[peer, DATA + SLOTS + s : DATA + SLOTS + s + 1, :] = padded

    for v in range(VT_DEV):
        hit = jnp.where(tiles_ref[0, slot] == v, 1.0, 0.0).astype(F32)
        row_ref[ROWS + v : ROWS + v + 1, :] += padded_row * hit
    acc = None
    totals = []
    for r in range(TV):
        val = x_ref[0, r].astype(F32) * mask_t[:, r : r + 1]
        acc = val if acc is None else acc + val
        totals.append(jnp.sum(val, axis=0, keepdims=True))
    store_sums(slot, tiles_ref, acc, totals, col_ref, row_ref)


def store_sums(slot, tiles_ref, acc, totals, col_ref, row_ref):
    here = pl.ds(pl.multiple_of(slot * PER, PER), PER)
    for peer in range(N_VIEW):
        col_ref[peer, here, :] = acc[peer * PER : (peer + 1) * PER]
    view_at = pl.multiple_of(tiles_ref[0, slot] * TV, TV)
    row_ref[pl.ds(view_at, TV), :] += jnp.concatenate(totals, axis=0)


def relu_mixed(x_ref, mask_t, weight, col_proj, row_proj, r0):
    block = x_ref[0, r0 : r0 + RC].reshape(RC * TP, D)
    prod = jnp.dot(block, weight, preferred_element_type=F32)
    for k in range(RC):
        r = r0 + k
        val = prod[k * TP : (k + 1) * TP] + col_proj + row_proj[r : r + 1, :]
        yield r, jnp.maximum(val, 0.0) * mask_t[:, r : r + 1]


def layer_sums(layer, tiles_ref, x_ref, m_ref, ret_ref, rowp_ref, w_ref, col_ref, row_ref):
    slot = pl.program_id(0)

    @pl.when(slot == 0)
    def _():
        row_ref[...] = jnp.zeros_like(row_ref)

    view_at = pl.multiple_of(tiles_ref[0, slot] * TV, TV)
    row_proj = rowp_ref[pl.ds(view_at, TV), :]
    mask_t = m_ref[0].astype(F32).T
    col_proj = ret_ref[:, pl.ds(pl.multiple_of(slot * PER, PER), PER), :].reshape(TP, D)
    acc = None
    totals = []
    for r0 in range(0, TV, RC):
        for _, val in relu_mixed(x_ref, mask_t, w_ref[layer], col_proj, row_proj, r0):
            acc = val if acc is None else acc + val
            totals.append(jnp.sum(val, axis=0, keepdims=True))
    store_sums(slot, tiles_ref, acc, totals, col_ref, row_ref)


def layer_state(layer, base, tiles_ref, x_ref, m_ref, ret_ref, rowp_ref, w_ref, *outs):
    slot = pl.program_id(0) + base
    count = x_ref.shape[1]
    start = pl.multiple_of(pl.program_id(1) * count, count)
    view_at = pl.multiple_of(tiles_ref[0, slot] * TV + start, count)
    row_proj = rowp_ref[pl.ds(view_at, count), :]
    mask_t = m_ref[0, pl.ds(start, count), :].astype(F32).T
    col_proj = ret_ref[:, pl.ds(pl.multiple_of(slot * PER, PER), PER), :].reshape(TP, D)
    for r0 in range(0, count, RC):
        for r, val in relu_mixed(x_ref, mask_t, w_ref[layer], col_proj, row_proj, r0):
            outs[-1][0, r] = val.astype(BF16)


def owner_sums(first, at_ref, got_ref, row_ref, a_ref, b_ref, *sums):
    b_ref[a_ref.shape[0] :, :] = row_ref[...]
    for ref in sums:
        ref[...] = jnp.zeros_like(ref)
    for d in range(N_VIEW):
        for s in range(SLOTS):
            place = at_ref[d, s]
            rows = pl.ds(pl.multiple_of(place * PER, PER), PER)
            sums[s][rows, :] += got_ref[d, s * PER : (s + 1) * PER, :]
            if first:
                line = pl.ds(2 * DATA + place, 1)
                sums[s][line, :] += got_ref[d, DATA + SLOTS + s : DATA + SLOTS + s + 1, :]
    for n, ref in enumerate((a_ref, b_ref)):
        spots = [(0, slice(n * DATA, (n + 1) * DATA), DATA)]
        if first:
            start = 2 * DATA + n * PT_DEV
            spots.append((DATA, slice(start, start + PT_DEV), PT_DEV))
            ref[DATA + PT_DEV : DATA + EXTRA, :] = jnp.zeros((EXTRA - PT_DEV, D), F32)
        for to, rows, size in spots:
            ref[to : to + size, :] = (sums[0][rows, :] + sums[1][rows, :]) + (
                sums[2][rows, :] + sums[3][rows, :]
            )


def owner_project(first, layer, at_ref, me_ref, a_ref, b_ref, ra_ref, rb_ref, w_ref, bias_ref, *rest):
    if first:
        ret_ref, row_ref, scale_ref, proj_ref = rest
    else:
        scale_ref, ret_ref, row_ref, proj_ref = rest
    row_ref[...] = b_ref[a_ref.shape[0] :, :] + rb_ref[a_ref.shape[0] :, :]
    for n, (ref, rref) in enumerate(((a_ref, ra_ref), (b_ref, rb_ref))):
        if first:
            for j in range(PT_DEV):
                line = slice(DATA + j, DATA + j + 1)
                count = ref[line, :TP] + rref[line, :TP]
                at = n * DATA + j * PER
                scale_ref[at : at + PER, :] = spread(count, me_ref[0] * PER, PER)
        half = slice(n * DATA, (n + 1) * DATA)
        term = ((ref[:DATA, :] + rref[:DATA, :]) * scale_ref[half, :]).astype(BF16)
        proj = jnp.dot(term, w_ref[layer], preferred_element_type=F32)
        proj_ref[half, :] = proj + bias_ref[layer : layer + 1, :]
    for d in range(N_VIEW):
        for s in range(SLOTS):
            rows = pl.ds(pl.multiple_of(at_ref[d, s] * PER, PER), PER)
            ret_ref[d, s * PER : (s + 1) * PER, :] = proj_ref[rows, :]


def add_rows(mine_ref, other_ref, out_ref):
    out_ref[...] = mine_ref[...] + other_ref[...]


def view_project(first, layer, row_ref, other_ref, *rest):
    if first:
        w_ref, out_ref, scale_ref = rest
        for v in range(VT_DEV):
            line = slice(ROWS + v, ROWS + v + 1)
            count = row_ref[line, :TP] + other_ref[line, :TP]
            scale_ref[v * TV : (v + 1) * TV, :] = spread(count, 0, TV)
    else:
        scale_ref, w_ref, out_ref = rest
    total = row_ref[:ROWS, :] + other_ref[:ROWS, :]
    term = (total * scale_ref[...]).astype(BF16)
    out_ref[...] = jnp.dot(term, w_ref[layer], preferred_element_type=F32)


def array(*shape, dtype=F32):
    return jax.ShapeDtypeStruct(shape, dtype)


def call(kernel, name, out_shape, in_specs, scratch=(), cost=None):
    return pl.pallas_call(
        kernel,
        out_shape=out_shape,
        in_specs=in_specs,
        out_specs=[full()] * len(out_shape),
        scratch_shapes=list(scratch),
        compiler_params=SMALL,
        cost_estimate=cost,
        name=name,
    )


def from_partner(block, flip):
    route = [(i, i ^ flip) for i in range(lax.axis_size("point"))]
    return lax.ppermute(block, "point", route)


def doubled(block, flip):
    return block + from_partner(block, flip)


def shards(features, tiles, masks, w_self, w_col, w_row, bias):
    barrier = lax.optimization_barrier
    smem = full(pltpu.SMEM)
    me_view = lax.axis_index("view").astype(jnp.int32)
    even = (lax.axis_index("point") % 2) == 0
    n_point = lax.axis_size("point")
    pair_a = [(i, i ^ 1) for i in range(n_point)]
    pair_b = [(i, (i + 1) % n_point if i % 2 else (i - 1) % n_point) for i in range(n_point)]
    tiles_t = pltpu.with_memory_space_constraint(tiles.T, pltpu.HBM)
    slot_shape = (SLOTS, TV, TP, D)
    ret_shape = array(N_VIEW, DATA, D)

    def whole(*shape):
        return pl.BlockSpec(shape, lambda i, j, t: (0,) * len(shape))

    def slot_spec(base=0, views=TV):
        return pl.BlockSpec((1, views, TP, D), lambda i, j, t: (i + base, j, 0, 0))

    def mask_spec(base=0):
        return pl.BlockSpec((1, TV, TP), lambda i, j, t: (i + base, 0, 0))

    def by_slot(kernel, name, out_shape, in_specs, out_specs, grid=(SLOTS, 1), **kwargs):
        return pl.pallas_call(
            kernel,
            out_shape=out_shape,
            grid_spec=pltpu.PrefetchScalarGridSpec(
                num_scalar_prefetch=1, grid=grid, in_specs=in_specs, out_specs=out_specs
            ),
            compiler_params=LARGE,
            name=name,
            **kwargs,
        )

    def layer_specs(base=0, views=TV):
        return [
            slot_spec(base, views),
            mask_spec(base),
            whole(N_VIEW, DATA, D),
            whole(ROWS, D),
            whole(LAYERS, D, D),
        ]

    def some_state(layer, base, slots, views, old, partial=None):
        tail = [] if partial is None else [partial]
        (out,) = by_slot(
            functools.partial(layer_state, layer, base),
            "layer_state",
            [array(*slot_shape, dtype=BF16)],
            layer_specs(base, views) + [full(pltpu.HBM)] * len(tail),
            [slot_spec(base, views)],
            (slots, TV // views),
            input_output_aliases={6: 0} if tail else {},
            cost_estimate=STATE,
        )(*old, *tail)
        return out

    def after(old, value):
        value, back, row_proj = barrier((value, old[3], old[4]))
        return old[:3] + (back, row_proj, old[5]), value

    masks = pltpu.with_memory_space_constraint(masks, pltpu.HBM)
    features = pltpu.with_memory_space_constraint(features, pltpu.HBM)
    col_pay, row_sum = by_slot(
        first_sums,
        "first_sums",
        [array(N_VIEW, DATA + EXTRA, D), array(ROWS + 8, D)],
        [slot_spec(), mask_spec()],
        [whole(N_VIEW, DATA + EXTRA, D), whole(ROWS + 8, D)],
    )(tiles_t, features, masks)

    state = features
    place = col_scale = row_scale = old = None
    for layer in range(LAYERS):
        first = layer == 0
        last = layer == LAYERS - 1
        got = lax.all_to_all(col_pay, "view", 0, 0, tiled=True)
        row_other = from_partner(row_sum, 4)
        if not first:
            old, row_other = after(old, row_other)
            state = some_state(layer - 1, 0, 1, TV // 2, old)
        (row_sum,) = call(
            add_rows, "add_rows", [array(*row_sum.shape)], [full()] * 2, cost=EARLY
        )(row_sum, row_other)
        row_sum = doubled(row_sum, 1)
        got, row_sum, state = barrier((got, row_sum, state))
        if first:
            point_id = got[:, DATA : DATA + SLOTS, 0].astype(jnp.int32)
            place = jnp.where(even, point_id ^ PT_DEV, point_id)
        extra = EXTRA if first else 0
        part_a, part_b = call(
            functools.partial(owner_sums, first),
            "owner_sums",
            [array(DATA + extra, D), array(DATA + ROWS + 2 * extra, D)],
            [smem, full(), full()],
            [pltpu.VMEM((2 * DATA + extra, D), F32)] * SLOTS,
        )(place, got, row_sum)
        from_b = lax.ppermute(part_b, "point", pair_b)
        from_a = lax.ppermute(part_a, "point", pair_a)
        if not first:
            old, from_a = after(old, from_a)
            state = some_state(layer - 1, 1, 1, TV // 2, old, state)
            from_b, state = barrier((from_b, state))
        outs = call(
            functools.partial(owner_project, first, layer),
            "owner_project",
            [ret_shape, array(ROWS + extra, D)] + ([array(2 * DATA, D)] if first else []),
            [smem, smem] + [full()] * (6 if first else 7),
            [pltpu.VMEM((2 * DATA, D), F32)],
        )(
            place,
            me_view[None],
            part_a,
            part_b,
            from_a,
            from_b,
            w_col,
            bias,
            *(() if first else (col_scale,)),
        )
        row_sum = outs[1]
        row_other = from_partner(row_sum, 8)
        if first:
            col_scale = outs[2]
        back = lax.all_to_all(outs[0], "view", 0, 0, tiled=True)
        if not first:
            old, row_other = after(old, row_other)
            state = some_state(layer - 1, 2, 2, TV // 2, old, state)
            back, state = barrier((back, state))
        outs = call(
            functools.partial(view_project, first, layer),
            "view_project",
            [array(ROWS, D)] * (2 if first else 1),
            [full()] * (3 if first else 4),
            cost=EARLY,
        )(row_sum, row_other, *(() if first else (row_scale,)), w_row)
        row_proj = outs[0]
        if first:
            row_scale = outs[1]
        old = (tiles_t, state, masks, back, row_proj, w_self)
        if last:
            return some_state(layer, 0, SLOTS, TV, old)
        col_pay, row_sum = by_slot(
            functools.partial(layer_sums, layer),
            "layer_sums",
            [ret_shape, array(ROWS, D)],
            layer_specs(),
            [whole(N_VIEW, DATA, D), whole(ROWS, D)],
        )(*old)


def solution(mesh):
    in_specs = (
        P(("view", "point"), None, None, None),
        P(("view", "point"), None),
        P(("view", "point"), None, None),
        P(),
        P(),
        P(),
        P(),
    )
    out_specs = P(("view", "point"), None, None, None)
    return jax.shard_map(shards, mesh=mesh, in_specs=in_specs, out_specs=out_specs, check_vma=False)
```

```python
import functools

import jax
import jax.numpy as jnp
from jax import lax
from jax.experimental import pallas as pl
from jax.experimental.pallas import tpu as pltpu
from jax.sharding import PartitionSpec as P

VT_DEV = 4
PT_DEV = 4
LAYERS = 3
SLOTS = 4
TV = 32
TP = 128
D = 256
N_VIEW = 8
PER = TP // N_VIEW
DATA = SLOTS * PER
EXTRA = 8
ROWS = VT_DEV * TV
RC = 4
EARLY = pl.CostEstimate(flops=40_000_000_000, transcendentals=0, bytes_accessed=100_000_000)
STATE = pl.CostEstimate(flops=1_100_000_000, transcendentals=0, bytes_accessed=12_000_000)
F32 = jnp.float32
BF16 = jnp.bfloat16
SMALL = pltpu.CompilerParams(vmem_limit_bytes=8 * 1024 * 1024)
LARGE = pltpu.CompilerParams(vmem_limit_bytes=48 * 1024 * 1024)


def full(memory_space=pltpu.VMEM):
    return pl.BlockSpec(memory_space=memory_space)


def spread(counts, first_lane, rows):
    lane = lax.broadcasted_iota(jnp.int32, (rows, TP), 1)
    line = lax.broadcasted_iota(jnp.int32, (rows, TP), 0) + first_lane
    picked = jnp.where(lane == line, jnp.broadcast_to(counts, (rows, TP)), 0.0)
    count = jnp.sum(picked, axis=1, keepdims=True)
    return jnp.broadcast_to(1.0 / jnp.sqrt(jnp.maximum(count, 1.0)), (rows, D))


def first_sums(tiles_ref, x_ref, m_ref, col_ref, row_ref):
    slot = pl.program_id(0)
    mask = m_ref[0].astype(F32)
    mask_t = mask.T
    col_count = jnp.sum(mask, axis=0, keepdims=True)
    row_count = jnp.sum(mask_t, axis=0, keepdims=True)
    padded = jnp.concatenate([col_count, jnp.zeros((1, D - TP), F32)], axis=1)
    padded_row = jnp.concatenate([row_count, jnp.zeros((1, D - TV), F32)], axis=1)
    point_id = jnp.full((1, D), tiles_ref[1, slot], jnp.int32).astype(F32)

    @pl.when(slot == 0)
    def _():
        row_ref[...] = jnp.zeros_like(row_ref)

    for s in range(SLOTS):

        @pl.when(slot == s)
        def _():
            for peer in range(N_VIEW):
                col_ref[peer, DATA + s : DATA + s + 1, :] = point_id
                col_ref[peer, DATA + SLOTS + s : DATA + SLOTS + s + 1, :] = padded

    for v in range(VT_DEV):
        hit = jnp.where(tiles_ref[0, slot] == v, 1.0, 0.0).astype(F32)
        row_ref[ROWS + v : ROWS + v + 1, :] += padded_row * hit
    acc = None
    totals = []
    for r in range(TV):
        val = x_ref[0, r].astype(F32) * mask_t[:, r : r + 1]
        acc = val if acc is None else acc + val
        totals.append(jnp.sum(val, axis=0, keepdims=True))
    store_sums(slot, tiles_ref, acc, totals, col_ref, row_ref)


def store_sums(slot, tiles_ref, acc, totals, col_ref, row_ref):
    here = pl.ds(pl.multiple_of(slot * PER, PER), PER)
    for peer in range(N_VIEW):
        col_ref[peer, here, :] = acc[peer * PER : (peer + 1) * PER]
    view_at = pl.multiple_of(tiles_ref[0, slot] * TV, TV)
    row_ref[pl.ds(view_at, TV), :] += jnp.concatenate(totals, axis=0)


def relu_mixed(x_ref, mask_t, weight, col_proj, row_proj, r0):
    block = x_ref[0, r0 : r0 + RC].reshape(RC * TP, D)
    prod = jnp.dot(block, weight, preferred_element_type=F32)
    for k in range(RC):
        r = r0 + k
        val = prod[k * TP : (k + 1) * TP] + col_proj + row_proj[r : r + 1, :]
        yield r, jnp.maximum(val, 0.0) * mask_t[:, r : r + 1]


def layer_sums(layer, tiles_ref, x_ref, m_ref, ret_ref, rowp_ref, w_ref, col_ref, row_ref):
    slot = pl.program_id(0)

    @pl.when(slot == 0)
    def _():
        row_ref[...] = jnp.zeros_like(row_ref)

    view_at = pl.multiple_of(tiles_ref[0, slot] * TV, TV)
    row_proj = rowp_ref[pl.ds(view_at, TV), :]
    mask_t = m_ref[0].astype(F32).T
    col_proj = ret_ref[:, pl.ds(pl.multiple_of(slot * PER, PER), PER), :].reshape(TP, D)
    acc = None
    totals = []
    for r0 in range(0, TV, RC):
        for _, val in relu_mixed(x_ref, mask_t, w_ref[layer], col_proj, row_proj, r0):
            acc = val if acc is None else acc + val
            totals.append(jnp.sum(val, axis=0, keepdims=True))
    store_sums(slot, tiles_ref, acc, totals, col_ref, row_ref)


def layer_state(layer, base, tiles_ref, x_ref, m_ref, ret_ref, rowp_ref, w_ref, *outs):
    slot = pl.program_id(0) + base
    count = x_ref.shape[1]
    start = pl.multiple_of(pl.program_id(1) * count, count)
    view_at = pl.multiple_of(tiles_ref[0, slot] * TV + start, count)
    row_proj = rowp_ref[pl.ds(view_at, count), :]
    mask_t = m_ref[0, pl.ds(start, count), :].astype(F32).T
    col_proj = ret_ref[:, pl.ds(pl.multiple_of(slot * PER, PER), PER), :].reshape(TP, D)
    for r0 in range(0, count, RC):
        for r, val in relu_mixed(x_ref, mask_t, w_ref[layer], col_proj, row_proj, r0):
            outs[-1][0, r] = val.astype(BF16)


def owner_sums(first, at_ref, got_ref, row_ref, a_ref, b_ref, *sums):
    b_ref[a_ref.shape[0] :, :] = row_ref[...]
    for ref in sums:
        ref[...] = jnp.zeros_like(ref)
    for d in range(N_VIEW):
        for s in range(SLOTS):
            place = at_ref[d, s]
            rows = pl.ds(pl.multiple_of(place * PER, PER), PER)
            sums[s][rows, :] += got_ref[d, s * PER : (s + 1) * PER, :]
            if first:
                line = pl.ds(2 * DATA + place, 1)
                sums[s][line, :] += got_ref[d, DATA + SLOTS + s : DATA + SLOTS + s + 1, :]
    for n, ref in enumerate((a_ref, b_ref)):
        spots = [(0, slice(n * DATA, (n + 1) * DATA), DATA)]
        if first:
            start = 2 * DATA + n * PT_DEV
            spots.append((DATA, slice(start, start + PT_DEV), PT_DEV))
            ref[DATA + PT_DEV : DATA + EXTRA, :] = jnp.zeros((EXTRA - PT_DEV, D), F32)
        for to, rows, size in spots:
            ref[to : to + size, :] = (sums[0][rows, :] + sums[1][rows, :]) + (
                sums[2][rows, :] + sums[3][rows, :]
            )


def owner_project(first, layer, at_ref, me_ref, a_ref, b_ref, ra_ref, rb_ref, w_ref, bias_ref, *rest):
    if first:
        ret_ref, row_ref, scale_ref, proj_ref = rest
    else:
        scale_ref, ret_ref, row_ref, proj_ref = rest
    row_ref[...] = b_ref[a_ref.shape[0] :, :] + rb_ref[a_ref.shape[0] :, :]
    for n, (ref, rref) in enumerate(((a_ref, ra_ref), (b_ref, rb_ref))):
        if first:
            for j in range(PT_DEV):
                line = slice(DATA + j, DATA + j + 1)
                count = ref[line, :TP] + rref[line, :TP]
                at = n * DATA + j * PER
                scale_ref[at : at + PER, :] = spread(count, me_ref[0] * PER, PER)
        half = slice(n * DATA, (n + 1) * DATA)
        term = ((ref[:DATA, :] + rref[:DATA, :]) * scale_ref[half, :]).astype(BF16)
        proj = jnp.dot(term, w_ref[layer], preferred_element_type=F32)
        proj_ref[half, :] = proj + bias_ref[layer : layer + 1, :]
    for d in range(N_VIEW):
        for s in range(SLOTS):
            rows = pl.ds(pl.multiple_of(at_ref[d, s] * PER, PER), PER)
            ret_ref[d, s * PER : (s + 1) * PER, :] = proj_ref[rows, :]


def add_rows(mine_ref, other_ref, out_ref):
    out_ref[...] = mine_ref[...] + other_ref[...]


def view_project(first, layer, row_ref, other_ref, *rest):
    if first:
        w_ref, out_ref, scale_ref = rest
        for v in range(VT_DEV):
            line = slice(ROWS + v, ROWS + v + 1)
            count = row_ref[line, :TP] + other_ref[line, :TP]
            scale_ref[v * TV : (v + 1) * TV, :] = spread(count, 0, TV)
    else:
        scale_ref, w_ref, out_ref = rest
    total = row_ref[:ROWS, :] + other_ref[:ROWS, :]
    term = (total * scale_ref[...]).astype(BF16)
    out_ref[...] = jnp.dot(term, w_ref[layer], preferred_element_type=F32)


def array(*shape, dtype=F32):
    return jax.ShapeDtypeStruct(shape, dtype)


def call(kernel, name, out_shape, in_specs, scratch=(), cost=None):
    return pl.pallas_call(
        kernel,
        out_shape=out_shape,
        in_specs=in_specs,
        out_specs=[full()] * len(out_shape),
        scratch_shapes=list(scratch),
        compiler_params=SMALL,
        cost_estimate=cost,
        name=name,
    )


def from_partner(block, flip):
    route = [(i, i ^ flip) for i in range(lax.axis_size("point"))]
    return lax.ppermute(block, "point", route)


def doubled(block, flip):
    return block + from_partner(block, flip)


def shards(features, tiles, masks, w_self, w_col, w_row, bias):
    barrier = lax.optimization_barrier
    smem = full(pltpu.SMEM)
    me_view = lax.axis_index("view").astype(jnp.int32)
    even = (lax.axis_index("point") % 2) == 0
    n_point = lax.axis_size("point")
    pair_a = [(i, i ^ 1) for i in range(n_point)]
    pair_b = [(i, (i + 1) % n_point if i % 2 else (i - 1) % n_point) for i in range(n_point)]
    tiles_t = pltpu.with_memory_space_constraint(tiles.T, pltpu.HBM)
    slot_shape = (SLOTS, TV, TP, D)
    ret_shape = array(N_VIEW, DATA, D)

    def whole(*shape):
        return pl.BlockSpec(shape, lambda i, j, t: (0,) * len(shape))

    def slot_spec(base=0, views=TV):
        return pl.BlockSpec((1, views, TP, D), lambda i, j, t: (i + base, j, 0, 0))

    def mask_spec(base=0):
        return pl.BlockSpec((1, TV, TP), lambda i, j, t: (i + base, 0, 0))

    def by_slot(kernel, name, out_shape, in_specs, out_specs, grid=(SLOTS, 1), **kwargs):
        return pl.pallas_call(
            kernel,
            out_shape=out_shape,
            grid_spec=pltpu.PrefetchScalarGridSpec(
                num_scalar_prefetch=1, grid=grid, in_specs=in_specs, out_specs=out_specs
            ),
            compiler_params=LARGE,
            name=name,
            **kwargs,
        )

    def layer_specs(base=0, views=TV):
        return [
            slot_spec(base, views),
            mask_spec(base),
            whole(N_VIEW, DATA, D),
            whole(ROWS, D),
            whole(LAYERS, D, D),
        ]

    def some_state(layer, base, slots, views, old, partial=None):
        tail = [] if partial is None else [partial]
        (out,) = by_slot(
            functools.partial(layer_state, layer, base),
            "layer_state",
            [array(*slot_shape, dtype=BF16)],
            layer_specs(base, views) + [full(pltpu.HBM)] * len(tail),
            [slot_spec(base, views)],
            (slots, TV // views),
            input_output_aliases={6: 0} if tail else {},
            cost_estimate=STATE,
        )(*old, *tail)
        return out

    def after(old, value):
        value, back, row_proj = barrier((value, old[3], old[4]))
        return old[:3] + (back, row_proj, old[5]), value

    masks = pltpu.with_memory_space_constraint(masks, pltpu.HBM)
    features = pltpu.with_memory_space_constraint(features, pltpu.HBM)
    col_pay, row_sum = by_slot(
        first_sums,
        "first_sums",
        [array(N_VIEW, DATA + EXTRA, D), array(ROWS + 8, D)],
        [slot_spec(), mask_spec()],
        [whole(N_VIEW, DATA + EXTRA, D), whole(ROWS + 8, D)],
    )(tiles_t, features, masks)

    state = features
    place = col_scale = row_scale = old = None
    for layer in range(LAYERS):
        first = layer == 0
        last = layer == LAYERS - 1
        got = lax.all_to_all(col_pay, "view", 0, 0, tiled=True)
        row_other = from_partner(row_sum, 4)
        if not first:
            old, row_other = after(old, row_other)
            state = some_state(layer - 1, 0, 1, TV, old)
        (row_sum,) = call(
            add_rows, "add_rows", [array(*row_sum.shape)], [full()] * 2, cost=EARLY
        )(row_sum, row_other)
        row_sum = doubled(row_sum, 1)
        got, row_sum, state = barrier((got, row_sum, state))
        if first:
            point_id = got[:, DATA : DATA + SLOTS, 0].astype(jnp.int32)
            place = jnp.where(even, point_id ^ PT_DEV, point_id)
        extra = EXTRA if first else 0
        part_a, part_b = call(
            functools.partial(owner_sums, first),
            "owner_sums",
            [array(DATA + extra, D), array(DATA + ROWS + 2 * extra, D)],
            [smem, full(), full()],
            [pltpu.VMEM((2 * DATA + extra, D), F32)] * SLOTS,
        )(place, got, row_sum)
        from_b = lax.ppermute(part_b, "point", pair_b)
        from_a = lax.ppermute(part_a, "point", pair_a)
        if not first:
            old, from_a = after(old, from_a)
            state = some_state(layer - 1, 1, 1, TV, old, state)
            from_b, state = barrier((from_b, state))
        outs = call(
            functools.partial(owner_project, first, layer),
            "owner_project",
            [ret_shape, array(ROWS + extra, D)] + ([array(2 * DATA, D)] if first else []),
            [smem, smem] + [full()] * (6 if first else 7),
            [pltpu.VMEM((2 * DATA, D), F32)],
        )(
            place,
            me_view[None],
            part_a,
            part_b,
            from_a,
            from_b,
            w_col,
            bias,
            *(() if first else (col_scale,)),
        )
        row_sum = outs[1]
        row_other = from_partner(row_sum, 8)
        if first:
            col_scale = outs[2]
        back = lax.all_to_all(outs[0], "view", 0, 0, tiled=True)
        if not first:
            old, row_other = after(old, row_other)
            state = some_state(layer - 1, 2, 2, TV, old, state)
            back, state = barrier((back, state))
        outs = call(
            functools.partial(view_project, first, layer),
            "view_project",
            [array(ROWS, D)] * (2 if first else 1),
            [full()] * (3 if first else 4),
            cost=EARLY,
        )(row_sum, row_other, *(() if first else (row_scale,)), w_row)
        row_proj = outs[0]
        if first:
            row_scale = outs[1]
        old = (tiles_t, state, masks, back, row_proj, w_self)
        if last:
            return some_state(layer, 0, SLOTS, TV, old)
        col_pay, row_sum = by_slot(
            functools.partial(layer_sums, layer),
            "layer_sums",
            [ret_shape, array(ROWS, D)],
            layer_specs(),
            [whole(N_VIEW, DATA, D), whole(ROWS, D)],
        )(*old)


def solution(mesh):
    in_specs = (
        P(("view", "point"), None, None, None),
        P(("view", "point"), None),
        P(("view", "point"), None, None),
        P(),
        P(),
        P(),
        P(),
    )
    out_specs = P(("view", "point"), None, None, None)
    return jax.shard_map(shards, mesh=mesh, in_specs=in_specs, out_specs=out_specs, check_vma=False)
```

```python
import functools

import jax
import jax.numpy as jnp
from jax import lax
from jax.experimental import pallas as pl
from jax.experimental.pallas import tpu as pltpu
from jax.sharding import PartitionSpec as P

VT_DEV = 4
PT_DEV = 4
LAYERS = 3
SLOTS = 4
TV = 32
TP = 128
D = 256
N_VIEW = 8
PER = TP // N_VIEW
DATA = SLOTS * PER
EXTRA = 8
ROWS = VT_DEV * TV
RC = 4
KEPT = 2
EARLY = pl.CostEstimate(flops=40_000_000_000, transcendentals=0, bytes_accessed=100_000_000)
STATE = pl.CostEstimate(flops=1_100_000_000, transcendentals=0, bytes_accessed=12_000_000)
F32 = jnp.float32
BF16 = jnp.bfloat16
SMALL = pltpu.CompilerParams(vmem_limit_bytes=8 * 1024 * 1024)
LARGE = pltpu.CompilerParams(vmem_limit_bytes=48 * 1024 * 1024)


def full(memory_space=pltpu.VMEM):
    return pl.BlockSpec(memory_space=memory_space)


def spread(counts, first_lane, rows):
    lane = lax.broadcasted_iota(jnp.int32, (rows, TP), 1)
    line = lax.broadcasted_iota(jnp.int32, (rows, TP), 0) + first_lane
    picked = jnp.where(lane == line, jnp.broadcast_to(counts, (rows, TP)), 0.0)
    count = jnp.sum(picked, axis=1, keepdims=True)
    return jnp.broadcast_to(1.0 / jnp.sqrt(jnp.maximum(count, 1.0)), (rows, D))


def first_sums(tiles_ref, x_ref, m_ref, col_ref, row_ref):
    slot = pl.program_id(0)
    mask = m_ref[0].astype(F32)
    mask_t = mask.T
    col_count = jnp.sum(mask, axis=0, keepdims=True)
    row_count = jnp.sum(mask_t, axis=0, keepdims=True)
    padded = jnp.concatenate([col_count, jnp.zeros((1, D - TP), F32)], axis=1)
    padded_row = jnp.concatenate([row_count, jnp.zeros((1, D - TV), F32)], axis=1)
    point_id = jnp.full((1, D), tiles_ref[1, slot], jnp.int32).astype(F32)

    @pl.when(slot == 0)
    def _():
        row_ref[...] = jnp.zeros_like(row_ref)

    for s in range(SLOTS):

        @pl.when(slot == s)
        def _():
            for peer in range(N_VIEW):
                col_ref[peer, DATA + s : DATA + s + 1, :] = point_id
                col_ref[peer, DATA + SLOTS + s : DATA + SLOTS + s + 1, :] = padded

    for v in range(VT_DEV):
        hit = jnp.where(tiles_ref[0, slot] == v, 1.0, 0.0).astype(F32)
        row_ref[ROWS + v : ROWS + v + 1, :] += padded_row * hit
    acc = None
    totals = []
    for r in range(TV):
        val = x_ref[0, r].astype(F32) * mask_t[:, r : r + 1]
        acc = val if acc is None else acc + val
        totals.append(jnp.sum(val, axis=0, keepdims=True))
    store_sums(slot, tiles_ref, acc, totals, col_ref, row_ref)


def store_sums(slot, tiles_ref, acc, totals, col_ref, row_ref):
    here = pl.ds(pl.multiple_of(slot * PER, PER), PER)
    for peer in range(N_VIEW):
        col_ref[peer, here, :] = acc[peer * PER : (peer + 1) * PER]
    view_at = pl.multiple_of(tiles_ref[0, slot] * TV, TV)
    row_ref[pl.ds(view_at, TV), :] += jnp.concatenate(totals, axis=0)


def relu_mixed(x_ref, mask_t, weight, col_proj, row_proj, r0):
    block = x_ref[0, r0 : r0 + RC].reshape(RC * TP, D)
    prod = jnp.dot(block, weight, preferred_element_type=F32)
    for k in range(RC):
        r = r0 + k
        val = prod[k * TP : (k + 1) * TP] + col_proj + row_proj[r : r + 1, :]
        yield r, jnp.maximum(val, 0.0) * mask_t[:, r : r + 1]


def layer_sums(
    layer, tiles_ref, x_ref, m_ref, ret_ref, rowp_ref, w_ref, *outs
):
    col_ref, row_ref, state_hbm, held, sems = outs
    slot = pl.program_id(0)
    spot = jnp.minimum(slot, KEPT)
    copies = [
        pltpu.make_async_copy(held.at[k], state_hbm.at[k], sems.at[k]) for k in range(KEPT)
    ]

    @pl.when(slot == 0)
    def _():
        row_ref[...] = jnp.zeros_like(row_ref)

    view_at = pl.multiple_of(tiles_ref[0, slot] * TV, TV)
    row_proj = rowp_ref[pl.ds(view_at, TV), :]
    mask_t = m_ref[0].astype(F32).T
    col_proj = ret_ref[:, pl.ds(pl.multiple_of(slot * PER, PER), PER), :].reshape(TP, D)
    acc = None
    totals = []
    for r0 in range(0, TV, RC):
        for r, val in relu_mixed(x_ref, mask_t, w_ref[layer], col_proj, row_proj, r0):
            held[spot, r] = val.astype(BF16)
            acc = val if acc is None else acc + val
            totals.append(jnp.sum(val, axis=0, keepdims=True))
    store_sums(slot, tiles_ref, acc, totals, col_ref, row_ref)
    for k, copy in enumerate(copies):
        pl.when(slot == k)(copy.start)

    @pl.when(slot == SLOTS - 1)
    def _():
        for copy in copies:
            copy.wait()


def layer_state(layer, base, tiles_ref, x_ref, m_ref, ret_ref, rowp_ref, w_ref, *outs):
    slot = pl.program_id(0) + base
    count = x_ref.shape[1]
    start = pl.multiple_of(pl.program_id(1) * count, count)
    view_at = pl.multiple_of(tiles_ref[0, slot] * TV + start, count)
    row_proj = rowp_ref[pl.ds(view_at, count), :]
    mask_t = m_ref[0, pl.ds(start, count), :].astype(F32).T
    col_proj = ret_ref[:, pl.ds(pl.multiple_of(slot * PER, PER), PER), :].reshape(TP, D)
    for r0 in range(0, count, RC):
        for r, val in relu_mixed(x_ref, mask_t, w_ref[layer], col_proj, row_proj, r0):
            outs[-1][0, r] = val.astype(BF16)


def owner_sums(first, at_ref, got_ref, row_ref, a_ref, b_ref, *sums):
    b_ref[a_ref.shape[0] :, :] = row_ref[...]
    for ref in sums:
        ref[...] = jnp.zeros_like(ref)
    for d in range(N_VIEW):
        for s in range(SLOTS):
            place = at_ref[d, s]
            rows = pl.ds(pl.multiple_of(place * PER, PER), PER)
            sums[s][rows, :] += got_ref[d, s * PER : (s + 1) * PER, :]
            if first:
                line = pl.ds(2 * DATA + place, 1)
                sums[s][line, :] += got_ref[d, DATA + SLOTS + s : DATA + SLOTS + s + 1, :]
    for n, ref in enumerate((a_ref, b_ref)):
        spots = [(0, slice(n * DATA, (n + 1) * DATA), DATA)]
        if first:
            start = 2 * DATA + n * PT_DEV
            spots.append((DATA, slice(start, start + PT_DEV), PT_DEV))
            ref[DATA + PT_DEV : DATA + EXTRA, :] = jnp.zeros((EXTRA - PT_DEV, D), F32)
        for to, rows, size in spots:
            ref[to : to + size, :] = (sums[0][rows, :] + sums[1][rows, :]) + (
                sums[2][rows, :] + sums[3][rows, :]
            )


def owner_project(first, layer, at_ref, me_ref, a_ref, b_ref, ra_ref, rb_ref, w_ref, bias_ref, *rest):
    if first:
        ret_ref, row_ref, scale_ref, proj_ref = rest
    else:
        scale_ref, ret_ref, row_ref, proj_ref = rest
    row_ref[...] = b_ref[a_ref.shape[0] :, :] + rb_ref[a_ref.shape[0] :, :]
    for n, (ref, rref) in enumerate(((a_ref, ra_ref), (b_ref, rb_ref))):
        if first:
            for j in range(PT_DEV):
                line = slice(DATA + j, DATA + j + 1)
                count = ref[line, :TP] + rref[line, :TP]
                at = n * DATA + j * PER
                scale_ref[at : at + PER, :] = spread(count, me_ref[0] * PER, PER)
        half = slice(n * DATA, (n + 1) * DATA)
        term = ((ref[:DATA, :] + rref[:DATA, :]) * scale_ref[half, :]).astype(BF16)
        proj = jnp.dot(term, w_ref[layer], preferred_element_type=F32)
        proj_ref[half, :] = proj + bias_ref[layer : layer + 1, :]
    for d in range(N_VIEW):
        for s in range(SLOTS):
            rows = pl.ds(pl.multiple_of(at_ref[d, s] * PER, PER), PER)
            ret_ref[d, s * PER : (s + 1) * PER, :] = proj_ref[rows, :]


def add_rows(mine_ref, other_ref, out_ref):
    out_ref[...] = mine_ref[...] + other_ref[...]


def view_project(first, layer, row_ref, other_ref, *rest):
    if first:
        w_ref, out_ref, scale_ref = rest
        for v in range(VT_DEV):
            line = slice(ROWS + v, ROWS + v + 1)
            count = row_ref[line, :TP] + other_ref[line, :TP]
            scale_ref[v * TV : (v + 1) * TV, :] = spread(count, 0, TV)
    else:
        scale_ref, w_ref, out_ref = rest
    total = row_ref[:ROWS, :] + other_ref[:ROWS, :]
    term = (total * scale_ref[...]).astype(BF16)
    out_ref[...] = jnp.dot(term, w_ref[layer], preferred_element_type=F32)


def array(*shape, dtype=F32):
    return jax.ShapeDtypeStruct(shape, dtype)


def call(kernel, name, out_shape, in_specs, scratch=(), cost=None):
    return pl.pallas_call(
        kernel,
        out_shape=out_shape,
        in_specs=in_specs,
        out_specs=[full()] * len(out_shape),
        scratch_shapes=list(scratch),
        compiler_params=SMALL,
        cost_estimate=cost,
        name=name,
    )


def from_partner(block, flip):
    route = [(i, i ^ flip) for i in range(lax.axis_size("point"))]
    return lax.ppermute(block, "point", route)


def doubled(block, flip):
    return block + from_partner(block, flip)


def shards(features, tiles, masks, w_self, w_col, w_row, bias):
    barrier = lax.optimization_barrier
    smem = full(pltpu.SMEM)
    me_view = lax.axis_index("view").astype(jnp.int32)
    even = (lax.axis_index("point") % 2) == 0
    n_point = lax.axis_size("point")
    pair_a = [(i, i ^ 1) for i in range(n_point)]
    pair_b = [(i, (i + 1) % n_point if i % 2 else (i - 1) % n_point) for i in range(n_point)]
    tiles_t = pltpu.with_memory_space_constraint(tiles.T, pltpu.HBM)
    slot_shape = (SLOTS, TV, TP, D)
    ret_shape = array(N_VIEW, DATA, D)

    def whole(*shape):
        return pl.BlockSpec(shape, lambda i, j, t: (0,) * len(shape))

    def slot_spec(base=0, views=TV):
        return pl.BlockSpec((1, views, TP, D), lambda i, j, t: (i + base, j, 0, 0))

    def mask_spec(base=0):
        return pl.BlockSpec((1, TV, TP), lambda i, j, t: (i + base, 0, 0))

    def by_slot(kernel, name, out_shape, in_specs, out_specs, grid=(SLOTS, 1), scratch=(), **kwargs):
        return pl.pallas_call(
            kernel,
            out_shape=out_shape,
            grid_spec=pltpu.PrefetchScalarGridSpec(
                num_scalar_prefetch=1,
                grid=grid,
                in_specs=in_specs,
                out_specs=out_specs,
                scratch_shapes=list(scratch),
            ),
            compiler_params=LARGE,
            name=name,
            **kwargs,
        )

    def layer_specs(base=0, views=TV):
        return [
            slot_spec(base, views),
            mask_spec(base),
            whole(N_VIEW, DATA, D),
            whole(ROWS, D),
            whole(LAYERS, D, D),
        ]

    def some_state(layer, base, slots, views, old, partial=None):
        tail = [] if partial is None else [partial]
        (out,) = by_slot(
            functools.partial(layer_state, layer, base),
            "layer_state",
            [array(*slot_shape, dtype=BF16)],
            layer_specs(base, views) + [full(pltpu.HBM)] * len(tail),
            [slot_spec(base, views)],
            (slots, TV // views),
            input_output_aliases={6: 0} if tail else {},
            cost_estimate=STATE,
        )(*old, *tail)
        return out

    def after(old, value):
        value, back, row_proj = barrier((value, old[3], old[4]))
        return old[:3] + (back, row_proj, old[5]), value

    masks = pltpu.with_memory_space_constraint(masks, pltpu.HBM)
    features = pltpu.with_memory_space_constraint(features, pltpu.HBM)
    col_pay, row_sum = by_slot(
        first_sums,
        "first_sums",
        [array(N_VIEW, DATA + EXTRA, D), array(ROWS + 8, D)],
        [slot_spec(), mask_spec()],
        [whole(N_VIEW, DATA + EXTRA, D), whole(ROWS + 8, D)],
    )(tiles_t, features, masks)

    state = features
    place = col_scale = row_scale = old = None
    for layer in range(LAYERS):
        first = layer == 0
        last = layer == LAYERS - 1
        got = lax.all_to_all(col_pay, "view", 0, 0, tiled=True)
        row_other = from_partner(row_sum, 4)
        (row_sum,) = call(
            add_rows, "add_rows", [array(*row_sum.shape)], [full()] * 2, cost=EARLY
        )(row_sum, row_other)
        row_sum = doubled(row_sum, 1)
        got, row_sum = barrier((got, row_sum))
        if first:
            point_id = got[:, DATA : DATA + SLOTS, 0].astype(jnp.int32)
            place = jnp.where(even, point_id ^ PT_DEV, point_id)
        extra = EXTRA if first else 0
        part_a, part_b = call(
            functools.partial(owner_sums, first),
            "owner_sums",
            [array(DATA + extra, D), array(DATA + ROWS + 2 * extra, D)],
            [smem, full(), full()],
            [pltpu.VMEM((2 * DATA + extra, D), F32)] * SLOTS,
        )(place, got, row_sum)
        from_b = lax.ppermute(part_b, "point", pair_b)
        from_a = lax.ppermute(part_a, "point", pair_a)
        outs = call(
            functools.partial(owner_project, first, layer),
            "owner_project",
            [ret_shape, array(ROWS + extra, D)] + ([array(2 * DATA, D)] if first else []),
            [smem, smem] + [full()] * (6 if first else 7),
            [pltpu.VMEM((2 * DATA, D), F32)],
        )(
            place,
            me_view[None],
            part_a,
            part_b,
            from_a,
            from_b,
            w_col,
            bias,
            *(() if first else (col_scale,)),
        )
        row_sum = outs[1]
        row_other = from_partner(row_sum, 8)
        if first:
            col_scale = outs[2]
        back = lax.all_to_all(outs[0], "view", 0, 0, tiled=True)
        if not first:
            old, row_other = after(old, row_other)
            state = some_state(layer - 1, KEPT, SLOTS - KEPT, TV, old, state)
            back, state = barrier((back, state))
        outs = call(
            functools.partial(view_project, first, layer),
            "view_project",
            [array(ROWS, D)] * (2 if first else 1),
            [full()] * (3 if first else 4),
            cost=EARLY,
        )(row_sum, row_other, *(() if first else (row_scale,)), w_row)
        row_proj = outs[0]
        if first:
            row_scale = outs[1]
        old = (tiles_t, state, masks, back, row_proj, w_self)
        if last:
            return some_state(layer, 0, SLOTS, TV, old)
        col_pay, row_sum, state = by_slot(
            functools.partial(layer_sums, layer),
            "layer_sums",
            [ret_shape, array(ROWS, D), array(*slot_shape, dtype=BF16)],
            layer_specs(),
            [whole(N_VIEW, DATA, D), whole(ROWS, D), full(pltpu.HBM)],
            scratch=[
                pltpu.VMEM((KEPT + 1, TV, TP, D), BF16),
                pltpu.SemaphoreType.DMA((KEPT,)),
            ],
        )(*old)


def solution(mesh):
    in_specs = (
        P(("view", "point"), None, None, None),
        P(("view", "point"), None),
        P(("view", "point"), None, None),
        P(),
        P(),
        P(),
        P(),
    )
    out_specs = P(("view", "point"), None, None, None)
    return jax.shard_map(shards, mesh=mesh, in_specs=in_specs, out_specs=out_specs, check_vma=False)
```

```python
import functools

import jax
import jax.numpy as jnp
from jax import lax
from jax.experimental import pallas as pl
from jax.experimental.pallas import tpu as pltpu
from jax.sharding import PartitionSpec as P

VT_DEV = 4
PT_DEV = 4
LAYERS = 3
SLOTS = 4
TV = 32
TP = 128
D = 256
N_VIEW = 8
PER = TP // N_VIEW
DATA = SLOTS * PER
EXTRA = 8
ROWS = VT_DEV * TV
RC = 4
KEPT = 2
EARLY = pl.CostEstimate(flops=40_000_000_000, transcendentals=0, bytes_accessed=100_000_000)
STATE = pl.CostEstimate(flops=1_100_000_000, transcendentals=0, bytes_accessed=12_000_000)
F32 = jnp.float32
BF16 = jnp.bfloat16
SMALL = pltpu.CompilerParams(vmem_limit_bytes=8 * 1024 * 1024)
LARGE = pltpu.CompilerParams(vmem_limit_bytes=48 * 1024 * 1024)


def full(memory_space=pltpu.VMEM):
    return pl.BlockSpec(memory_space=memory_space)


def spread(counts, first_lane, rows):
    lane = lax.broadcasted_iota(jnp.int32, (rows, TP), 1)
    line = lax.broadcasted_iota(jnp.int32, (rows, TP), 0) + first_lane
    picked = jnp.where(lane == line, jnp.broadcast_to(counts, (rows, TP)), 0.0)
    count = jnp.sum(picked, axis=1, keepdims=True)
    return jnp.broadcast_to(1.0 / jnp.sqrt(jnp.maximum(count, 1.0)), (rows, D))


def first_sums(tiles_ref, x_ref, m_ref, col_ref, row_ref):
    slot = pl.program_id(0)
    mask = m_ref[0].astype(F32)
    mask_t = mask.T
    col_count = jnp.sum(mask, axis=0, keepdims=True)
    row_count = jnp.sum(mask_t, axis=0, keepdims=True)
    padded = jnp.concatenate([col_count, jnp.zeros((1, D - TP), F32)], axis=1)
    padded_row = jnp.concatenate([row_count, jnp.zeros((1, D - TV), F32)], axis=1)
    point_id = jnp.full((1, D), tiles_ref[1, slot], jnp.int32).astype(F32)

    @pl.when(slot == 0)
    def _():
        row_ref[...] = jnp.zeros_like(row_ref)

    for s in range(SLOTS):

        @pl.when(slot == s)
        def _():
            for peer in range(N_VIEW):
                col_ref[peer, DATA + s : DATA + s + 1, :] = point_id
                col_ref[peer, DATA + SLOTS + s : DATA + SLOTS + s + 1, :] = padded

    for v in range(VT_DEV):
        hit = jnp.where(tiles_ref[0, slot] == v, 1.0, 0.0).astype(F32)
        row_ref[ROWS + v : ROWS + v + 1, :] += padded_row * hit
    acc = None
    totals = []
    for r in range(TV):
        val = x_ref[0, r].astype(F32) * mask_t[:, r : r + 1]
        acc = val if acc is None else acc + val
        totals.append(jnp.sum(val, axis=0, keepdims=True))
    store_sums(slot, tiles_ref, acc, totals, col_ref, row_ref)


def store_sums(slot, tiles_ref, acc, totals, col_ref, row_ref):
    here = pl.ds(pl.multiple_of(slot * PER, PER), PER)
    for peer in range(N_VIEW):
        col_ref[peer, here, :] = acc[peer * PER : (peer + 1) * PER]
    view_at = pl.multiple_of(tiles_ref[0, slot] * TV, TV)
    row_ref[pl.ds(view_at, TV), :] += jnp.concatenate(totals, axis=0)


def relu_mixed(x_ref, mask_t, weight, col_proj, row_proj, r0):
    block = x_ref[0, r0 : r0 + RC].reshape(RC * TP, D)
    prod = jnp.dot(block, weight, preferred_element_type=F32)
    for k in range(RC):
        r = r0 + k
        val = prod[k * TP : (k + 1) * TP] + col_proj + row_proj[r : r + 1, :]
        yield r, jnp.maximum(val, 0.0) * mask_t[:, r : r + 1]


def layer_sums(
    layer, tiles_ref, x_ref, m_ref, ret_ref, rowp_ref, w_ref, *outs
):
    col_ref, row_ref, state_hbm, held, sems = outs
    slot = pl.program_id(0)
    spot = jnp.minimum(slot, KEPT)
    copies = [
        pltpu.make_async_copy(held.at[k], state_hbm.at[k], sems.at[k]) for k in range(KEPT)
    ]

    @pl.when(slot == 0)
    def _():
        row_ref[...] = jnp.zeros_like(row_ref)

    view_at = pl.multiple_of(tiles_ref[0, slot] * TV, TV)
    row_proj = rowp_ref[pl.ds(view_at, TV), :]
    mask_t = m_ref[0].astype(F32).T
    col_proj = ret_ref[:, pl.ds(pl.multiple_of(slot * PER, PER), PER), :].reshape(TP, D)
    acc = None
    totals = []
    for r0 in range(0, TV, RC):
        for r, val in relu_mixed(x_ref, mask_t, w_ref[layer], col_proj, row_proj, r0):
            held[spot, r] = val.astype(BF16)
            acc = val if acc is None else acc + val
            totals.append(jnp.sum(val, axis=0, keepdims=True))
    store_sums(slot, tiles_ref, acc, totals, col_ref, row_ref)
    for k, copy in enumerate(copies):
        pl.when(slot == k)(copy.start)

    @pl.when(slot == SLOTS - 1)
    def _():
        for copy in copies:
            copy.wait()


def layer_state(layer, base, tiles_ref, x_ref, m_ref, ret_ref, rowp_ref, w_ref, *outs):
    slot = pl.program_id(0) + base
    count = x_ref.shape[1]
    start = pl.multiple_of(pl.program_id(1) * count, count)
    view_at = pl.multiple_of(tiles_ref[0, slot] * TV + start, count)
    row_proj = rowp_ref[pl.ds(view_at, count), :]
    mask_t = m_ref[0, pl.ds(start, count), :].astype(F32).T
    col_proj = ret_ref[:, pl.ds(pl.multiple_of(slot * PER, PER), PER), :].reshape(TP, D)
    for r0 in range(0, count, RC):
        for r, val in relu_mixed(x_ref, mask_t, w_ref[layer], col_proj, row_proj, r0):
            outs[-1][0, r] = val.astype(BF16)


def owner_sums(first, at_ref, got_ref, row_ref, a_ref, b_ref, *sums):
    b_ref[a_ref.shape[0] :, :] = row_ref[...]
    for ref in sums:
        ref[...] = jnp.zeros_like(ref)
    for d in range(N_VIEW):
        for s in range(SLOTS):
            place = at_ref[d, s]
            rows = pl.ds(pl.multiple_of(place * PER, PER), PER)
            sums[s][rows, :] += got_ref[d, s * PER : (s + 1) * PER, :]
            if first:
                line = pl.ds(2 * DATA + place, 1)
                sums[s][line, :] += got_ref[d, DATA + SLOTS + s : DATA + SLOTS + s + 1, :]
    for n, ref in enumerate((a_ref, b_ref)):
        spots = [(0, slice(n * DATA, (n + 1) * DATA), DATA)]
        if first:
            start = 2 * DATA + n * PT_DEV
            spots.append((DATA, slice(start, start + PT_DEV), PT_DEV))
            ref[DATA + PT_DEV : DATA + EXTRA, :] = jnp.zeros((EXTRA - PT_DEV, D), F32)
        for to, rows, size in spots:
            ref[to : to + size, :] = (sums[0][rows, :] + sums[1][rows, :]) + (
                sums[2][rows, :] + sums[3][rows, :]
            )


def owner_project(first, layer, at_ref, me_ref, a_ref, b_ref, ra_ref, rb_ref, w_ref, bias_ref, *rest):
    if first:
        ret_ref, row_ref, scale_ref, proj_ref = rest
    else:
        scale_ref, ret_ref, row_ref, proj_ref = rest
    row_ref[...] = b_ref[a_ref.shape[0] :, :] + rb_ref[a_ref.shape[0] :, :]
    for n, (ref, rref) in enumerate(((a_ref, ra_ref), (b_ref, rb_ref))):
        if first:
            for j in range(PT_DEV):
                line = slice(DATA + j, DATA + j + 1)
                count = ref[line, :TP] + rref[line, :TP]
                at = n * DATA + j * PER
                scale_ref[at : at + PER, :] = spread(count, me_ref[0] * PER, PER)
        half = slice(n * DATA, (n + 1) * DATA)
        term = ((ref[:DATA, :] + rref[:DATA, :]) * scale_ref[half, :]).astype(BF16)
        proj = jnp.dot(term, w_ref[layer], preferred_element_type=F32)
        proj_ref[half, :] = proj + bias_ref[layer : layer + 1, :]
    for d in range(N_VIEW):
        for s in range(SLOTS):
            rows = pl.ds(pl.multiple_of(at_ref[d, s] * PER, PER), PER)
            ret_ref[d, s * PER : (s + 1) * PER, :] = proj_ref[rows, :]


def add_rows(mine_ref, other_ref, out_ref):
    out_ref[...] = mine_ref[...] + other_ref[...]


def view_project(first, layer, row_ref, other_ref, *rest):
    if first:
        w_ref, out_ref, scale_ref = rest
        for v in range(VT_DEV):
            line = slice(ROWS + v, ROWS + v + 1)
            count = row_ref[line, :TP] + other_ref[line, :TP]
            scale_ref[v * TV : (v + 1) * TV, :] = spread(count, 0, TV)
    else:
        scale_ref, w_ref, out_ref = rest
    total = row_ref[:ROWS, :] + other_ref[:ROWS, :]
    term = (total * scale_ref[...]).astype(BF16)
    out_ref[...] = jnp.dot(term, w_ref[layer], preferred_element_type=F32)


def array(*shape, dtype=F32):
    return jax.ShapeDtypeStruct(shape, dtype)


def call(kernel, name, out_shape, in_specs, scratch=(), cost=None):
    return pl.pallas_call(
        kernel,
        out_shape=out_shape,
        in_specs=in_specs,
        out_specs=[full()] * len(out_shape),
        scratch_shapes=list(scratch),
        compiler_params=SMALL,
        cost_estimate=cost,
        name=name,
    )


def from_partner(block, flip):
    route = [(i, i ^ flip) for i in range(lax.axis_size("point"))]
    return lax.ppermute(block, "point", route)


def doubled(block, flip):
    return block + from_partner(block, flip)


def shards(features, tiles, masks, w_self, w_col, w_row, bias):
    barrier = lax.optimization_barrier
    smem = full(pltpu.SMEM)
    me_view = lax.axis_index("view").astype(jnp.int32)
    even = (lax.axis_index("point") % 2) == 0
    n_point = lax.axis_size("point")
    pair_a = [(i, i ^ 1) for i in range(n_point)]
    pair_b = [(i, (i + 1) % n_point if i % 2 else (i - 1) % n_point) for i in range(n_point)]
    tiles_t = pltpu.with_memory_space_constraint(tiles.T, pltpu.HBM)
    slot_shape = (SLOTS, TV, TP, D)
    ret_shape = array(N_VIEW, DATA, D)

    def whole(*shape):
        return pl.BlockSpec(shape, lambda i, j, t: (0,) * len(shape))

    def slot_spec(base=0, views=TV):
        return pl.BlockSpec((1, views, TP, D), lambda i, j, t: (i + base, j, 0, 0))

    def mask_spec(base=0):
        return pl.BlockSpec((1, TV, TP), lambda i, j, t: (i + base, 0, 0))

    def by_slot(kernel, name, out_shape, in_specs, out_specs, grid=(SLOTS, 1), scratch=(), **kwargs):
        return pl.pallas_call(
            kernel,
            out_shape=out_shape,
            grid_spec=pltpu.PrefetchScalarGridSpec(
                num_scalar_prefetch=1,
                grid=grid,
                in_specs=in_specs,
                out_specs=out_specs,
                scratch_shapes=list(scratch),
            ),
            compiler_params=LARGE,
            name=name,
            **kwargs,
        )

    def layer_specs(base=0, views=TV):
        return [
            slot_spec(base, views),
            mask_spec(base),
            whole(N_VIEW, DATA, D),
            whole(ROWS, D),
            whole(LAYERS, D, D),
        ]

    def some_state(layer, base, slots, views, old, partial=None):
        tail = [] if partial is None else [partial]
        (out,) = by_slot(
            functools.partial(layer_state, layer, base),
            "layer_state",
            [array(*slot_shape, dtype=BF16)],
            layer_specs(base, views) + [full(pltpu.HBM)] * len(tail),
            [slot_spec(base, views)],
            (slots, TV // views),
            input_output_aliases={6: 0} if tail else {},
            cost_estimate=STATE,
        )(*old, *tail)
        return out

    def after(old, value):
        value, back, row_proj = barrier((value, old[3], old[4]))
        return old[:3] + (back, row_proj, old[5]), value

    masks = pltpu.with_memory_space_constraint(masks, pltpu.HBM)
    features = pltpu.with_memory_space_constraint(features, pltpu.HBM)
    col_pay, row_sum = by_slot(
        first_sums,
        "first_sums",
        [array(N_VIEW, DATA + EXTRA, D), array(ROWS + 8, D)],
        [slot_spec(), mask_spec()],
        [whole(N_VIEW, DATA + EXTRA, D), whole(ROWS + 8, D)],
    )(tiles_t, features, masks)

    state = features
    place = col_scale = row_scale = old = None
    for layer in range(LAYERS):
        first = layer == 0
        last = layer == LAYERS - 1
        got = lax.all_to_all(col_pay, "view", 0, 0, tiled=True)
        row_other = from_partner(row_sum, 8)
        (row_sum,) = call(
            add_rows, "add_rows", [array(*row_sum.shape)], [full()] * 2, cost=EARLY
        )(row_sum, row_other)
        row_sum = doubled(row_sum, 1)
        got, row_sum = barrier((got, row_sum))
        if first:
            point_id = got[:, DATA : DATA + SLOTS, 0].astype(jnp.int32)
            place = jnp.where(even, point_id ^ PT_DEV, point_id)
        extra = EXTRA if first else 0
        part_a, part_b = call(
            functools.partial(owner_sums, first),
            "owner_sums",
            [array(DATA + extra, D), array(DATA + ROWS + 2 * extra, D)],
            [smem, full(), full()],
            [pltpu.VMEM((2 * DATA + extra, D), F32)] * SLOTS,
        )(place, got, row_sum)
        from_b = lax.ppermute(part_b, "point", pair_b)
        from_a = lax.ppermute(part_a, "point", pair_a)
        outs = call(
            functools.partial(owner_project, first, layer),
            "owner_project",
            [ret_shape, array(ROWS + extra, D)] + ([array(2 * DATA, D)] if first else []),
            [smem, smem] + [full()] * (6 if first else 7),
            [pltpu.VMEM((2 * DATA, D), F32)],
        )(
            place,
            me_view[None],
            part_a,
            part_b,
            from_a,
            from_b,
            w_col,
            bias,
            *(() if first else (col_scale,)),
        )
        row_sum = outs[1]
        row_other = from_partner(row_sum, 4)
        if first:
            col_scale = outs[2]
        back = lax.all_to_all(outs[0], "view", 0, 0, tiled=True)
        if not first:
            old, row_other = after(old, row_other)
            state = some_state(layer - 1, KEPT, SLOTS - KEPT, TV, old, state)
            back, state = barrier((back, state))
        outs = call(
            functools.partial(view_project, first, layer),
            "view_project",
            [array(ROWS, D)] * (2 if first else 1),
            [full()] * (3 if first else 4),
            cost=EARLY,
        )(row_sum, row_other, *(() if first else (row_scale,)), w_row)
        row_proj = outs[0]
        if first:
            row_scale = outs[1]
        old = (tiles_t, state, masks, back, row_proj, w_self)
        if last:
            return some_state(layer, 0, SLOTS, TV, old)
        col_pay, row_sum, state = by_slot(
            functools.partial(layer_sums, layer),
            "layer_sums",
            [ret_shape, array(ROWS, D), array(*slot_shape, dtype=BF16)],
            layer_specs(),
            [whole(N_VIEW, DATA, D), whole(ROWS, D), full(pltpu.HBM)],
            scratch=[
                pltpu.VMEM((KEPT + 1, TV, TP, D), BF16),
                pltpu.SemaphoreType.DMA((KEPT,)),
            ],
        )(*old)


def solution(mesh):
    in_specs = (
        P(("view", "point"), None, None, None),
        P(("view", "point"), None),
        P(("view", "point"), None, None),
        P(),
        P(),
        P(),
        P(),
    )
    out_specs = P(("view", "point"), None, None, None)
    return jax.shard_map(shards, mesh=mesh, in_specs=in_specs, out_specs=out_specs, check_vma=False)
```

```python
import functools

import jax
import jax.numpy as jnp
from jax import lax
from jax.experimental import pallas as pl
from jax.experimental.pallas import tpu as pltpu
from jax.sharding import PartitionSpec as P

VT_DEV = 4
PT_DEV = 4
LAYERS = 3
SLOTS = 4
TV = 32
TP = 128
D = 256
N_VIEW = 8
PER = TP // N_VIEW
DATA = SLOTS * PER
EXTRA = 8
ROWS = VT_DEV * TV
RC = 4
KEPT = 2
EARLY = pl.CostEstimate(flops=40_000_000_000, transcendentals=0, bytes_accessed=100_000_000)
STATE = pl.CostEstimate(flops=1_100_000_000, transcendentals=0, bytes_accessed=12_000_000)
F32 = jnp.float32
BF16 = jnp.bfloat16
SMALL = pltpu.CompilerParams(vmem_limit_bytes=8 * 1024 * 1024)
LARGE = pltpu.CompilerParams(vmem_limit_bytes=48 * 1024 * 1024)


def full(memory_space=pltpu.VMEM):
    return pl.BlockSpec(memory_space=memory_space)


def spread(counts, first_lane, rows):
    lane = lax.broadcasted_iota(jnp.int32, (rows, TP), 1)
    line = lax.broadcasted_iota(jnp.int32, (rows, TP), 0) + first_lane
    picked = jnp.where(lane == line, jnp.broadcast_to(counts, (rows, TP)), 0.0)
    count = jnp.sum(picked, axis=1, keepdims=True)
    return jnp.broadcast_to(1.0 / jnp.sqrt(jnp.maximum(count, 1.0)), (rows, D))


def first_sums(tiles_ref, x_ref, m_ref, col_ref, row_ref):
    slot = pl.program_id(0)
    mask = m_ref[0].astype(F32)
    mask_t = mask.T
    col_count = jnp.sum(mask, axis=0, keepdims=True)
    row_count = jnp.sum(mask_t, axis=0, keepdims=True)
    padded = jnp.concatenate([col_count, jnp.zeros((1, D - TP), F32)], axis=1)
    padded_row = jnp.concatenate([row_count, jnp.zeros((1, D - TV), F32)], axis=1)
    point_id = jnp.full((1, D), tiles_ref[1, slot], jnp.int32).astype(F32)

    @pl.when(slot == 0)
    def _():
        row_ref[...] = jnp.zeros_like(row_ref)

    for s in range(SLOTS):

        @pl.when(slot == s)
        def _():
            for peer in range(N_VIEW):
                col_ref[peer, DATA + s : DATA + s + 1, :] = point_id
                col_ref[peer, DATA + SLOTS + s : DATA + SLOTS + s + 1, :] = padded

    for v in range(VT_DEV):
        hit = jnp.where(tiles_ref[0, slot] == v, 1.0, 0.0).astype(F32)
        row_ref[ROWS + v : ROWS + v + 1, :] += padded_row * hit
    acc = None
    totals = []
    for r in range(TV):
        val = x_ref[0, r].astype(F32) * mask_t[:, r : r + 1]
        acc = val if acc is None else acc + val
        totals.append(jnp.sum(val, axis=0, keepdims=True))
    store_sums(slot, tiles_ref, acc, totals, col_ref, row_ref)


def store_sums(slot, tiles_ref, acc, totals, col_ref, row_ref):
    here = pl.ds(pl.multiple_of(slot * PER, PER), PER)
    for peer in range(N_VIEW):
        col_ref[peer, here, :] = acc[peer * PER : (peer + 1) * PER]
    view_at = pl.multiple_of(tiles_ref[0, slot] * TV, TV)
    row_ref[pl.ds(view_at, TV), :] += jnp.concatenate(totals, axis=0)


def relu_mixed(x_ref, mask_t, weight, col_proj, row_proj, r0):
    block = x_ref[0, r0 : r0 + RC].reshape(RC * TP, D)
    prod = jnp.dot(block, weight, preferred_element_type=F32)
    for k in range(RC):
        r = r0 + k
        val = prod[k * TP : (k + 1) * TP] + col_proj + row_proj[r : r + 1, :]
        yield r, jnp.maximum(val, 0.0) * mask_t[:, r : r + 1]


def layer_sums(
    layer, tiles_ref, x_ref, m_ref, ret_ref, rowp_ref, w_ref, *outs
):
    col_ref, row_ref, state_hbm, held, sems = outs
    slot = pl.program_id(0)
    spot = jnp.minimum(slot, KEPT)
    copies = [
        pltpu.make_async_copy(held.at[k], state_hbm.at[k], sems.at[k]) for k in range(KEPT)
    ]

    @pl.when(slot == 0)
    def _():
        row_ref[...] = jnp.zeros_like(row_ref)

    view_at = pl.multiple_of(tiles_ref[0, slot] * TV, TV)
    row_proj = rowp_ref[pl.ds(view_at, TV), :]
    mask_t = m_ref[0].astype(F32).T
    col_proj = ret_ref[:, pl.ds(pl.multiple_of(slot * PER, PER), PER), :].reshape(TP, D)
    acc = None
    totals = []
    for r0 in range(0, TV, RC):
        for r, val in relu_mixed(x_ref, mask_t, w_ref[layer], col_proj, row_proj, r0):
            held[spot, r] = val.astype(BF16)
            acc = val if acc is None else acc + val
            totals.append(jnp.sum(val, axis=0, keepdims=True))
    store_sums(slot, tiles_ref, acc, totals, col_ref, row_ref)
    for k, copy in enumerate(copies):
        pl.when(slot == k)(copy.start)

    @pl.when(slot == SLOTS - 1)
    def _():
        for copy in copies:
            copy.wait()


def layer_state(layer, base, tiles_ref, x_ref, m_ref, ret_ref, rowp_ref, w_ref, *outs):
    slot = pl.program_id(0) + base
    count = x_ref.shape[1]
    start = pl.multiple_of(pl.program_id(1) * count, count)
    view_at = pl.multiple_of(tiles_ref[0, slot] * TV + start, count)
    row_proj = rowp_ref[pl.ds(view_at, count), :]
    mask_t = m_ref[0, pl.ds(start, count), :].astype(F32).T
    col_proj = ret_ref[:, pl.ds(pl.multiple_of(slot * PER, PER), PER), :].reshape(TP, D)
    for r0 in range(0, count, RC):
        for r, val in relu_mixed(x_ref, mask_t, w_ref[layer], col_proj, row_proj, r0):
            outs[-1][0, r] = val.astype(BF16)


def owner_sums(first, at_ref, got_ref, row_ref, a_ref, b_ref, *sums):
    b_ref[a_ref.shape[0] :, :] = row_ref[...]
    for ref in sums:
        ref[...] = jnp.zeros_like(ref)
    for d in range(N_VIEW):
        for s in range(SLOTS):
            place = at_ref[d, s]
            rows = pl.ds(pl.multiple_of(place * PER, PER), PER)
            sums[s][rows, :] += got_ref[d, s * PER : (s + 1) * PER, :]
            if first:
                line = pl.ds(2 * DATA + place, 1)
                sums[s][line, :] += got_ref[d, DATA + SLOTS + s : DATA + SLOTS + s + 1, :]
    for n, ref in enumerate((a_ref, b_ref)):
        spots = [(0, slice(n * DATA, (n + 1) * DATA), DATA)]
        if first:
            start = 2 * DATA + n * PT_DEV
            spots.append((DATA, slice(start, start + PT_DEV), PT_DEV))
            ref[DATA + PT_DEV : DATA + EXTRA, :] = jnp.zeros((EXTRA - PT_DEV, D), F32)
        for to, rows, size in spots:
            ref[to : to + size, :] = (sums[0][rows, :] + sums[1][rows, :]) + (
                sums[2][rows, :] + sums[3][rows, :]
            )


def owner_project(first, layer, at_ref, me_ref, a_ref, b_ref, ra_ref, rb_ref, w_ref, bias_ref, *rest):
    if first:
        ret_ref, row_ref, scale_ref, proj_ref = rest
    else:
        scale_ref, ret_ref, row_ref, proj_ref = rest
    row_ref[...] = b_ref[a_ref.shape[0] :, :] + rb_ref[a_ref.shape[0] :, :]
    for n, (ref, rref) in enumerate(((a_ref, ra_ref), (b_ref, rb_ref))):
        if first:
            for j in range(PT_DEV):
                line = slice(DATA + j, DATA + j + 1)
                count = ref[line, :TP] + rref[line, :TP]
                at = n * DATA + j * PER
                scale_ref[at : at + PER, :] = spread(count, me_ref[0] * PER, PER)
        half = slice(n * DATA, (n + 1) * DATA)
        term = ((ref[:DATA, :] + rref[:DATA, :]) * scale_ref[half, :]).astype(BF16)
        proj = jnp.dot(term, w_ref[layer], preferred_element_type=F32)
        proj_ref[half, :] = proj + bias_ref[layer : layer + 1, :]
    for d in range(N_VIEW):
        for s in range(SLOTS):
            rows = pl.ds(pl.multiple_of(at_ref[d, s] * PER, PER), PER)
            ret_ref[d, s * PER : (s + 1) * PER, :] = proj_ref[rows, :]


def add_rows(mine_ref, other_ref, out_ref):
    out_ref[...] = mine_ref[...] + other_ref[...]


def view_project(first, layer, row_ref, other_ref, *rest):
    if first:
        w_ref, out_ref, scale_ref = rest
        for v in range(VT_DEV):
            line = slice(ROWS + v, ROWS + v + 1)
            count = row_ref[line, :TP] + other_ref[line, :TP]
            scale_ref[v * TV : (v + 1) * TV, :] = spread(count, 0, TV)
    else:
        scale_ref, w_ref, out_ref = rest
    total = row_ref[:ROWS, :] + other_ref[:ROWS, :]
    term = (total * scale_ref[...]).astype(BF16)
    out_ref[...] = jnp.dot(term, w_ref[layer], preferred_element_type=F32)


def array(*shape, dtype=F32):
    return jax.ShapeDtypeStruct(shape, dtype)


def call(kernel, name, out_shape, in_specs, scratch=(), cost=None):
    return pl.pallas_call(
        kernel,
        out_shape=out_shape,
        in_specs=in_specs,
        out_specs=[full()] * len(out_shape),
        scratch_shapes=list(scratch),
        compiler_params=SMALL,
        cost_estimate=cost,
        name=name,
    )


def from_partner(block, flip):
    route = [(i, i ^ flip) for i in range(lax.axis_size("point"))]
    return lax.ppermute(block, "point", route)


def doubled(block, flip):
    return block + from_partner(block, flip)


def shards(features, tiles, masks, w_self, w_col, w_row, bias):
    barrier = lax.optimization_barrier
    smem = full(pltpu.SMEM)
    me_view = lax.axis_index("view").astype(jnp.int32)
    even = (lax.axis_index("point") % 2) == 0
    n_point = lax.axis_size("point")
    pair_a = [(i, i ^ 1) for i in range(n_point)]
    pair_b = [(i, (i + 1) % n_point if i % 2 else (i - 1) % n_point) for i in range(n_point)]
    tiles_t = pltpu.with_memory_space_constraint(tiles.T, pltpu.HBM)
    slot_shape = (SLOTS, TV, TP, D)
    ret_shape = array(N_VIEW, DATA, D)

    def whole(*shape):
        return pl.BlockSpec(shape, lambda i, j, t: (0,) * len(shape))

    def slot_spec(base=0, views=TV):
        return pl.BlockSpec((1, views, TP, D), lambda i, j, t: (i + base, j, 0, 0))

    def mask_spec(base=0):
        return pl.BlockSpec((1, TV, TP), lambda i, j, t: (i + base, 0, 0))

    def by_slot(kernel, name, out_shape, in_specs, out_specs, grid=(SLOTS, 1), scratch=(), **kwargs):
        return pl.pallas_call(
            kernel,
            out_shape=out_shape,
            grid_spec=pltpu.PrefetchScalarGridSpec(
                num_scalar_prefetch=1,
                grid=grid,
                in_specs=in_specs,
                out_specs=out_specs,
                scratch_shapes=list(scratch),
            ),
            compiler_params=LARGE,
            name=name,
            **kwargs,
        )

    def layer_specs(base=0, views=TV):
        return [
            slot_spec(base, views),
            mask_spec(base),
            whole(N_VIEW, DATA, D),
            whole(ROWS, D),
            whole(LAYERS, D, D),
        ]

    def some_state(layer, base, slots, views, old, partial=None):
        tail = [] if partial is None else [partial]
        (out,) = by_slot(
            functools.partial(layer_state, layer, base),
            "layer_state",
            [array(*slot_shape, dtype=BF16)],
            layer_specs(base, views) + [full(pltpu.HBM)] * len(tail),
            [slot_spec(base, views)],
            (slots, TV // views),
            input_output_aliases={6: 0} if tail else {},
            cost_estimate=STATE,
        )(*old, *tail)
        return out

    def after(old, value):
        value, back, row_proj = barrier((value, old[3], old[4]))
        return old[:3] + (back, row_proj, old[5]), value

    masks = pltpu.with_memory_space_constraint(masks, pltpu.HBM)
    features = pltpu.with_memory_space_constraint(features, pltpu.HBM)
    col_pay, row_sum = by_slot(
        first_sums,
        "first_sums",
        [array(N_VIEW, DATA + EXTRA, D), array(ROWS + 8, D)],
        [slot_spec(), mask_spec()],
        [whole(N_VIEW, DATA + EXTRA, D), whole(ROWS + 8, D)],
    )(tiles_t, features, masks)

    state = features
    place = col_scale = row_scale = old = None
    for layer in range(LAYERS):
        first = layer == 0
        last = layer == LAYERS - 1
        got = lax.all_to_all(col_pay, "view", 0, 0, tiled=True)
        row_other = from_partner(row_sum, 8)
        if not first:
            old, row_other = after(old, row_other)
            state = some_state(layer - 1, KEPT, SLOTS - KEPT, TV, old, state)
        (row_sum,) = call(
            add_rows, "add_rows", [array(*row_sum.shape)], [full()] * 2, cost=EARLY
        )(row_sum, row_other)
        row_sum, state = barrier((row_sum, state))
        row_sum = doubled(row_sum, 1)
        got, row_sum = barrier((got, row_sum))
        if first:
            point_id = got[:, DATA : DATA + SLOTS, 0].astype(jnp.int32)
            place = jnp.where(even, point_id ^ PT_DEV, point_id)
        extra = EXTRA if first else 0
        part_a, part_b = call(
            functools.partial(owner_sums, first),
            "owner_sums",
            [array(DATA + extra, D), array(DATA + ROWS + 2 * extra, D)],
            [smem, full(), full()],
            [pltpu.VMEM((2 * DATA + extra, D), F32)] * SLOTS,
        )(place, got, row_sum)
        from_b = lax.ppermute(part_b, "point", pair_b)
        from_a = lax.ppermute(part_a, "point", pair_a)
        outs = call(
            functools.partial(owner_project, first, layer),
            "owner_project",
            [ret_shape, array(ROWS + extra, D)] + ([array(2 * DATA, D)] if first else []),
            [smem, smem] + [full()] * (6 if first else 7),
            [pltpu.VMEM((2 * DATA, D), F32)],
        )(
            place,
            me_view[None],
            part_a,
            part_b,
            from_a,
            from_b,
            w_col,
            bias,
            *(() if first else (col_scale,)),
        )
        row_sum = outs[1]
        row_other = from_partner(row_sum, 4)
        if first:
            col_scale = outs[2]
        back = lax.all_to_all(outs[0], "view", 0, 0, tiled=True)
        outs = call(
            functools.partial(view_project, first, layer),
            "view_project",
            [array(ROWS, D)] * (2 if first else 1),
            [full()] * (3 if first else 4),
            cost=EARLY,
        )(row_sum, row_other, *(() if first else (row_scale,)), w_row)
        row_proj = outs[0]
        if first:
            row_scale = outs[1]
        old = (tiles_t, state, masks, back, row_proj, w_self)
        if last:
            return some_state(layer, 0, SLOTS, TV, old)
        col_pay, row_sum, state = by_slot(
            functools.partial(layer_sums, layer),
            "layer_sums",
            [ret_shape, array(ROWS, D), array(*slot_shape, dtype=BF16)],
            layer_specs(),
            [whole(N_VIEW, DATA, D), whole(ROWS, D), full(pltpu.HBM)],
            scratch=[
                pltpu.VMEM((KEPT + 1, TV, TP, D), BF16),
                pltpu.SemaphoreType.DMA((KEPT,)),
            ],
        )(*old)


def solution(mesh):
    in_specs = (
        P(("view", "point"), None, None, None),
        P(("view", "point"), None),
        P(("view", "point"), None, None),
        P(),
        P(),
        P(),
        P(),
    )
    out_specs = P(("view", "point"), None, None, None)
    return jax.shard_map(shards, mesh=mesh, in_specs=in_specs, out_specs=out_specs, check_vma=False)
```

```python
import functools

import jax
import jax.numpy as jnp
from jax import lax
from jax.experimental import pallas as pl
from jax.experimental.pallas import tpu as pltpu
from jax.sharding import PartitionSpec as P

VT_DEV = 4
PT_DEV = 4
LAYERS = 3
SLOTS = 4
TV = 32
TP = 128
D = 256
N_VIEW = 8
PER = TP // N_VIEW
DATA = SLOTS * PER
EXTRA = 8
ROWS = VT_DEV * TV
RC = 4
HALF = SLOTS // 2
EARLY = pl.CostEstimate(flops=40_000_000_000, transcendentals=0, bytes_accessed=100_000_000)
STATE = pl.CostEstimate(flops=1_100_000_000, transcendentals=0, bytes_accessed=12_000_000)
F32 = jnp.float32
BF16 = jnp.bfloat16
SMALL = pltpu.CompilerParams(vmem_limit_bytes=8 * 1024 * 1024)
LARGE = pltpu.CompilerParams(vmem_limit_bytes=48 * 1024 * 1024)


def full(memory_space=pltpu.VMEM):
    return pl.BlockSpec(memory_space=memory_space)


def spread(counts, first_lane, rows):
    lane = lax.broadcasted_iota(jnp.int32, (rows, TP), 1)
    line = lax.broadcasted_iota(jnp.int32, (rows, TP), 0) + first_lane
    picked = jnp.where(lane == line, jnp.broadcast_to(counts, (rows, TP)), 0.0)
    count = jnp.sum(picked, axis=1, keepdims=True)
    return jnp.broadcast_to(1.0 / jnp.sqrt(jnp.maximum(count, 1.0)), (rows, D))


def first_sums(tiles_ref, x_ref, m_ref, col_ref, row_ref):
    slot = pl.program_id(0)
    mask = m_ref[0].astype(F32)
    mask_t = mask.T
    col_count = jnp.sum(mask, axis=0, keepdims=True)
    row_count = jnp.sum(mask_t, axis=0, keepdims=True)
    padded = jnp.concatenate([col_count, jnp.zeros((1, D - TP), F32)], axis=1)
    padded_row = jnp.concatenate([row_count, jnp.zeros((1, D - TV), F32)], axis=1)
    point_id = jnp.full((1, D), tiles_ref[1, slot], jnp.int32).astype(F32)

    @pl.when(slot == 0)
    def _():
        row_ref[...] = jnp.zeros_like(row_ref)

    for s in range(SLOTS):

        @pl.when(slot == s)
        def _():
            for peer in range(N_VIEW):
                col_ref[peer, DATA + s : DATA + s + 1, :] = point_id
                col_ref[peer, DATA + SLOTS + s : DATA + SLOTS + s + 1, :] = padded

    for v in range(VT_DEV):
        hit = jnp.where(tiles_ref[0, slot] == v, 1.0, 0.0).astype(F32)
        row_ref[ROWS + v : ROWS + v + 1, :] += padded_row * hit
    acc = None
    totals = []
    for r in range(TV):
        val = x_ref[0, r].astype(F32) * mask_t[:, r : r + 1]
        acc = val if acc is None else acc + val
        totals.append(jnp.sum(val, axis=0, keepdims=True))
    store_sums(slot, tiles_ref, acc, totals, col_ref, row_ref)


def store_sums(slot, tiles_ref, acc, totals, col_ref, row_ref):
    here = pl.ds(pl.multiple_of(slot * PER, PER), PER)
    for peer in range(N_VIEW):
        col_ref[peer, here, :] = acc[peer * PER : (peer + 1) * PER]
    view_at = pl.multiple_of(tiles_ref[0, slot] * TV, TV)
    row_ref[pl.ds(view_at, TV), :] += jnp.concatenate(totals, axis=0)


def relu_mixed(x_ref, mask_t, weight, col_proj, row_proj, r0):
    block = x_ref[0, r0 : r0 + RC].reshape(RC * TP, D)
    prod = jnp.dot(block, weight, preferred_element_type=F32)
    for k in range(RC):
        r = r0 + k
        val = prod[k * TP : (k + 1) * TP] + col_proj + row_proj[r : r + 1, :]
        yield r, jnp.maximum(val, 0.0) * mask_t[:, r : r + 1]


def layer_sums(layer, tiles_ref, x_ref, m_ref, ret_ref, rowp_ref, w_ref, col_ref, row_ref):
    slot = pl.program_id(0)

    @pl.when(slot == 0)
    def _():
        row_ref[...] = jnp.zeros_like(row_ref)

    view_at = pl.multiple_of(tiles_ref[0, slot] * TV, TV)
    row_proj = rowp_ref[pl.ds(view_at, TV), :]
    mask_t = m_ref[0].astype(F32).T
    col_proj = ret_ref[:, pl.ds(pl.multiple_of(slot * PER, PER), PER), :].reshape(TP, D)
    acc = None
    totals = []
    for r0 in range(0, TV, RC):
        for _, val in relu_mixed(x_ref, mask_t, w_ref[layer], col_proj, row_proj, r0):
            acc = val if acc is None else acc + val
            totals.append(jnp.sum(val, axis=0, keepdims=True))
    store_sums(slot, tiles_ref, acc, totals, col_ref, row_ref)


def layer_state(layer, base, tiles_ref, x_ref, m_ref, ret_ref, rowp_ref, w_ref, *outs):
    slot = pl.program_id(0) + base
    count = x_ref.shape[1]
    start = pl.multiple_of(pl.program_id(1) * count, count)
    view_at = pl.multiple_of(tiles_ref[0, slot] * TV + start, count)
    row_proj = rowp_ref[pl.ds(view_at, count), :]
    mask_t = m_ref[0, pl.ds(start, count), :].astype(F32).T
    col_proj = ret_ref[:, pl.ds(pl.multiple_of(slot * PER, PER), PER), :].reshape(TP, D)
    for r0 in range(0, count, RC):
        for r, val in relu_mixed(x_ref, mask_t, w_ref[layer], col_proj, row_proj, r0):
            outs[-1][0, r] = val.astype(BF16)


def owner_sums(first, at_ref, got_ref, row_ref, a_ref, b_ref, *sums):
    b_ref[a_ref.shape[0] :, :] = row_ref[...]
    for ref in sums:
        ref[...] = jnp.zeros_like(ref)
    for d in range(N_VIEW):
        for s in range(SLOTS):
            place = at_ref[d, s]
            rows = pl.ds(pl.multiple_of(place * PER, PER), PER)
            sums[s][rows, :] += got_ref[d, s * PER : (s + 1) * PER, :]
            if first:
                line = pl.ds(2 * DATA + place, 1)
                sums[s][line, :] += got_ref[d, DATA + SLOTS + s : DATA + SLOTS + s + 1, :]
    for n, ref in enumerate((a_ref, b_ref)):
        spots = [(0, slice(n * DATA, (n + 1) * DATA), DATA)]
        if first:
            start = 2 * DATA + n * PT_DEV
            spots.append((DATA, slice(start, start + PT_DEV), PT_DEV))
            ref[DATA + PT_DEV : DATA + EXTRA, :] = jnp.zeros((EXTRA - PT_DEV, D), F32)
        for to, rows, size in spots:
            ref[to : to + size, :] = (sums[0][rows, :] + sums[1][rows, :]) + (
                sums[2][rows, :] + sums[3][rows, :]
            )


def owner_project(first, layer, at_ref, me_ref, a_ref, b_ref, ra_ref, rb_ref, w_ref, bias_ref, *rest):
    if first:
        ret_ref, row_ref, scale_ref, proj_ref = rest
    else:
        scale_ref, ret_ref, row_ref, proj_ref = rest
    row_ref[...] = b_ref[a_ref.shape[0] :, :] + rb_ref[a_ref.shape[0] :, :]
    for n, (ref, rref) in enumerate(((a_ref, ra_ref), (b_ref, rb_ref))):
        if first:
            for j in range(PT_DEV):
                line = slice(DATA + j, DATA + j + 1)
                count = ref[line, :TP] + rref[line, :TP]
                at = n * DATA + j * PER
                scale_ref[at : at + PER, :] = spread(count, me_ref[0] * PER, PER)
        half = slice(n * DATA, (n + 1) * DATA)
        term = ((ref[:DATA, :] + rref[:DATA, :]) * scale_ref[half, :]).astype(BF16)
        proj = jnp.dot(term, w_ref[layer], preferred_element_type=F32)
        proj_ref[half, :] = proj + bias_ref[layer : layer + 1, :]
    for d in range(N_VIEW):
        for s in range(SLOTS):
            rows = pl.ds(pl.multiple_of(at_ref[d, s] * PER, PER), PER)
            ret_ref[d, s * PER : (s + 1) * PER, :] = proj_ref[rows, :]


def add_rows(mine_ref, other_ref, out_ref):
    out_ref[...] = mine_ref[...] + other_ref[...]


def view_project(first, layer, row_ref, other_ref, *rest):
    if first:
        w_ref, out_ref, scale_ref = rest
        for v in range(VT_DEV):
            line = slice(ROWS + v, ROWS + v + 1)
            count = row_ref[line, :TP] + other_ref[line, :TP]
            scale_ref[v * TV : (v + 1) * TV, :] = spread(count, 0, TV)
    else:
        scale_ref, w_ref, out_ref = rest
    total = row_ref[:ROWS, :] + other_ref[:ROWS, :]
    term = (total * scale_ref[...]).astype(BF16)
    out_ref[...] = jnp.dot(term, w_ref[layer], preferred_element_type=F32)


def array(*shape, dtype=F32):
    return jax.ShapeDtypeStruct(shape, dtype)


def call(kernel, name, out_shape, in_specs, scratch=(), cost=None):
    return pl.pallas_call(
        kernel,
        out_shape=out_shape,
        in_specs=in_specs,
        out_specs=[full()] * len(out_shape),
        scratch_shapes=list(scratch),
        compiler_params=SMALL,
        cost_estimate=cost,
        name=name,
    )


def from_partner(block, flip):
    route = [(i, i ^ flip) for i in range(lax.axis_size("point"))]
    return lax.ppermute(block, "point", route)


def doubled(block, flip):
    return block + from_partner(block, flip)


def shards(features, tiles, masks, w_self, w_col, w_row, bias):
    barrier = lax.optimization_barrier
    smem = full(pltpu.SMEM)
    me_view = lax.axis_index("view").astype(jnp.int32)
    even = (lax.axis_index("point") % 2) == 0
    n_point = lax.axis_size("point")
    pair_a = [(i, i ^ 1) for i in range(n_point)]
    pair_b = [(i, (i + 1) % n_point if i % 2 else (i - 1) % n_point) for i in range(n_point)]
    tiles_t = pltpu.with_memory_space_constraint(tiles.T, pltpu.HBM)
    slot_shape = (SLOTS, TV, TP, D)
    ret_shape = array(N_VIEW, DATA, D)

    def whole(*shape):
        return pl.BlockSpec(shape, lambda i, j, t: (0,) * len(shape))

    def slot_spec(base=0, views=TV):
        return pl.BlockSpec((1, views, TP, D), lambda i, j, t: (i + base, j, 0, 0))

    def mask_spec(base=0):
        return pl.BlockSpec((1, TV, TP), lambda i, j, t: (i + base, 0, 0))

    def by_slot(kernel, name, out_shape, in_specs, out_specs, grid=(SLOTS, 1), scratch=(), **kwargs):
        return pl.pallas_call(
            kernel,
            out_shape=out_shape,
            grid_spec=pltpu.PrefetchScalarGridSpec(
                num_scalar_prefetch=1,
                grid=grid,
                in_specs=in_specs,
                out_specs=out_specs,
                scratch_shapes=list(scratch),
            ),
            compiler_params=LARGE,
            name=name,
            **kwargs,
        )

    def layer_specs(base=0, views=TV):
        return [
            slot_spec(base, views),
            mask_spec(base),
            whole(N_VIEW, DATA, D),
            whole(ROWS, D),
            whole(LAYERS, D, D),
        ]

    def some_state(layer, base, slots, views, old, partial=None):
        tail = [] if partial is None else [partial]
        (out,) = by_slot(
            functools.partial(layer_state, layer, base),
            "layer_state",
            [array(*slot_shape, dtype=BF16)],
            layer_specs(base, views) + [full(pltpu.HBM)] * len(tail),
            [slot_spec(base, views)],
            (slots, TV // views),
            input_output_aliases={6: 0} if tail else {},
            cost_estimate=STATE,
        )(*old, *tail)
        return out

    def after(old, value):
        value, back, row_proj = barrier((value, old[3], old[4]))
        return old[:3] + (back, row_proj, old[5]), value

    masks = pltpu.with_memory_space_constraint(masks, pltpu.HBM)
    features = pltpu.with_memory_space_constraint(features, pltpu.HBM)
    col_pay, row_sum = by_slot(
        first_sums,
        "first_sums",
        [array(N_VIEW, DATA + EXTRA, D), array(ROWS + 8, D)],
        [slot_spec(), mask_spec()],
        [whole(N_VIEW, DATA + EXTRA, D), whole(ROWS + 8, D)],
    )(tiles_t, features, masks)

    state = features
    place = col_scale = row_scale = old = None
    for layer in range(LAYERS):
        first = layer == 0
        last = layer == LAYERS - 1
        got = lax.all_to_all(col_pay, "view", 0, 0, tiled=True)
        row_other = from_partner(row_sum, 8)
        if not first:
            old, row_other = after(old, row_other)
            state = some_state(layer - 1, 0, HALF, TV, old)
        (row_sum,) = call(
            add_rows, "add_rows", [array(*row_sum.shape)], [full()] * 2, cost=EARLY
        )(row_sum, row_other)
        row_sum, state = barrier((row_sum, state))
        row_sum = doubled(row_sum, 1)
        got, row_sum = barrier((got, row_sum))
        if first:
            point_id = got[:, DATA : DATA + SLOTS, 0].astype(jnp.int32)
            place = jnp.where(even, point_id ^ PT_DEV, point_id)
        extra = EXTRA if first else 0
        part_a, part_b = call(
            functools.partial(owner_sums, first),
            "owner_sums",
            [array(DATA + extra, D), array(DATA + ROWS + 2 * extra, D)],
            [smem, full(), full()],
            [pltpu.VMEM((2 * DATA + extra, D), F32)] * SLOTS,
        )(place, got, row_sum)
        from_b = lax.ppermute(part_b, "point", pair_b)
        from_a = lax.ppermute(part_a, "point", pair_a)
        outs = call(
            functools.partial(owner_project, first, layer),
            "owner_project",
            [ret_shape, array(ROWS + extra, D)] + ([array(2 * DATA, D)] if first else []),
            [smem, smem] + [full()] * (6 if first else 7),
            [pltpu.VMEM((2 * DATA, D), F32)],
        )(
            place,
            me_view[None],
            part_a,
            part_b,
            from_a,
            from_b,
            w_col,
            bias,
            *(() if first else (col_scale,)),
        )
        row_sum = outs[1]
        row_other = from_partner(row_sum, 4)
        if first:
            col_scale = outs[2]
        back = lax.all_to_all(outs[0], "view", 0, 0, tiled=True)
        if not first:
            old, row_other = after(old, row_other)
            state = some_state(layer - 1, HALF, HALF, TV, old, state)
            back, state = barrier((back, state))
        outs = call(
            functools.partial(view_project, first, layer),
            "view_project",
            [array(ROWS, D)] * (2 if first else 1),
            [full()] * (3 if first else 4),
            cost=EARLY,
        )(row_sum, row_other, *(() if first else (row_scale,)), w_row)
        row_proj = outs[0]
        if first:
            row_scale = outs[1]
        old = (tiles_t, state, masks, back, row_proj, w_self)
        if last:
            return some_state(layer, 0, SLOTS, TV, old)
        col_pay, row_sum = by_slot(
            functools.partial(layer_sums, layer),
            "layer_sums",
            [ret_shape, array(ROWS, D)],
            layer_specs(),
            [whole(N_VIEW, DATA, D), whole(ROWS, D)],
        )(*old)


def solution(mesh):
    in_specs = (
        P(("view", "point"), None, None, None),
        P(("view", "point"), None),
        P(("view", "point"), None, None),
        P(),
        P(),
        P(),
        P(),
    )
    out_specs = P(("view", "point"), None, None, None)
    return jax.shard_map(shards, mesh=mesh, in_specs=in_specs, out_specs=out_specs, check_vma=False)
```

```python
import functools

import jax
import jax.numpy as jnp
from jax import lax
from jax.experimental import pallas as pl
from jax.experimental.pallas import tpu as pltpu
from jax.sharding import PartitionSpec as P

VT_DEV = 4
PT_DEV = 4
LAYERS = 3
SLOTS = 4
TV = 32
TP = 128
D = 256
N_VIEW = 8
PER = TP // N_VIEW
DATA = SLOTS * PER
EXTRA = 8
ROWS = VT_DEV * TV
RC = 4
HALF = SLOTS // 2
EARLY = pl.CostEstimate(flops=40_000_000_000, transcendentals=0, bytes_accessed=100_000_000)
STATE = pl.CostEstimate(flops=1_100_000_000, transcendentals=0, bytes_accessed=12_000_000)
F32 = jnp.float32
BF16 = jnp.bfloat16
SMALL = pltpu.CompilerParams(vmem_limit_bytes=8 * 1024 * 1024)
LARGE = pltpu.CompilerParams(vmem_limit_bytes=48 * 1024 * 1024)


def full(memory_space=pltpu.VMEM):
    return pl.BlockSpec(memory_space=memory_space)


def spread(counts, first_lane, rows):
    lane = lax.broadcasted_iota(jnp.int32, (rows, TP), 1)
    line = lax.broadcasted_iota(jnp.int32, (rows, TP), 0) + first_lane
    picked = jnp.where(lane == line, jnp.broadcast_to(counts, (rows, TP)), 0.0)
    count = jnp.sum(picked, axis=1, keepdims=True)
    return jnp.broadcast_to(1.0 / jnp.sqrt(jnp.maximum(count, 1.0)), (rows, D))


def first_sums(tiles_ref, x_ref, m_ref, col_ref, row_ref):
    slot = pl.program_id(0)
    mask = m_ref[0].astype(F32)
    mask_t = mask.T
    col_count = jnp.sum(mask, axis=0, keepdims=True)
    row_count = jnp.sum(mask_t, axis=0, keepdims=True)
    padded = jnp.concatenate([col_count, jnp.zeros((1, D - TP), F32)], axis=1)
    padded_row = jnp.concatenate([row_count, jnp.zeros((1, D - TV), F32)], axis=1)
    point_id = jnp.full((1, D), tiles_ref[1, slot], jnp.int32).astype(F32)

    @pl.when(slot == 0)
    def _():
        row_ref[...] = jnp.zeros_like(row_ref)

    for s in range(SLOTS):

        @pl.when(slot == s)
        def _():
            for peer in range(N_VIEW):
                col_ref[peer, DATA + s : DATA + s + 1, :] = point_id
                col_ref[peer, DATA + SLOTS + s : DATA + SLOTS + s + 1, :] = padded

    for v in range(VT_DEV):
        hit = jnp.where(tiles_ref[0, slot] == v, 1.0, 0.0).astype(F32)
        row_ref[ROWS + v : ROWS + v + 1, :] += padded_row * hit
    acc = None
    totals = []
    for r in range(TV):
        val = x_ref[0, r].astype(F32) * mask_t[:, r : r + 1]
        acc = val if acc is None else acc + val
        totals.append(jnp.sum(val, axis=0, keepdims=True))
    store_sums(slot, tiles_ref, acc, totals, col_ref, row_ref)


def store_sums(slot, tiles_ref, acc, totals, col_ref, row_ref):
    here = pl.ds(pl.multiple_of(slot * PER, PER), PER)
    for peer in range(N_VIEW):
        col_ref[peer, here, :] = acc[peer * PER : (peer + 1) * PER]
    view_at = pl.multiple_of(tiles_ref[0, slot] * TV, TV)
    row_ref[pl.ds(view_at, TV), :] += jnp.concatenate(totals, axis=0)


def relu_mixed(x_ref, mask_t, weight, col_proj, row_proj, r0):
    block = x_ref[0, r0 : r0 + RC].reshape(RC * TP, D)
    prod = jnp.dot(block, weight, preferred_element_type=F32)
    for k in range(RC):
        r = r0 + k
        val = prod[k * TP : (k + 1) * TP] + col_proj + row_proj[r : r + 1, :]
        yield r, jnp.maximum(val, 0.0) * mask_t[:, r : r + 1]


def layer_sums(layer, tiles_ref, x_ref, m_ref, ret_ref, rowp_ref, w_ref, col_ref, row_ref):
    slot = pl.program_id(0)

    @pl.when(slot == 0)
    def _():
        row_ref[...] = jnp.zeros_like(row_ref)

    view_at = pl.multiple_of(tiles_ref[0, slot] * TV, TV)
    row_proj = rowp_ref[pl.ds(view_at, TV), :]
    mask_t = m_ref[0].astype(F32).T
    col_proj = ret_ref[:, pl.ds(pl.multiple_of(slot * PER, PER), PER), :].reshape(TP, D)
    acc = None
    totals = []
    for r0 in range(0, TV, RC):
        for _, val in relu_mixed(x_ref, mask_t, w_ref[layer], col_proj, row_proj, r0):
            acc = val if acc is None else acc + val
            totals.append(jnp.sum(val, axis=0, keepdims=True))
    store_sums(slot, tiles_ref, acc, totals, col_ref, row_ref)


def layer_state(layer, base, tiles_ref, x_ref, m_ref, ret_ref, rowp_ref, w_ref, *outs):
    slot = pl.program_id(0) + base
    count = x_ref.shape[1]
    start = pl.multiple_of(pl.program_id(1) * count, count)
    view_at = pl.multiple_of(tiles_ref[0, slot] * TV + start, count)
    row_proj = rowp_ref[pl.ds(view_at, count), :]
    mask_t = m_ref[0, pl.ds(start, count), :].astype(F32).T
    col_proj = ret_ref[:, pl.ds(pl.multiple_of(slot * PER, PER), PER), :].reshape(TP, D)
    for r0 in range(0, count, RC):
        for r, val in relu_mixed(x_ref, mask_t, w_ref[layer], col_proj, row_proj, r0):
            outs[-1][0, r] = val.astype(BF16)


def owner_sums(first, at_ref, got_ref, row_ref, a_ref, b_ref, *sums):
    b_ref[a_ref.shape[0] :, :] = row_ref[...]
    for ref in sums:
        ref[...] = jnp.zeros_like(ref)
    for d in range(N_VIEW):
        for s in range(SLOTS):
            place = at_ref[d, s]
            rows = pl.ds(pl.multiple_of(place * PER, PER), PER)
            sums[s][rows, :] += got_ref[d, s * PER : (s + 1) * PER, :]
            if first:
                line = pl.ds(2 * DATA + place, 1)
                sums[s][line, :] += got_ref[d, DATA + SLOTS + s : DATA + SLOTS + s + 1, :]
    for n, ref in enumerate((a_ref, b_ref)):
        spots = [(0, slice(n * DATA, (n + 1) * DATA), DATA)]
        if first:
            start = 2 * DATA + n * PT_DEV
            spots.append((DATA, slice(start, start + PT_DEV), PT_DEV))
            ref[DATA + PT_DEV : DATA + EXTRA, :] = jnp.zeros((EXTRA - PT_DEV, D), F32)
        for to, rows, size in spots:
            ref[to : to + size, :] = (sums[0][rows, :] + sums[1][rows, :]) + (
                sums[2][rows, :] + sums[3][rows, :]
            )


def owner_project(first, layer, at_ref, me_ref, a_ref, b_ref, ra_ref, rb_ref, w_ref, bias_ref, *rest):
    if first:
        ret_ref, row_ref, scale_ref, proj_ref = rest
    else:
        scale_ref, ret_ref, row_ref, proj_ref = rest
    row_ref[...] = b_ref[a_ref.shape[0] :, :] + rb_ref[a_ref.shape[0] :, :]
    for n, (ref, rref) in enumerate(((a_ref, ra_ref), (b_ref, rb_ref))):
        if first:
            for j in range(PT_DEV):
                line = slice(DATA + j, DATA + j + 1)
                count = ref[line, :TP] + rref[line, :TP]
                at = n * DATA + j * PER
                scale_ref[at : at + PER, :] = spread(count, me_ref[0] * PER, PER)
        half = slice(n * DATA, (n + 1) * DATA)
        term = ((ref[:DATA, :] + rref[:DATA, :]) * scale_ref[half, :]).astype(BF16)
        proj = jnp.dot(term, w_ref[layer], preferred_element_type=F32)
        proj_ref[half, :] = proj + bias_ref[layer : layer + 1, :]
    for d in range(N_VIEW):
        for s in range(SLOTS):
            rows = pl.ds(pl.multiple_of(at_ref[d, s] * PER, PER), PER)
            ret_ref[d, s * PER : (s + 1) * PER, :] = proj_ref[rows, :]


def add_rows(mine_ref, other_ref, out_ref):
    out_ref[...] = mine_ref[...] + other_ref[...]


def view_project(first, layer, row_ref, other_ref, *rest):
    if first:
        w_ref, out_ref, scale_ref = rest
        for v in range(VT_DEV):
            line = slice(ROWS + v, ROWS + v + 1)
            count = row_ref[line, :TP] + other_ref[line, :TP]
            scale_ref[v * TV : (v + 1) * TV, :] = spread(count, 0, TV)
    else:
        scale_ref, w_ref, out_ref = rest
    total = row_ref[:ROWS, :] + other_ref[:ROWS, :]
    term = (total * scale_ref[...]).astype(BF16)
    out_ref[...] = jnp.dot(term, w_ref[layer], preferred_element_type=F32)


def array(*shape, dtype=F32):
    return jax.ShapeDtypeStruct(shape, dtype)


def call(kernel, name, out_shape, in_specs, scratch=(), cost=None):
    return pl.pallas_call(
        kernel,
        out_shape=out_shape,
        in_specs=in_specs,
        out_specs=[full()] * len(out_shape),
        scratch_shapes=list(scratch),
        compiler_params=SMALL,
        cost_estimate=cost,
        name=name,
    )


def from_partner(block, flip):
    route = [(i, i ^ flip) for i in range(lax.axis_size("point"))]
    return lax.ppermute(block, "point", route)


def doubled(block, flip):
    return block + from_partner(block, flip)


def shards(features, tiles, masks, w_self, w_col, w_row, bias):
    barrier = lax.optimization_barrier
    smem = full(pltpu.SMEM)
    me_view = lax.axis_index("view").astype(jnp.int32)
    even = (lax.axis_index("point") % 2) == 0
    n_point = lax.axis_size("point")
    pair_a = [(i, i ^ 1) for i in range(n_point)]
    pair_b = [(i, (i + 1) % n_point if i % 2 else (i - 1) % n_point) for i in range(n_point)]
    tiles_t = pltpu.with_memory_space_constraint(tiles.T, pltpu.HBM)
    slot_shape = (SLOTS, TV, TP, D)
    ret_shape = array(N_VIEW, DATA, D)

    def whole(*shape):
        return pl.BlockSpec(shape, lambda i, j, t: (0,) * len(shape))

    def slot_spec(base=0, views=TV):
        return pl.BlockSpec((1, views, TP, D), lambda i, j, t: (i + base, j, 0, 0))

    def mask_spec(base=0):
        return pl.BlockSpec((1, TV, TP), lambda i, j, t: (i + base, 0, 0))

    def by_slot(kernel, name, out_shape, in_specs, out_specs, grid=(SLOTS, 1), scratch=(), **kwargs):
        return pl.pallas_call(
            kernel,
            out_shape=out_shape,
            grid_spec=pltpu.PrefetchScalarGridSpec(
                num_scalar_prefetch=1,
                grid=grid,
                in_specs=in_specs,
                out_specs=out_specs,
                scratch_shapes=list(scratch),
            ),
            compiler_params=LARGE,
            name=name,
            **kwargs,
        )

    def layer_specs(base=0, views=TV):
        return [
            slot_spec(base, views),
            mask_spec(base),
            whole(N_VIEW, DATA, D),
            whole(ROWS, D),
            whole(LAYERS, D, D),
        ]

    def some_state(layer, base, slots, views, old, partial=None):
        tail = [] if partial is None else [partial]
        (out,) = by_slot(
            functools.partial(layer_state, layer, base),
            "layer_state",
            [array(*slot_shape, dtype=BF16)],
            layer_specs(base, views) + [full(pltpu.HBM)] * len(tail),
            [slot_spec(base, views)],
            (slots, TV // views),
            input_output_aliases={6: 0} if tail else {},
            cost_estimate=STATE,
        )(*old, *tail)
        return out

    def after(old, value):
        value, back, row_proj = barrier((value, old[3], old[4]))
        return old[:3] + (back, row_proj, old[5]), value

    masks = pltpu.with_memory_space_constraint(masks, pltpu.HBM)
    features = pltpu.with_memory_space_constraint(features, pltpu.HBM)
    col_pay, row_sum = by_slot(
        first_sums,
        "first_sums",
        [array(N_VIEW, DATA + EXTRA, D), array(ROWS + 8, D)],
        [slot_spec(), mask_spec()],
        [whole(N_VIEW, DATA + EXTRA, D), whole(ROWS + 8, D)],
    )(tiles_t, features, masks)

    state = features
    place = col_scale = row_scale = old = None
    for layer in range(LAYERS):
        first = layer == 0
        last = layer == LAYERS - 1
        got = lax.all_to_all(col_pay, "view", 0, 0, tiled=True)
        row_other = from_partner(row_sum, 8)
        if not first:
            old, row_other = after(old, row_other)
            state = some_state(layer - 1, 0, HALF, TV, old)
        (row_sum,) = call(
            add_rows, "add_rows", [array(*row_sum.shape)], [full()] * 2, cost=EARLY
        )(row_sum, row_other)
        row_sum, state = barrier((row_sum, state))
        row_sum = doubled(row_sum, 1)
        got, row_sum = barrier((got, row_sum))
        if first:
            point_id = got[:, DATA : DATA + SLOTS, 0].astype(jnp.int32)
            place = jnp.where(even, point_id ^ PT_DEV, point_id)
        extra = EXTRA if first else 0
        part_a, part_b = call(
            functools.partial(owner_sums, first),
            "owner_sums",
            [array(DATA + extra, D), array(DATA + ROWS + 2 * extra, D)],
            [smem, full(), full()],
            [pltpu.VMEM((2 * DATA + extra, D), F32)] * SLOTS,
        )(place, got, row_sum)
        from_b = lax.ppermute(part_b, "point", pair_b)
        from_a = lax.ppermute(part_a, "point", pair_a)
        outs = call(
            functools.partial(owner_project, first, layer),
            "owner_project",
            [ret_shape, array(ROWS + extra, D)] + ([array(2 * DATA, D)] if first else []),
            [smem, smem] + [full()] * (6 if first else 7),
            [pltpu.VMEM((2 * DATA, D), F32)],
        )(
            place,
            me_view[None],
            part_a,
            part_b,
            from_a,
            from_b,
            w_col,
            bias,
            *(() if first else (col_scale,)),
        )
        row_sum = outs[1]
        row_other = from_partner(row_sum, 4)
        if first:
            col_scale = outs[2]
        back = lax.all_to_all(outs[0], "view", 0, 0, tiled=True)
        if not first:
            old, row_sum = after(old, row_sum)
            state = some_state(layer - 1, HALF, HALF, TV, old, state)
            row_other, state = barrier((row_other, state))
        outs = call(
            functools.partial(view_project, first, layer),
            "view_project",
            [array(ROWS, D)] * (2 if first else 1),
            [full()] * (3 if first else 4),
            cost=EARLY,
        )(row_sum, row_other, *(() if first else (row_scale,)), w_row)
        row_proj = outs[0]
        if first:
            row_scale = outs[1]
        old = (tiles_t, state, masks, back, row_proj, w_self)
        if last:
            return some_state(layer, 0, SLOTS, TV, old)
        col_pay, row_sum = by_slot(
            functools.partial(layer_sums, layer),
            "layer_sums",
            [ret_shape, array(ROWS, D)],
            layer_specs(),
            [whole(N_VIEW, DATA, D), whole(ROWS, D)],
        )(*old)


def solution(mesh):
    in_specs = (
        P(("view", "point"), None, None, None),
        P(("view", "point"), None),
        P(("view", "point"), None, None),
        P(),
        P(),
        P(),
        P(),
    )
    out_specs = P(("view", "point"), None, None, None)
    return jax.shard_map(shards, mesh=mesh, in_specs=in_specs, out_specs=out_specs, check_vma=False)
```
